32 devices in a mesh: dp: 16 (over z, y, core), mlp: 2 (over x).
Axes of the slice: x: 2, y: 2, z: 4, core: 2. Of those that a mesh axis runs over, the one named last changes fastest.
Arguments:
- tokens: bfloat16 [2, 20480, 768], P(None, ('dp', 'mlp')), may hold values from -6 to 6
- cotangent: bfloat16 [2, 20480, 768], P(None, ('dp', 'mlp')), may hold values from -6 to 6
- lengths: int32 [2, 32, 4], P(None, ('dp', 'mlp')), may hold values from 0 to 577, as said below
- buckets: int32 [2, 32], P(None, ('dp', 'mlp')), may hold values from 0 to 2, as said below
- pos_table: bfloat16 [875, 768], replicated, may hold values from -6 to 6
- prompts: bfloat16 [50, 768], replicated, may hold values from -6 to 6
- norm1_gain: bfloat16 [768], replicated, may hold values from 0.25 to 1.75
- norm1_bias: bfloat16 [768], replicated, may hold values from -3 to 3
- qkv_weight: bfloat16 [768, 2304], P(('dp', 'mlp')), may hold values from -0.21875 to 0.21875
- q_bias: bfloat16 [768], replicated, may hold values from -3 to 3
- v_bias: bfloat16 [768], replicated, may hold values from -3 to 3
- out_weight: bfloat16 [768, 768], P(('dp', 'mlp')), may hold values from -2 to 2
- out_bias: bfloat16 [768], replicated, may hold values from -3 to 3
- norm2_gain: bfloat16 [768], replicated, may hold values from 0.25 to 1.75
- norm2_bias: bfloat16 [768], replicated, may hold values from -3 to 3
- up_weight: bfloat16 [768, 3072], P('dp', 'mlp'), may hold values from -0.21875 to 0.21875
- up_bias: bfloat16 [3072], P('mlp'), may hold values from -3 to 3
- down_weight: bfloat16 [3072, 768], P('mlp', 'dp'), may hold values from -0.109375 to 0.109375
- down_bias: bfloat16 [768], replicated, may hold values from -3 to 3
Outputs:
- output: bfloat16 [2, 20480, 768], P(None, ('dp', 'mlp'))
- input_grad: float32 [2, 20480, 768], P(None, ('dp', 'mlp'))
- prompts_grad: float32 [50, 768], replicated
- norm1_gain_grad: float32 [768], replicated
- norm1_bias_grad: float32 [768], replicated
- qkv_weight_grad: float32 [768, 2304], P(('dp', 'mlp'))
- q_bias_grad: float32 [768], replicated
- v_bias_grad: float32 [768], replicated
- out_weight_grad: float32 [768, 768], P(('dp', 'mlp'))
- out_bias_grad: float32 [768], replicated
- norm2_gain_grad: float32 [768], replicated
- norm2_bias_grad: float32 [768], replicated
- up_weight_grad: float32 [768, 3072], P('dp', 'mlp')
- up_bias_grad: float32 [3072], P('mlp')
- down_weight_grad: float32 [3072, 768], P('mlp', 'dp')
- down_bias_grad: float32 [768], replicated
The draws below stay inside these ranges and needn't reach their ends.
Inputs may be any that keep to these rules, and one draw needn't show every extreme that they name: `lengths`: in every buffer the first min(4, 640 // (50 + c)) slots hold c, the image tokens of the buffer's bucket (101, 197, 577 for buckets 0, 1, 2), and the others 0. `buckets`: every micro-batch has buffers of bucket 0 and of bucket 2.
All inputs are finite; a program needn't handle non-finite values.
Results may differ from the reference program's by a relative error of at most 0.012.
Values may be sent and summed in bfloat16 or wider, within the bound.
No kernel may reach another device: no remote copies, remote signals or barrier semaphores. Data moves between devices by JAX's collectives and lax.ppermute only.
A program may use at most 320 MiB of HBM per device.

```python
import math
import jax
import jax.numpy as jnp
from jax import lax

D = 768
HEADS = 12
HEAD_DIM = 64
FF = 3072
PROMPTS = 50
LEN_LOW = 101
LEN_MID = 197
LEN_HIGH = 577
TABLE = 875
SLOTS = 4
ROWS = 640
MICRO = 2
BUFFERS = 32
TOKENS = 20480


def bucket_plan(key):
    base = jax.random.fold_in(key, 911)
    picks = jax.random.randint(base, (MICRO, BUFFERS), 0, 3)
    orders = jax.vmap(lambda subkey: jax.random.permutation(subkey, BUFFERS))(jax.random.split(jax.random.fold_in(base, 5), MICRO))
    picks = jnp.where(orders == 0, 2, picks)
    picks = jnp.where(orders == 1, 0, picks)
    return picks.astype(jnp.int32)


def draw_buckets(key, part):
    return bucket_plan(key)


def draw_lengths(key, part):
    picks = bucket_plan(key)
    counts = jnp.array([LEN_LOW, LEN_MID, LEN_HIGH], dtype=jnp.int32)
    fits = jnp.minimum(SLOTS, ROWS // (PROMPTS + counts)).astype(jnp.int32)
    chosen = counts[picks]
    filled = fits[picks]
    slot_ids = jnp.arange(SLOTS, dtype=jnp.int32)
    return jnp.where(slot_ids[None, None, :] < filled[:, :, None], chosen[:, :, None], 0).astype(jnp.int32)


def levels(own_key, dims, cuts, least, largest):
    level, own = 1.0, jax.random.fold_in(own_key, 6)
    for dim, parts in cuts:
        steps = jnp.exp(jax.random.uniform(jax.random.fold_in(own, dim), (parts,), jnp.float32, least / len(cuts), largest / len(cuts)))
        level = level * jnp.repeat(steps, dims[dim] // parts).reshape([-1 if axis == dim else 1 for axis in range(len(dims))])
    return level


def normal_values(own_key, shape, deviation, bound, pieces=(), held_as=jnp.bfloat16):
    drawn = deviation * jax.random.normal(own_key, shape, jnp.float32)
    if pieces:
        drawn = drawn * levels(own_key, shape, pieces, -0.22, 0.18)
    return jnp.clip(drawn, -bound, bound).astype(held_as)


def setup_inputs(seed: int = 0) -> dict:
    key_list = jax.random.split(jax.random.key(seed), 20)
    tokens = normal_values(key_list[0], (MICRO, TOKENS, D), 1.0, 6.0, ((1, 32),))
    cotangent = normal_values(key_list[1], (MICRO, TOKENS, D), 1.0, 6.0, ((1, 32),))
    lengths = draw_lengths(jax.random.fold_in(key_list[19], 71), 0)
    buckets = draw_buckets(jax.random.fold_in(key_list[19], 71), 0)
    pos_table = normal_values(key_list[4], (TABLE, D), 1.0, 6.0)
    prompts = normal_values(key_list[5], (PROMPTS, D), 1.0, 6.0)
    norm1_gain = jnp.clip(1.0 + 0.15 * jax.random.normal(key_list[6], (D,), jnp.float32), 0.25, 1.75).astype(jnp.bfloat16)
    norm1_bias = normal_values(key_list[7], (D,), 0.5, 3.0)
    qkv_weight = normal_values(key_list[8], (D, 3 * D), D ** -0.5, 0.21875, ((0, 32),))
    q_bias = normal_values(key_list[9], (D,), 0.5, 3.0)
    v_bias = normal_values(key_list[10], (D,), 0.5, 3.0)
    out_weight = normal_values(key_list[11], (D, D), (max(D // 96, 1)) ** -0.5, 2.0, ((0, 32),))
    out_bias = normal_values(key_list[12], (D,), 0.5, 3.0)
    norm2_gain = jnp.clip(1.0 + 0.15 * jax.random.normal(key_list[13], (D,), jnp.float32), 0.25, 1.75).astype(jnp.bfloat16)
    norm2_bias = normal_values(key_list[14], (D,), 0.5, 3.0)
    up_weight = normal_values(key_list[15], (D, FF), D ** -0.5, 0.21875, ((0, 16), (1, 2)))
    up_bias = normal_values(key_list[16], (FF,), 0.5, 3.0, ((0, 2),))
    down_weight = normal_values(key_list[17], (FF, D), FF ** -0.5, 0.109375, ((0, 2), (1, 16)))
    down_bias = normal_values(key_list[18], (D,), 0.5, 3.0)
    return dict(tokens=tokens, cotangent=cotangent, lengths=lengths, buckets=buckets, pos_table=pos_table, prompts=prompts, norm1_gain=norm1_gain, norm1_bias=norm1_bias, qkv_weight=qkv_weight, q_bias=q_bias, v_bias=v_bias, out_weight=out_weight, out_bias=out_bias, norm2_gain=norm2_gain, norm2_bias=norm2_bias, up_weight=up_weight, up_bias=up_bias, down_weight=down_weight, down_bias=down_bias)


epsilon = 1e-06
masked_score = -1e+30
highest = lax.Precision.HIGHEST

@jax.custom_vjp
def low(v):
    return lax.optimization_barrier(v.astype(jnp.bfloat16)).astype(jnp.float32)

@jax.custom_vjp
def low_back(v):
    return v

def low_keep(v):
    return (low(v), None)

def low_pass(kept, grad):
    return (grad,)

def back_keep(v):
    return (v, None)

def back_low(kept, grad):
    return (low(grad),)
low.defvjp(low_keep, low_pass)
low_back.defvjp(back_keep, back_low)

def layout(slot_lengths, bucket_id, row_total):
    sizes_used = jnp.where(slot_lengths > 0, slot_lengths + PROMPTS, 0).astype(jnp.int32)
    seq_ends = jnp.cumsum(sizes_used).astype(jnp.int32)
    seq_starts = (seq_ends - sizes_used).astype(jnp.int32)
    row_ids = jnp.arange(row_total, dtype=jnp.int32)
    sequence = lax.optimization_barrier(jnp.sum((seq_ends[None, :] <= row_ids[:, None]).astype(jnp.int32), axis=1)).astype(jnp.int32)
    slot_ids = jnp.arange(SLOTS, dtype=jnp.int32)
    own_start = lax.optimization_barrier(jnp.sum(jnp.where(sequence[:, None] == slot_ids[None, :], seq_starts[None, :], 0), axis=1)).astype(jnp.int32)
    position = (row_ids - own_start).astype(jnp.int32)
    inside = sequence < SLOTS
    is_prompt = inside & (position < PROMPTS)
    is_image = inside & (position >= PROMPTS)
    table_start = jnp.where(bucket_id == 0, 0, jnp.where(bucket_id == 1, LEN_LOW, LEN_LOW + LEN_MID)).astype(jnp.int32)
    table_index = jnp.clip(table_start + position - PROMPTS, 0, TABLE - 1).astype(jnp.int32)
    prompt_index = jnp.clip(position, 0, PROMPTS - 1).astype(jnp.int32)
    return (sequence, inside, is_prompt, is_image, table_index, prompt_index)

def norm_apply(values_in, norm_gain, norm_shift):
    average = lax.optimization_barrier(jnp.mean(values_in, axis=-1, keepdims=True))
    centred = values_in - average
    variance = lax.optimization_barrier(jnp.mean(centred * centred, axis=-1, keepdims=True))
    return centred * lax.rsqrt(variance + epsilon) * norm_gain + norm_shift

def forward(params, image_rows, slot_lengths, bucket_id, table_rows):
    prompt_rows, gain_one, shift_one, qkv_matrix, query_shift, value_shift, out_matrix, out_shift, gain_two, shift_two, up_matrix, up_shift, down_matrix, down_shift = params
    row_total = image_rows.shape[0]
    sequence, inside, is_prompt, is_image, table_index, prompt_index = layout(slot_lengths, bucket_id, row_total)
    start_rows = jnp.where(is_prompt[:, None], prompt_rows[prompt_index], jnp.where(is_image[:, None], image_rows + table_rows[table_index], 0.0))
    normed = low(norm_apply(start_rows, gain_one, shift_one))
    qkv_offset = jnp.concatenate([query_shift, jnp.zeros_like(query_shift), value_shift])
    qkv_rows = low_back(low(jnp.dot(normed, qkv_matrix, precision=highest) + qkv_offset))
    queries = qkv_rows[:, :D].reshape(row_total, HEADS, HEAD_DIM)
    key_rows = qkv_rows[:, D:2 * D].reshape(row_total, HEADS, HEAD_DIM)
    value_rows = qkv_rows[:, 2 * D:].reshape(row_total, HEADS, HEAD_DIM)
    scores = low_back(jnp.einsum('qhd,khd->hqk', queries, key_rows, precision=highest) / math.sqrt(HEAD_DIM))
    same_seq = sequence[:, None] == sequence[None, :]
    scores = jnp.where(same_seq[None], scores, masked_score)
    weights_soft = low(jax.nn.softmax(scores, axis=-1))
    attended = jnp.einsum('hqk,khd->qhd', weights_soft, value_rows, precision=highest).reshape(row_total, D)
    attended = low_back(low(attended))
    first_sum = start_rows + low_back(jnp.dot(attended, out_matrix, precision=highest)) + out_shift
    normed_two = low(norm_apply(first_sum, gain_two, shift_two))
    hidden_pre = low_back(jnp.dot(normed_two, up_matrix, precision=highest) + up_shift)
    activated = low(jax.nn.gelu(hidden_pre, approximate=False))
    branch = low_back(jnp.dot(activated, down_matrix, precision=highest))
    second_sum = first_sum + branch + down_shift
    return second_sum * inside[:, None].astype(second_sum.dtype)

def reference(tokens, cotangent, lengths, buckets, pos_table, prompts, norm1_gain, norm1_bias, qkv_weight, q_bias, v_bias, out_weight, out_bias, norm2_gain, norm2_bias, up_weight, up_bias, down_weight, down_bias):
    learned = (prompts, norm1_gain, norm1_bias, qkv_weight, q_bias, v_bias, out_weight, out_bias, norm2_gain, norm2_bias, up_weight, up_bias, down_weight, down_bias)
    params = tuple((item.astype(jnp.float32) for item in learned))
    table_rows = pos_table.astype(jnp.float32)
    buffer_total = MICRO * BUFFERS
    token_buffers = tokens.reshape(buffer_total, ROWS, D)
    cot_buffers = cotangent.reshape(buffer_total, ROWS, D)
    length_rows = lengths.reshape(buffer_total, SLOTS)
    bucket_rows = buckets.reshape(buffer_total)

    def step(totals, item):
        token_buf, cot_buf, slot_lengths, bucket_id = item

        def run(param_set, image_rows):
            return forward(param_set, image_rows, slot_lengths, bucket_id, table_rows)
        result, pull = jax.vjp(run, params, token_buf.astype(jnp.float32))
        param_grads, input_rows = pull(cot_buf.astype(jnp.float32))
        totals = jax.tree.map(lambda left, right: left + right, totals, param_grads)
        return (totals, (result.astype(jnp.bfloat16), input_rows))
    start = jax.tree.map(jnp.zeros_like, params)
    grads, (results, input_rows) = lax.scan(step, start, (token_buffers, cot_buffers, length_rows, bucket_rows))
    output = results.reshape(MICRO, TOKENS, D)
    input_grad = input_rows.reshape(MICRO, TOKENS, D)
    return (output, input_grad, grads[0], grads[1], grads[2], grads[3], grads[4], grads[5], grads[6], grads[7], grads[8], grads[9], grads[10], grads[11], grads[12], grads[13])
```

```python
import math

import jax
import jax.numpy as jnp
from jax import lax
from jax.experimental import pallas as pl
from jax.experimental.pallas import tpu as pltpu
from jax.sharding import PartitionSpec as P

D = 768
HEADS = 12
HEAD_DIM = 64
PAIRS = 6
PROMPTS = 50
LEN_LOW = 101
LEN_MID = 197
TABLE = 875
SLOTS = 4
ROWS = 640
GROUP = 3 * 128

epsilon = 1e-06
highest = lax.Precision.HIGHEST
bf16 = jnp.bfloat16
f32 = jnp.float32
log2_e = 1.4426950408889634
score_scale = log2_e / math.sqrt(HEAD_DIM)
erf_p = 0.3275911
erf_a = (0.254829592, -0.284496736, 1.421413741, -1.453152027, 1.061405429)

NT = (((1,), (1,)), ((), ()))
NN = (((1,), (0,)), ((), ()))
TN = (((0,), (0,)), ((), ()))


def dot(left, right, dims=NN):
    return lax.dot_general(left, right, dims, preferred_element_type=f32)


def layout(slot_lengths, bucket_id):
    sizes_used = jnp.where(slot_lengths > 0, slot_lengths + PROMPTS, 0)
    seq_ends = jnp.cumsum(sizes_used)
    seq_starts = seq_ends - sizes_used
    row_ids = jnp.arange(ROWS, dtype=jnp.int32)
    sequence = jnp.sum((seq_ends[None, :] <= row_ids[:, None]).astype(jnp.int32), axis=1)
    slot_ids = jnp.arange(SLOTS, dtype=jnp.int32)
    own_start = jnp.sum(
        jnp.where(sequence[:, None] == slot_ids[None, :], seq_starts[None, :], 0), axis=1
    )
    position = row_ids - own_start
    inside = sequence < SLOTS
    is_prompt = inside & (position < PROMPTS)
    is_image = inside & (position >= PROMPTS)
    table_start = jnp.where(
        bucket_id == 0, 0, jnp.where(bucket_id == 1, LEN_LOW, LEN_LOW + LEN_MID)
    ).astype(jnp.int32)
    table_index = jnp.clip(table_start + position - PROMPTS, 0, TABLE - 1)
    prompt_index = jnp.clip(position, 0, PROMPTS - 1)
    return (sequence, inside, is_prompt, is_image, table_index, prompt_index)


def norm_stats(values_in):
    average = jnp.mean(values_in, axis=-1, keepdims=True)
    centred = values_in - average
    variance = jnp.mean(centred * centred, axis=-1, keepdims=True)
    inverse = lax.rsqrt(variance + epsilon)
    return centred * inverse, inverse


def norm_back(grad_normed, normal, inverse, gain):
    scaled = grad_normed * gain
    mean_one = jnp.mean(scaled, axis=-1, keepdims=True)
    mean_two = jnp.mean(scaled * normal, axis=-1, keepdims=True)
    return (scaled - mean_one - normal * mean_two) * inverse


def attend_kernel(qkv_ref, fq_ref, fk_ref, o_ref, lse_ref, *, chunk):
    pair = pl.program_id(1)
    lane = lax.broadcasted_iota(jnp.int32, (1, 128), 1)
    keys = jnp.concatenate([qkv_ref[:, 128:256], fk_ref[...]], axis=1)
    values = jnp.concatenate([qkv_ref[:, 256:384], jnp.ones((ROWS, 128), bf16)], axis=1)
    for step in range(ROWS // chunk):
        rows = slice(step * chunk, (step + 1) * chunk)
        queries = qkv_ref[rows, 0:128]
        marks = fq_ref[rows, :]
        outs = []
        lse = lse_ref[rows, :]
        for half in range(2):
            keep = (lane < 64) if half == 0 else (lane >= 64)
            own = jnp.concatenate([jnp.where(keep, queries, jnp.zeros_like(queries)), marks], axis=1)
            scores = dot(own, keys, NT)
            top = jnp.max(scores, axis=1, keepdims=True)
            weights = jnp.exp2((scores - top) * score_scale)
            mixed = dot(weights.astype(bf16), values)
            total = mixed[:, 128:129]
            outs.append(mixed[:, :128] / total)
            log_total = top + jnp.log2(total) * (1.0 / score_scale)
            lse = jnp.where(lane == pair * 2 + half, log_total, lse)
        o_ref[rows, :] = jnp.where(lane < 64, outs[0], outs[1]).astype(bf16)
        lse_ref[rows, :] = lse


def attend(qkv, fq, fk, chunk=320):
    rows = qkv.shape[0]
    mark = pl.BlockSpec((ROWS, 128), lambda b, p: (b, 0))
    return pl.pallas_call(
        lambda *refs: attend_kernel(*refs, chunk=chunk),
        grid=(rows // ROWS, PAIRS),
        in_specs=[pl.BlockSpec((ROWS, GROUP), lambda b, p: (b, p)), mark, mark],
        out_specs=[pl.BlockSpec((ROWS, 128), lambda b, p: (b, p)), mark],
        out_shape=[
            jax.ShapeDtypeStruct((rows, D), bf16),
            jax.ShapeDtypeStruct((rows, 128), f32),
        ],
        compiler_params=pltpu.CompilerParams(
            dimension_semantics=("arbitrary", "arbitrary"), vmem_limit_bytes=40 << 20
        ),
        cost_estimate=pl.CostEstimate(
            flops=16 * rows * ROWS * D, bytes_accessed=rows * D * 8, transcendentals=rows * ROWS * HEADS
        ),
        name="attend",
    )(qkv, fq, fk)


def split_three(value):
    first = value.astype(bf16)
    rest = value - first.astype(f32)
    second = rest.astype(bf16)
    third = (rest - second.astype(f32)).astype(bf16)
    return first, second, third


def attend_back_kernel(qkv_ref, do_ref, o_ref, fq_ref, fk_ref, lse_ref, dqkv_ref, ds_ref, *, chunk):
    pair = pl.program_id(1)
    lane = lax.broadcasted_iota(jnp.int32, (1, 128), 1)
    queries = qkv_ref[:, 0:128]
    grads = do_ref[...]
    marks = fq_ref[...]
    product = grads.astype(f32) * o_ref[...].astype(f32)
    lse = lse_ref[...]
    zero = jnp.zeros_like(queries)
    own_q, own_g, wide_q, wide_g = [], [], [], []
    for half in range(2):
        keep = (lane < 64) if half == 0 else (lane >= 64)
        shift = -jnp.sum(jnp.where(lane == pair * 2 + half, lse, 0.0), axis=1, keepdims=True)
        inner = -jnp.sum(jnp.where(keep, product, 0.0), axis=1, keepdims=True)
        s0, s1, s2 = split_three(shift)
        i0, i1, i2 = split_three(inner)
        mark_q = jnp.where(lane == 8, s0, jnp.where(lane == 9, s1, jnp.where(lane == 10, s2, marks)))
        mark_g = jnp.where(lane == 8, i0, jnp.where(lane == 9, i1, jnp.where(lane == 10, i2, zero)))
        q_half = jnp.where(keep, queries, zero)
        g_half = jnp.where(keep, grads, zero)
        own_q.append(q_half)
        own_g.append(g_half)
        wide_q.append(jnp.concatenate([q_half, mark_q], axis=1))
        wide_g.append(jnp.concatenate([g_half, mark_g], axis=1))
    for step in range(ROWS // chunk):
        rows = slice(step * chunk, (step + 1) * chunk)
        keys = jnp.concatenate([qkv_ref[rows, 128:256], fk_ref[rows, :]], axis=1)
        values = jnp.concatenate([qkv_ref[rows, 256:384], fk_ref[rows, :]], axis=1)
        dv = jnp.zeros((chunk, 128), f32)
        dk = jnp.zeros((chunk, 128), f32)
        for half in range(2):
            weights = jnp.exp2(dot(keys, wide_q[half], NT) * score_scale)
            ds = (weights * dot(values, wide_g[half], NT)).astype(bf16)
            ds_ref[half, rows, :] = ds
            dv = dv + dot(weights.astype(bf16), own_g[half])
            dk = dk + dot(ds, own_q[half])
        dqkv_ref[rows, 256:384] = dv.astype(bf16)
        dqkv_ref[rows, 128:256] = (dk * 0.125).astype(bf16)
    keys_t = qkv_ref[:, 128:256].T
    dq = [dot(keys_t, ds_ref[half]).T for half in range(2)]
    dqkv_ref[:, 0:128] = (jnp.where(lane < 64, dq[0], dq[1]) * 0.125).astype(bf16)


def attend_back(qkv, do, o, fq, fk, lse, chunk=640):
    rows = qkv.shape[0]
    mark = pl.BlockSpec((ROWS, 128), lambda b, p: (b, 0))
    part = pl.BlockSpec((ROWS, 128), lambda b, p: (b, p))
    group = pl.BlockSpec((ROWS, GROUP), lambda b, p: (b, p))
    return pl.pallas_call(
        lambda *refs: attend_back_kernel(*refs, chunk=chunk),
        grid=(rows // ROWS, PAIRS),
        in_specs=[group, part, part, mark, mark, mark],
        out_specs=group,
        out_shape=jax.ShapeDtypeStruct(qkv.shape, bf16),
        scratch_shapes=[pltpu.VMEM((2, ROWS, ROWS), bf16)],
        compiler_params=pltpu.CompilerParams(
            dimension_semantics=("arbitrary", "arbitrary"), vmem_limit_bytes=40 << 20
        ),
        cost_estimate=pl.CostEstimate(
            flops=40 * rows * ROWS * D, bytes_accessed=rows * D * 16, transcendentals=rows * ROWS * HEADS
        ),
        name="attend_back",
    )(qkv, do, o, fq, fk, lse)


def gelu_parts(u):
    z = jnp.abs(u) * 0.7071067811865476
    t = 1.0 / (1.0 + erf_p * z)
    e = jnp.exp2(u * u * (-0.5 * log2_e))
    series = t * (erf_a[0] + t * (erf_a[1] + t * (erf_a[2] + t * (erf_a[3] + t * erf_a[4]))))
    tail = 0.5 * series * e
    return jnp.where(u < 0, tail, 1.0 - tail), e * 0.3989422804014327


def feed_kernel(
    b_ref, gm_ref, up_ref, dn_ref, ub_ref, h_ref, db_ref, gu_ref, gd_ref, gub_ref,
    act_s, du_s, h_s, db_s, *, chunk, steps,
):
    j = pl.program_id(0)
    rows_all = b_ref.shape[0]
    up, dn, ub = up_ref[...], dn_ref[...], ub_ref[...]
    sums = jnp.zeros((1, ub.shape[1]), f32)
    for step in range(rows_all // chunk):
        rows = slice(step * chunk, (step + 1) * chunk)
        u = dot(b_ref[rows, :], up) + ub
        cdf, pdf = gelu_parts(u)
        act = (u * cdf).astype(bf16)
        du = (dot(gm_ref[rows, :], dn) * (cdf + u * pdf)).astype(bf16)
        sums = sums + jnp.sum(du.astype(f32), axis=0, keepdims=True)
        act_s[rows, :] = act
        du_s[rows, :] = du
        hh = dot(act, dn, NT)
        dd = dot(du, up, NT)

        @pl.when(j == 0)
        def _():
            h_s[rows, :] = hh
            db_s[rows, :] = dd

        @pl.when(j > 0)
        def _():
            h_s[rows, :] += hh
            db_s[rows, :] += dd

    gub_ref[...] = sums
    gu_ref[...] = dot(b_ref[...], du_s[...], TN).astype(bf16)
    gd_ref[...] = dot(gm_ref[...], act_s[...], TN).astype(bf16)

    @pl.when(j == steps - 1)
    def _():
        h_ref[...] = h_s[...]
        db_ref[...] = db_s[...]


def feed(b, gm, up, dn, ub, block=512, chunk=640):
    rows = b.shape[0]
    splits, _, hidden = up.shape
    per = hidden // block
    steps = splits * per
    full = pl.BlockSpec((rows, D), lambda j: (0, 0), pipeline_mode=pl.Buffered(1))
    weight = pl.BlockSpec((None, D, block), lambda j: (j // per, 0, j % per))
    bias = pl.BlockSpec((1, block), lambda j: (0, j))
    return pl.pallas_call(
        lambda *refs: feed_kernel(*refs, chunk=chunk, steps=steps),
        grid=(steps,),
        in_specs=[full, full, weight, weight, bias],
        out_specs=[full, full, weight, weight, bias],
        out_shape=[jax.ShapeDtypeStruct((rows, D), f32)] * 2
        + [jax.ShapeDtypeStruct(up.shape, bf16)] * 2
        + [jax.ShapeDtypeStruct(ub.shape, f32)],
        scratch_shapes=[pltpu.VMEM((rows, block), bf16)] * 2 + [pltpu.VMEM((rows, D), f32)] * 2,
        compiler_params=pltpu.CompilerParams(
            dimension_semantics=("arbitrary",), vmem_limit_bytes=56 << 20
        ),
        cost_estimate=pl.CostEstimate(
            flops=12 * rows * steps * block * D,
            bytes_accessed=rows * D * 12 + steps * block * D * 8,
            transcendentals=2 * rows * steps * block,
        ),
        name="feed",
    )(b, gm, up, dn, ub)


def pair_major(columns):
    lead = columns.shape[:-1]
    return columns.reshape(lead + (3, PAIRS, 128)).swapaxes(-3, -2).reshape(lead + (3 * D,))


def pair_minor(columns):
    lead = columns.shape[:-1]
    return columns.reshape(lead + (PAIRS, 3, 128)).swapaxes(-3, -2).reshape(lead + (3 * D,))


def per_device(
    tokens,
    cotangent,
    lengths,
    buckets,
    pos_table,
    prompts,
    norm1_gain,
    norm1_bias,
    qkv_weight,
    q_bias,
    v_bias,
    out_weight,
    out_bias,
    norm2_gain,
    norm2_bias,
    up_weight,
    up_bias,
    down_weight,
    down_bias,
):
    everyone = ("dp", "mlp")
    mlp_size = lax.axis_size("mlp")
    micro_count, local_rows = tokens.shape[:2]
    rows = micro_count * local_rows
    hidden_local = up_weight.shape[1]
    hidden = hidden_local * mlp_size

    qkv_full = lax.all_gather(pair_major(qkv_weight), everyone, axis=0, tiled=True)
    out_full = lax.all_gather(out_weight, everyone, axis=0, tiled=True)
    up_full = lax.all_gather(up_weight, ("mlp", "dp"), axis=0, tiled=True)
    down_full = lax.all_gather(down_weight.T, ("mlp", "dp"), axis=0, tiled=True)
    up_full = up_full.reshape(mlp_size, D, hidden_local)
    down_full = down_full.reshape(mlp_size, D, hidden_local)
    up_shift = lax.all_gather(up_bias, "mlp", axis=0, tiled=True).astype(f32)[None, :]

    gain_one, shift_one = norm1_gain.astype(f32), norm1_bias.astype(f32)
    gain_two, shift_two = norm2_gain.astype(f32), norm2_bias.astype(f32)
    qkv_offset = pair_major(
        jnp.concatenate([q_bias.astype(f32), jnp.zeros((D,), f32), v_bias.astype(f32)])
    )

    flat = jax.vmap(layout)(lengths.reshape(-1, SLOTS), buckets.reshape(-1))
    sequence, inside, is_prompt, is_image, table_index, prompt_index = (
        item.reshape(rows) for item in flat
    )
    valid = inside[:, None]
    image = is_image[:, None]
    table_all = jnp.concatenate([pos_table, prompts], axis=0)
    picked = jnp.take(table_all, jnp.where(is_prompt, TABLE + prompt_index, table_index), axis=0)
    image_rows = tokens.reshape(rows, D).astype(f32)
    start_rows = jnp.where(
        valid, jnp.where(image, image_rows, 0.0) + picked.astype(f32), 0.0
    )
    lane = jnp.arange(128, dtype=jnp.int32)[None, :]
    same = lane == sequence[:, None]
    fq = same.astype(bf16)
    fk = jnp.where(
        lane <= SLOTS,
        jnp.where(same, 0.0, -1e30),
        jnp.where((lane >= 8) & (lane < 11), 1.0, 0.0),
    ).astype(bf16)
    grad_branch = jnp.where(valid, cotangent.reshape(rows, D), jnp.zeros((), bf16))
    grad_two = grad_branch.astype(f32)
    grad_down_shift = jnp.sum(grad_two, axis=0)

    normal_one, inverse_one = norm_stats(start_rows)
    normed = (normal_one * gain_one + shift_one).astype(bf16)
    qkv_rows = (dot(normed, qkv_full) + qkv_offset).astype(bf16)
    attended, log_total = attend(qkv_rows, fq, fk)
    first_sum = start_rows + dot(attended, out_full) + out_bias.astype(f32)
    normal_two, inverse_two = norm_stats(first_sum)
    normed_two = (normal_two * gain_two + shift_two).astype(bf16)

    branch, grad_normed, grad_up, grad_down, grad_up_shift = feed(
        normed_two, grad_branch, up_full, down_full, up_shift
    )
    output = jnp.where(valid, first_sum + branch + down_bias.astype(f32), 0.0).astype(bf16)

    grad_gain_two = jnp.sum(grad_normed * normal_two, axis=0)
    grad_shift_two = jnp.sum(grad_normed, axis=0)
    grad_one = grad_two + norm_back(grad_normed, normal_two, inverse_two, gain_two)
    grad_out_shift = jnp.sum(grad_one, axis=0)
    grad_att = grad_one.astype(bf16)
    grad_out = dot(attended, grad_att, TN).astype(bf16)
    grad_attended = dot(grad_att, out_full, NT).astype(bf16)
    grad_qkv_rows = attend_back(qkv_rows, grad_attended, attended, fq, fk, log_total)
    grad_qkv = dot(normed, grad_qkv_rows, TN).astype(bf16)
    column_sums = pair_minor(jnp.sum(grad_qkv_rows.astype(f32), axis=0))
    grad_normed_one = dot(grad_qkv_rows, qkv_full, NT)
    grad_gain_one = jnp.sum(grad_normed_one * normal_one, axis=0)
    grad_shift_one = jnp.sum(grad_normed_one, axis=0)
    grad_zero = grad_one + norm_back(grad_normed_one, normal_one, inverse_one, gain_one)
    input_grad = jnp.where(image, grad_zero, 0.0)
    prompt_hits = (
        (prompt_index[:, None] == jnp.arange(PROMPTS, dtype=jnp.int32)[None, :]) & is_prompt[:, None]
    ).astype(f32)
    grad_prompts = jnp.einsum("rp,rd->pd", prompt_hits, grad_zero, precision=highest)

    def scatter(value, axes):
        return lax.psum_scatter(value, axes, scatter_dimension=0, tiled=True).astype(f32)

    qkv_weight_grad = pair_minor(scatter(grad_qkv, everyone))
    out_weight_grad = scatter(grad_out, everyone)
    up_weight_grad = scatter(grad_up.reshape(mlp_size * D, hidden_local), ("mlp", "dp"))
    down_weight_grad = scatter(grad_down.reshape(mlp_size * D, hidden_local), ("mlp", "dp")).T

    packed = jnp.concatenate(
        [
            grad_prompts,
            grad_gain_one[None],
            grad_shift_one[None],
            column_sums[None, :D],
            column_sums[None, 2 * D :],
            grad_out_shift[None],
            grad_gain_two[None],
            grad_shift_two[None],
            grad_down_shift[None],
            grad_up_shift.reshape(hidden // D, D),
        ],
        axis=0,
    )
    summed = lax.psum(packed, everyone)
    singles = [summed[PROMPTS + i] for i in range(8)]
    up_bias_grad = lax.dynamic_slice_in_dim(
        summed[PROMPTS + 8 :].reshape(hidden), lax.axis_index("mlp") * hidden_local, hidden_local, 0
    )
    return (
        output.reshape(tokens.shape),
        input_grad.reshape(tokens.shape),
        summed[:PROMPTS],
        singles[0],
        singles[1],
        qkv_weight_grad,
        singles[2],
        singles[3],
        out_weight_grad,
        singles[4],
        singles[5],
        singles[6],
        up_weight_grad,
        up_bias_grad,
        down_weight_grad,
        singles[7],
    )


def solution(mesh):
    both = ("dp", "mlp")
    in_specs = (
        P(None, both, None),
        P(None, both, None),
        P(None, both, None),
        P(None, both),
        P(),
        P(),
        P(),
        P(),
        P(both, None),
        P(),
        P(),
        P(both, None),
        P(),
        P(),
        P(),
        P("dp", "mlp"),
        P("mlp"),
        P("mlp", "dp"),
        P(),
    )
    out_specs = (
        P(None, both, None),
        P(None, both, None),
        P(),
        P(),
        P(),
        P(both, None),
        P(),
        P(),
        P(both, None),
        P(),
        P(),
        P(),
        P("dp", "mlp"),
        P("mlp"),
        P("mlp", "dp"),
        P(),
    )
    return jax.shard_map(
        per_device, mesh=mesh, in_specs=in_specs, out_specs=out_specs, check_vma=False
    )
```

```python
import math

import jax
import jax.numpy as jnp
from jax import lax
from jax.experimental import pallas as pl
from jax.experimental.pallas import tpu as pltpu
from jax.sharding import PartitionSpec as P

D = 768
HEADS = 12
HEAD_DIM = 64
PAIRS = 6
PROMPTS = 50
LEN_LOW = 101
LEN_MID = 197
TABLE = 875
SLOTS = 4
ROWS = 640
GROUP = 3 * 128
PACK = 64
BLOCK = 320
weigh = 5
FIRST = 2

epsilon = 1e-06
bf16 = jnp.bfloat16
f32 = jnp.float32
log2_e = 1.4426950408889634
score_scale = log2_e / math.sqrt(HEAD_DIM)
erf_p = 0.3275911
erf_a = (0.254829592, -0.284496736, 1.421413741, -1.453152027, 1.061405429)

NT = (((1,), (1,)), ((), ()))
NN = (((1,), (0,)), ((), ()))
TN = (((0,), (0,)), ((), ()))


def cost(flops, bytes_accessed, transcendentals):
    return pl.CostEstimate(
        flops=weigh * flops, bytes_accessed=weigh * bytes_accessed, transcendentals=weigh * transcendentals
    )


def dot(left, right, dims=NN):
    return lax.dot_general(left, right, dims, preferred_element_type=f32)


def row_plan(lengths_ref, buckets_ref, buffer, rows):
    sequence = jnp.zeros_like(rows)
    start = jnp.zeros_like(rows)
    end = 0
    for slot in range(SLOTS):
        length = lengths_ref[buffer, slot]
        end = end + jnp.where(length > 0, length + PROMPTS, 0)
        sequence = sequence + jnp.where(end <= rows, 1, 0)
        start = jnp.where(end <= rows, end, start)
    position = rows - start
    bucket = buckets_ref[buffer]
    table = jnp.where(bucket == 0, 0, jnp.where(bucket == 1, LEN_LOW, LEN_LOW + LEN_MID))
    inside = sequence < SLOTS
    prompt = inside & (position < PROMPTS)
    image = inside & (position >= PROMPTS)
    index = jnp.where(
        prompt,
        TABLE + position,
        jnp.where(image, jnp.clip(table + position - PROMPTS, 0, TABLE - 1), -1),
    )
    return sequence, position, inside, prompt, image, index


def norm_stats(values_in):
    average = jnp.mean(values_in, axis=-1, keepdims=True)
    centred = values_in - average
    variance = jnp.mean(centred * centred, axis=-1, keepdims=True)
    inverse = lax.rsqrt(variance + epsilon)
    return centred * inverse, inverse


def norm_back(grad_normed, normal, inverse, gain):
    scaled = grad_normed * gain
    mean_one = jnp.mean(scaled, axis=-1, keepdims=True)
    mean_two = jnp.mean(scaled * normal, axis=-1, keepdims=True)
    return (scaled - mean_one - normal * mean_two) * inverse


def add_rows(ref, step, row, value):
    total = jnp.sum(value, axis=0, keepdims=True)

    @pl.when(step == 0)
    def _():
        ref[row : row + 1, :] = total

    @pl.when(step > 0)
    def _():
        ref[row : row + 1, :] += total


def block_rows(shape, axis):
    step = pl.program_id(0)
    per = ROWS // BLOCK
    ids = lax.broadcasted_iota(jnp.int32, shape, axis) + lax.rem(step, per) * BLOCK
    return lax.div(step, per), ids


def embed_kernel(
    lengths_ref, buckets_ref, tokens_ref, cot_ref, table_ref, gain_ref, shift_ref,
    h_ref, a_ref, gm_ref, fq_ref, fk_ref, sum_ref,
):
    buffer, ids = block_rows((BLOCK, 1), 0)
    lane = lax.broadcasted_iota(jnp.int32, (1, 128), 1)
    sequence, _, inside, _, image, index = row_plan(lengths_ref, buckets_ref, buffer, ids)
    places = lax.broadcasted_iota(jnp.int32, (1, table_ref.shape[0]), 1)
    hits = jnp.where(places == index, 1.0, 0.0).astype(bf16)
    start = dot(hits, table_ref[...]) + jnp.where(image, tokens_ref[...].astype(f32), 0.0)
    h_ref[...] = start
    normal, _ = norm_stats(start)
    a_ref[...] = (normal * gain_ref[...] + shift_ref[...]).astype(bf16)
    grad = jnp.where(inside, cot_ref[...].astype(f32), 0.0)
    gm_ref[...] = grad.astype(bf16)
    same = lane == sequence
    fq_ref[...] = jnp.where(same, 1.0, 0.0).astype(bf16)
    ones = jnp.where((lane >= 8) & (lane < 11), 1.0, 0.0)
    fk_ref[...] = jnp.where((lane <= SLOTS) & ~same, -1e30, ones).astype(bf16)
    add_rows(sum_ref, pl.program_id(0), 0, grad)


def whole_spec(shape):
    return pl.BlockSpec(shape, lambda b: (0,) * len(shape), pipeline_mode=pl.Buffered(1))


def scalar_spec():
    return pl.BlockSpec(memory_space=pltpu.SMEM)


def buffer_spec(columns):
    return pl.BlockSpec((BLOCK, columns), lambda b: (b, 0))


def buffer_params():
    return pltpu.CompilerParams(dimension_semantics=("arbitrary",), vmem_limit_bytes=56 << 20)


def embed(lengths, buckets, tokens, cotangent, table, gain, shift):
    rows = tokens.shape[0]
    kept = whole_spec((1, D))
    return pl.pallas_call(
        embed_kernel,
        grid=(rows // BLOCK,),
        in_specs=[
            scalar_spec(), scalar_spec(), buffer_spec(D), buffer_spec(D), whole_spec(table.shape), kept, kept,
        ],
        out_specs=[buffer_spec(D), buffer_spec(D), buffer_spec(D), buffer_spec(128), buffer_spec(128), kept],
        out_shape=[
            jax.ShapeDtypeStruct((rows, D), f32),
            jax.ShapeDtypeStruct((rows, D), bf16),
            jax.ShapeDtypeStruct((rows, D), bf16),
            jax.ShapeDtypeStruct((rows, 128), bf16),
            jax.ShapeDtypeStruct((rows, 128), bf16),
            jax.ShapeDtypeStruct((1, D), f32),
        ],
        compiler_params=buffer_params(),
        cost_estimate=cost(
            flops=2 * rows * table.shape[0] * D, bytes_accessed=rows * D * 12, transcendentals=0
        ),
        name="embed",
    )(lengths, buckets, tokens, cotangent, table, gain, shift)


def middle_kernel(o1_ref, o2_ref, w_ref, h_ref, bias_ref, gain_ref, shift_ref, h1_ref, b_ref):
    cut = o1_ref.shape[1]
    mixed = dot(o1_ref[...], w_ref[:cut, :]) + dot(o2_ref[...], w_ref[cut:, :])
    total = h_ref[...] + mixed + bias_ref[...]
    h1_ref[...] = total
    normal, _ = norm_stats(total)
    b_ref[...] = (normal * gain_ref[...] + shift_ref[...]).astype(bf16)


def middle(o1, o2, weight, start, bias, gain, shift):
    rows = start.shape[0]
    kept = whole_spec((1, D))
    return pl.pallas_call(
        middle_kernel,
        grid=(rows // BLOCK,),
        in_specs=[
            buffer_spec(o1.shape[1]), buffer_spec(o2.shape[1]), whole_spec((D, D)), buffer_spec(D), kept, kept, kept,
        ],
        out_specs=[buffer_spec(D), buffer_spec(D)],
        out_shape=[jax.ShapeDtypeStruct((rows, D), f32), jax.ShapeDtypeStruct((rows, D), bf16)],
        compiler_params=buffer_params(),
        cost_estimate=cost(
            flops=2 * rows * D * D, bytes_accessed=rows * D * 12, transcendentals=0
        ),
        name="middle",
    )(o1, o2, weight, start, bias, gain, shift)


def middle_back_kernel(
    lengths_ref, buckets_ref, h1_ref, branch_ref, db_ref, gm_ref, o1_ref, o2_ref, w_ref, gain_ref,
    down_ref, gdown_ref, gup_ref, out_ref, g1_ref, do_ref, gw_ref, early_ref, gw_s,
):
    step = pl.program_id(0)
    cut = o1_ref.shape[1]
    buffer, ids = block_rows((BLOCK, 1), 0)
    _, _, inside, _, _, _ = row_plan(lengths_ref, buckets_ref, buffer, ids)
    h1 = h1_ref[...]
    out_ref[...] = jnp.where(inside, h1 + branch_ref[...] + down_ref[...], 0.0).astype(bf16)
    normal, inverse = norm_stats(h1)
    db = db_ref[...]
    g1 = gm_ref[...].astype(f32) + norm_back(db, normal, inverse, gain_ref[...])
    g1_ref[...] = g1
    ga = g1.astype(bf16)
    do_ref[...] = dot(ga, w_ref[...], NT).astype(bf16)
    for row, value in ((0, g1), (1, db * normal), (2, db)):
        add_rows(early_ref, step, row, value)
    first = dot(o1_ref[...], ga, TN)
    second = dot(o2_ref[...], ga, TN)

    @pl.when(step == 0)
    def _():
        gw_s[:cut, :] = first
        gw_s[cut:, :] = second

    @pl.when(step > 0)
    def _():
        gw_s[:cut, :] += first
        gw_s[cut:, :] += second

    @pl.when(step == pl.num_programs(0) - 1)
    def _():
        gw_ref[...] = gw_s[...].astype(bf16)
        early_ref[3:4, :] = gdown_ref[...]
        for i in range(gup_ref.shape[1] // D):
            early_ref[4 + i : 5 + i, :] = gup_ref[:, i * D : (i + 1) * D]


def middle_back(
    lengths, buckets, h1, branch, db, gm, o1, o2, weight, gain, down_bias, grad_down, grad_up
):
    rows = h1.shape[0]
    kept = whole_spec((1, D))
    wide = buffer_spec(D)
    square = whole_spec((D, D))
    return pl.pallas_call(
        middle_back_kernel,
        grid=(rows // BLOCK,),
        in_specs=[
            scalar_spec(), scalar_spec(), wide, wide, wide, wide, buffer_spec(o1.shape[1]),
            buffer_spec(o2.shape[1]), square, kept, kept, kept, whole_spec(grad_up.shape),
        ],
        out_specs=[wide, wide, wide, square, whole_spec((8, D))],
        out_shape=[
            jax.ShapeDtypeStruct((rows, D), bf16),
            jax.ShapeDtypeStruct((rows, D), f32),
            jax.ShapeDtypeStruct((rows, D), bf16),
            jax.ShapeDtypeStruct((D, D), bf16),
            jax.ShapeDtypeStruct((8, D), f32),
        ],
        scratch_shapes=[pltpu.VMEM((D, D), f32)],
        compiler_params=buffer_params(),
        cost_estimate=cost(
            flops=4 * rows * D * D, bytes_accessed=rows * D * 26, transcendentals=0
        ),
        name="middle_back",
    )(lengths, buckets, h1, branch, db, gm, o1, o2, weight, gain, down_bias, grad_down, grad_up)


def finish_kernel(
    lengths_ref, buckets_ref, d1_ref, d2_ref, w1_ref, w2_ref, h_ref, g1_ref, gain_ref, early_ref,
    input_ref, pack_ref, column_s,
):
    step = pl.program_id(0)
    cut = d1_ref.shape[1]
    count = pack_ref.shape[0]
    buffer, ids = block_rows((BLOCK, 1), 0)
    _, _, _, _, image, _ = row_plan(lengths_ref, buckets_ref, buffer, ids)
    da = dot(d1_ref[...], w1_ref[...], NT) + dot(d2_ref[...], w2_ref[...], NT)
    normal, inverse = norm_stats(h_ref[...])
    g0 = g1_ref[...] + norm_back(da, normal, inverse, gain_ref[...])
    input_ref[...] = jnp.where(image, g0, 0.0)
    _, across = block_rows((1, BLOCK), 1)
    _, position, _, prompt, _, _ = row_plan(lengths_ref, buckets_ref, buffer, across)
    wanted = lax.broadcasted_iota(jnp.int32, (count, 1), 0)
    hits = jnp.where(prompt & (wanted == position), 1.0, 0.0).astype(bf16)
    sums = sum(dot(hits, part) for part in split_three(g0))
    lines = [jnp.sum(da * normal, axis=0, keepdims=True), jnp.sum(da, axis=0, keepdims=True)]
    for row, line in enumerate(lines):
        sums = jnp.where(wanted == PROMPTS + row, line, sums)
    columns = [jnp.sum(item[...].astype(f32), axis=0, keepdims=True) for item in (d1_ref, d2_ref)]

    @pl.when(step == 0)
    def _():
        pack_ref[...] = sums
        column_s[:, :cut] = columns[0]
        column_s[:, cut:] = columns[1]

    @pl.when(step > 0)
    def _():
        pack_ref[...] += sums
        column_s[:, :cut] += columns[0]
        column_s[:, cut:] += columns[1]

    @pl.when(step == pl.num_programs(0) - 1)
    def _():
        for pair in range(PAIRS):
            to = slice(pair * 128, (pair + 1) * 128)
            for row, part in ((PROMPTS + 2, 0), (PROMPTS + 3, 2)):
                at = pair * GROUP + part * 128
                pack_ref[row : row + 1, to] = column_s[:, at : at + 128]
        pack_ref[PROMPTS + 4 : PROMPTS + 12, :] = early_ref[...]


def finish(lengths, buckets, d1, d2, w1, w2, start, g1, gain, early):
    rows = start.shape[0]
    wide = buffer_spec(D)
    return pl.pallas_call(
        finish_kernel,
        grid=(rows // BLOCK,),
        in_specs=[
            scalar_spec(), scalar_spec(), buffer_spec(d1.shape[1]), buffer_spec(d2.shape[1]),
            whole_spec(w1.shape), whole_spec(w2.shape), wide, wide, whole_spec((1, D)), whole_spec((8, D)),
        ],
        out_specs=[wide, whole_spec((PACK, D))],
        out_shape=[jax.ShapeDtypeStruct((rows, D), f32), jax.ShapeDtypeStruct((PACK, D), f32)],
        scratch_shapes=[pltpu.VMEM((1, 3 * D), f32)],
        compiler_params=buffer_params(),
        cost_estimate=cost(
            flops=6 * rows * D * D, bytes_accessed=rows * D * 18, transcendentals=0
        ),
        name="finish",
    )(lengths, buckets, d1, d2, w1, w2, start, g1, gain, early)


def attend_kernel(qkv_ref, fq_ref, fk_ref, o_ref, lse_ref, *, chunk):
    pair = pl.program_id(1)
    lane = lax.broadcasted_iota(jnp.int32, (1, 128), 1)
    keys = jnp.concatenate([qkv_ref[:, 128:256], fk_ref[...]], axis=1)
    values = jnp.concatenate([qkv_ref[:, 256:384], jnp.ones((ROWS, 128), bf16)], axis=1)
    for step in range(ROWS // chunk):
        rows = slice(step * chunk, (step + 1) * chunk)
        queries = qkv_ref[rows, 0:128]
        marks = fq_ref[rows, :]
        outs = []
        lse = lse_ref[rows, :]
        for half in range(2):
            keep = (lane < 64) if half == 0 else (lane >= 64)
            own = jnp.concatenate([jnp.where(keep, queries, jnp.zeros_like(queries)), marks], axis=1)
            scores = dot(own, keys, NT)
            top = jnp.max(scores, axis=1, keepdims=True)
            weights = jnp.exp2((scores - top) * score_scale)
            mixed = dot(weights.astype(bf16), values)
            total = mixed[:, 128:129]
            outs.append(mixed[:, :128] / total)
            log_total = top + jnp.log2(total) * (1.0 / score_scale)
            lse = jnp.where(lane == pair * 2 + half, log_total, lse)
        o_ref[rows, :] = jnp.where(lane < 64, outs[0], outs[1]).astype(bf16)
        lse_ref[rows, :] = lse


def attend(qkv, fq, fk, chunk=320):
    rows = qkv.shape[0]
    mark = pl.BlockSpec((ROWS, 128), lambda b, p: (b, 0))
    return pl.pallas_call(
        lambda *refs: attend_kernel(*refs, chunk=chunk),
        grid=(rows // ROWS, qkv.shape[1] // GROUP),
        in_specs=[pl.BlockSpec((ROWS, GROUP), lambda b, p: (b, p)), mark, mark],
        out_specs=[pl.BlockSpec((ROWS, 128), lambda b, p: (b, p)), mark],
        out_shape=[
            jax.ShapeDtypeStruct((rows, qkv.shape[1] // 3), bf16),
            jax.ShapeDtypeStruct((rows, 128), f32),
        ],
        compiler_params=pltpu.CompilerParams(
            dimension_semantics=("arbitrary", "arbitrary"), vmem_limit_bytes=40 << 20
        ),
        cost_estimate=cost(
            flops=5 * rows * ROWS * qkv.shape[1],
            bytes_accessed=rows * qkv.shape[1] * 3,
            transcendentals=rows * ROWS * qkv.shape[1] // 192,
        ),
        name="attend",
    )(qkv, fq, fk)


def split_three(value):
    first = value.astype(bf16)
    rest = value - first.astype(f32)
    second = rest.astype(bf16)
    third = (rest - second.astype(f32)).astype(bf16)
    return first, second, third


def attend_back_kernel(qkv_ref, do_ref, o_ref, fq_ref, fk_ref, lse_ref, dqkv_ref, ds_ref, *, chunk):
    pair = pl.program_id(1)
    lane = lax.broadcasted_iota(jnp.int32, (1, 128), 1)
    queries = qkv_ref[:, 0:128]
    grads = do_ref[...]
    marks = fq_ref[...]
    product = grads.astype(f32) * o_ref[...].astype(f32)
    lse = lse_ref[...]
    zero = jnp.zeros_like(queries)
    own_q, own_g, wide_q, wide_g = [], [], [], []
    for half in range(2):
        keep = (lane < 64) if half == 0 else (lane >= 64)
        shift = -jnp.sum(jnp.where(lane == pair * 2 + half, lse, 0.0), axis=1, keepdims=True)
        inner = -jnp.sum(jnp.where(keep, product, 0.0), axis=1, keepdims=True)
        s0, s1, s2 = split_three(shift)
        i0, i1, i2 = split_three(inner)
        mark_q = jnp.where(lane == 8, s0, jnp.where(lane == 9, s1, jnp.where(lane == 10, s2, marks)))
        mark_g = jnp.where(lane == 8, i0, jnp.where(lane == 9, i1, jnp.where(lane == 10, i2, zero)))
        q_half = jnp.where(keep, queries, zero)
        g_half = jnp.where(keep, grads, zero)
        own_q.append(q_half)
        own_g.append(g_half)
        wide_q.append(jnp.concatenate([q_half, mark_q], axis=1))
        wide_g.append(jnp.concatenate([g_half, mark_g], axis=1))
    for step in range(ROWS // chunk):
        rows = slice(step * chunk, (step + 1) * chunk)
        keys = jnp.concatenate([qkv_ref[rows, 128:256], fk_ref[rows, :]], axis=1)
        values = jnp.concatenate([qkv_ref[rows, 256:384], fk_ref[rows, :]], axis=1)
        dv = jnp.zeros((chunk, 128), f32)
        dk = jnp.zeros((chunk, 128), f32)
        for half in range(2):
            weights = jnp.exp2(dot(keys, wide_q[half], NT) * score_scale)
            ds = (weights * dot(values, wide_g[half], NT)).astype(bf16)
            ds_ref[half, rows, :] = ds
            dv = dv + dot(weights.astype(bf16), own_g[half])
            dk = dk + dot(ds, own_q[half])
        dqkv_ref[rows, 256:384] = dv.astype(bf16)
        dqkv_ref[rows, 128:256] = (dk * 0.125).astype(bf16)
    keys_t = qkv_ref[:, 128:256].T
    dq = [dot(keys_t, ds_ref[half]).T for half in range(2)]
    dqkv_ref[:, 0:128] = (jnp.where(lane < 64, dq[0], dq[1]) * 0.125).astype(bf16)


def attend_back(qkv, do, o, fq, fk, lse, first, chunk=640):
    rows = qkv.shape[0]
    mark = pl.BlockSpec((ROWS, 128), lambda b, p: (b, 0))
    wide = pl.BlockSpec((ROWS, 128), lambda b, p: (b, first + p))
    part = pl.BlockSpec((ROWS, 128), lambda b, p: (b, p))
    group = pl.BlockSpec((ROWS, GROUP), lambda b, p: (b, p))
    return pl.pallas_call(
        lambda *refs: attend_back_kernel(*refs, chunk=chunk),
        grid=(rows // ROWS, qkv.shape[1] // GROUP),
        in_specs=[group, wide, part, mark, mark, mark],
        out_specs=group,
        out_shape=jax.ShapeDtypeStruct(qkv.shape, bf16),
        scratch_shapes=[pltpu.VMEM((2, ROWS, ROWS), bf16)],
        compiler_params=pltpu.CompilerParams(
            dimension_semantics=("arbitrary", "arbitrary"), vmem_limit_bytes=40 << 20
        ),
        cost_estimate=cost(
            flops=12 * rows * ROWS * qkv.shape[1],
            bytes_accessed=rows * qkv.shape[1] * 6,
            transcendentals=rows * ROWS * qkv.shape[1] // 192,
        ),
        name="attend_back",
    )(qkv, do, o, fq, fk, lse)


def gelu_parts(u):
    z = jnp.abs(u) * 0.7071067811865476
    t = 1.0 / (1.0 + erf_p * z)
    e = jnp.exp2(u * u * (-0.5 * log2_e))
    series = t * (erf_a[0] + t * (erf_a[1] + t * (erf_a[2] + t * (erf_a[3] + t * erf_a[4]))))
    tail = 0.5 * series * e
    return jnp.where(u < 0, tail, 1.0 - tail), e * 0.3989422804014327


def feed_kernel(*refs, chunk, more):
    b_ref, gm_ref, up_ref, dn_ref, ub_ref = refs[:5]
    h_ref, db_ref, gu_ref, gd_ref, gub_ref, act_s, du_s = refs[-7:]
    j = pl.program_id(0)
    rows_all = b_ref.shape[0]
    up, dn, ub = up_ref[...], dn_ref[...], ub_ref[...]
    sums = jnp.zeros((1, ub.shape[1]), f32)
    for step in range(rows_all // chunk):
        rows = slice(step * chunk, (step + 1) * chunk)
        u = dot(b_ref[rows, :], up) + ub
        cdf, pdf = gelu_parts(u)
        act = (u * cdf).astype(bf16)
        du = (dot(gm_ref[rows, :], dn) * (cdf + u * pdf)).astype(bf16)
        sums = sums + jnp.sum(du.astype(f32), axis=0, keepdims=True)
        act_s[rows, :] = act
        du_s[rows, :] = du
        hh = dot(act, dn, NT)
        dd = dot(du, up, NT)

        @pl.when(j == 0)
        def _():
            h_ref[rows, :] = hh + refs[5][rows, :] if more else hh
            db_ref[rows, :] = dd + refs[6][rows, :] if more else dd

        @pl.when(j > 0)
        def _():
            h_ref[rows, :] += hh
            db_ref[rows, :] += dd

    gub_ref[...] = sums
    gu_ref[...] = dot(b_ref[...], du_s[...], TN).astype(bf16)
    gd_ref[...] = dot(gm_ref[...], act_s[...], TN).astype(bf16)


def feed(b, gm, up, dn, ub, before=(), block=512, chunk=640):
    rows = b.shape[0]
    hidden = up.shape[1]
    full = pl.BlockSpec((rows, D), lambda j: (0, 0), pipeline_mode=pl.Buffered(1))
    weight = pl.BlockSpec((D, block), lambda j: (0, j))
    bias = pl.BlockSpec((1, block), lambda j: (0, j))
    return pl.pallas_call(
        lambda *refs: feed_kernel(*refs, chunk=chunk, more=bool(before)),
        grid=(hidden // block,),
        in_specs=[full, full, weight, weight, bias] + [full] * len(before),
        out_specs=[full, full, weight, weight, bias],
        out_shape=[jax.ShapeDtypeStruct((rows, D), f32)] * 2
        + [jax.ShapeDtypeStruct(up.shape, bf16)] * 2
        + [jax.ShapeDtypeStruct(ub.shape, f32)],
        scratch_shapes=[pltpu.VMEM((rows, block), bf16)] * 2,
        compiler_params=pltpu.CompilerParams(
            dimension_semantics=("arbitrary",), vmem_limit_bytes=58 << 20
        ),
        cost_estimate=cost(
            flops=12 * rows * hidden * D,
            bytes_accessed=rows * D * 12 + hidden * D * 8,
            transcendentals=2 * rows * hidden,
        ),
        name="feed",
    )(b, gm, up, dn, ub, *before)


def pair_major(columns):
    lead = columns.shape[:-1]
    return columns.reshape(lead + (3, PAIRS, 128)).swapaxes(-3, -2).reshape(lead + (3 * D,))


def pair_minor(columns):
    lead = columns.shape[:-1]
    return columns.reshape(lead + (PAIRS, 3, 128)).swapaxes(-3, -2).reshape(lead + (3 * D,))


class Place:
    def __init__(self):
        dp, self.nx = lax.axis_size("dp"), lax.axis_size("mlp")
        self.ny, self.nc = 2, 2
        self.nz = dp // (self.ny * self.nc)
        index = lax.axis_index("dp")
        self.x = lax.axis_index("mlp")
        self.c = index % self.nc
        self.y = (index // self.nc) % self.ny
        self.z = index // (self.nc * self.ny)

    def send(self, value, move):
        pairs = []
        for z in range(self.nz):
            for y in range(self.ny):
                for c in range(self.nc):
                    for x in range(self.nx):
                        source = ((z * self.ny + y) * self.nc + c) * self.nx + x
                        z2, y2, c2, x2 = move(z, y, c, x)
                        pairs.append((source, ((z2 * self.ny + y2) * self.nc + c2) * self.nx + x2))
        return lax.ppermute(value, ("dp", "mlp"), pairs)

    def shift(self, value, dz=0, dy=0, dc=0, dx=0):
        return self.send(
            value,
            lambda z, y, c, x: (
                (z + dz) % self.nz,
                (y + dy) % self.ny,
                (c + dc) % self.nc,
                (x + dx) % self.nx,
            ),
        )


def spread_z(place, shard):
    return {k: place.shift(shard, dz=k) if k else shard for k in range(place.nz)}


def line_up(place, pieces):
    ids = jnp.arange(place.nz).reshape(place.nz, 1, 1)
    whole = jnp.broadcast_to(pieces[0][None], (place.nz,) + pieces[0].shape)
    for k in range(1, place.nz):
        whole = jnp.where(ids == (place.z - k) % place.nz, pieces[k][None], whole)
    return whole


def spread_plane(place, line, route):
    over_x = place.shift(line, dx=1)
    over_y = place.shift(line, dy=1)
    if route == "xy":
        both = place.shift(over_x, dy=1)
    elif route == "yx":
        both = place.shift(over_y, dx=1)
    else:
        both = place.shift(line, dx=1, dy=1)
    return {(0, 0): line, (1, 0): over_x, (0, 1): over_y, (1, 1): both}


def spread_cores(place, pieces):
    whole = {key + (0,): piece for key, piece in pieces.items()}
    whole.update({key + (1,): place.shift(piece, dc=1) for key, piece in pieces.items()})
    return whole


def assemble_kernel(*refs, keys, plan, nz, nx):
    sources, targets = refs[: len(keys)], refs[len(keys) :]
    index = lax.axis_index("dp")
    here = {"x": lax.axis_index("mlp"), "c": index % 2, "y": (index // 2) % 2, "z": index // 4}
    many = {"x": nx, "c": 2, "y": 2, "z": nz}

    def at(axis, distance):
        return lax.rem(here[axis] + many[axis] - distance, many[axis])

    for source, key in zip(sources, keys):
        for target, (order, moves) in zip(targets, plan):
            for rows, columns, to in moves:
                if "z" in key:
                    for i, (dx, dy) in enumerate(((0, 0), (1, 0), (0, 1), (1, 1))):
                        spot = {"x": at("x", dx), "y": at("y", dy), "z": at("z", key["z"]), "c": at("c", key["c"])}
                        target[tuple(spot[axis] for axis in order) + (slice(None), to)] = source[i, rows, columns]
                else:
                    spot = {axis: at(axis, key[axis]) for axis in key}
                    spot["z"] = slice(None)
                    target[tuple(spot[axis] for axis in order) + (slice(None), to)] = source[:, rows, columns]


def assemble(place, pieces, names, plan):
    keys = [dict(zip(names, key)) for key in pieces]
    arrays = list(pieces.values())
    many = {"x": place.nx, "y": place.ny, "c": place.nc, "z": place.nz}
    shapes = []
    for order, moves in plan:
        rows = moves[0][0].stop - moves[0][0].start
        columns = max(to.stop for _, _, to in moves)
        shapes.append(tuple(many[axis] for axis in order) + (rows, columns))
    size = sum(math.prod(shape) for shape in shapes)
    out = pl.pallas_call(
        lambda *refs: assemble_kernel(*refs, keys=keys, plan=plan, nz=place.nz, nx=place.nx),
        in_specs=[pl.BlockSpec(memory_space=pltpu.VMEM)] * len(arrays),
        out_specs=[pl.BlockSpec(memory_space=pltpu.VMEM)] * len(plan),
        out_shape=[jax.ShapeDtypeStruct(shape, bf16) for shape in shapes],
        compiler_params=pltpu.CompilerParams(vmem_limit_bytes=40 << 20),
        cost_estimate=cost(flops=0, bytes_accessed=4 * size, transcendentals=0),
        name="assemble",
    )(*arrays)
    return [item.reshape(-1, item.shape[-1]) for item in out]


def after(value, *others):
    return lax.optimization_barrier((value,) + others)[0]


class Scatter:
    def __init__(self, place, whole, order):
        self.place, self.total, self.axes = place, whole, order

    def hop(self, axis):
        place = self.place
        here = getattr(place, axis)
        many = getattr(place, "n" + axis)
        at = self.axes.index(axis)
        own = lax.dynamic_index_in_dim(self.total, here, at, keepdims=False).astype(f32)
        moved = []
        for k in range(1, many):
            theirs = lax.dynamic_index_in_dim(self.total, (here + k) % many, at, keepdims=False)
            moved.append(place.shift(theirs.astype(bf16), **{"d" + axis: k}))
            own = own + moved[-1].astype(f32)
        self.total, self.axes = own, self.axes.replace(axis, "")
        return moved

    def join(self, other):
        moved = self.place.shift(other.total.astype(bf16), dx=1)
        self.total = self.total.astype(f32) + moved.astype(f32)
        return [moved]


def add_all(place, value):
    half = value.shape[0] // place.nc
    parts = value.reshape((place.nc, half) + value.shape[1:])
    own = lax.dynamic_index_in_dim(parts, place.c, 0, keepdims=False)
    other = lax.dynamic_index_in_dim(parts, 1 - place.c, 0, keepdims=False)
    total = own + place.shift(other, dc=1)
    total = total + place.shift(total, dx=1)
    total = total + place.shift(total, dy=1)
    bit = 1
    while bit < place.nz:
        total = total + place.send(total, lambda z, y, c, x, bit=bit: (z ^ bit, y, c, x))
        bit *= 2
    other = place.shift(total, dc=1)
    return jnp.where(
        place.c == 0, jnp.concatenate([total, other], 0), jnp.concatenate([other, total], 0)
    )


def per_device(
    tokens,
    cotangent,
    lengths,
    buckets,
    pos_table,
    prompts,
    norm1_gain,
    norm1_bias,
    qkv_weight,
    q_bias,
    v_bias,
    out_weight,
    out_bias,
    norm2_gain,
    norm2_bias,
    up_weight,
    up_bias,
    down_weight,
    down_bias,
):
    mlp_size = lax.axis_size("mlp")
    micro_count, local_rows = tokens.shape[:2]
    rows = micro_count * local_rows
    hidden_local = up_weight.shape[1]
    hidden = hidden_local * mlp_size

    place = Place()
    rows_in = qkv_weight.shape[0]
    rows_up = up_weight.shape[0]
    qkv_shard = pair_major(qkv_weight)
    cut = FIRST * GROUP
    pack_one = jnp.concatenate([qkv_shard[:, :cut], out_weight], axis=1)
    pack_two = qkv_shard[:, cut:]
    line_one = line_up(place, spread_z(place, pack_one))
    line_two = line_up(place, spread_z(place, pack_two))
    whole_one = spread_cores(place, spread_plane(place, line_one, ""))
    whole_two = spread_cores(place, spread_plane(place, line_two, ""))
    every = slice(0, rows_in)
    qkv_one, out_full = assemble(
        place,
        whole_one,
        "xyc",
        [
            ("zycx", [(every, slice(0, cut), slice(0, cut))]),
            ("zycx", [(every, slice(cut, cut + D), slice(0, D))]),
        ],
    )
    (qkv_two,) = assemble(
        place, whole_two, "xyc", [("zycx", [(every, slice(0, 3 * D - cut), slice(0, 3 * D - cut))])]
    )

    up_pack, down_pack, _ = lax.optimization_barrier((up_weight, down_weight.T, line_two))
    up_line = line_up(place, spread_z(place, up_pack))
    down_line = line_up(place, spread_z(place, down_pack))
    own_keys, other_keys = ((0, 0), (0, 1)), ((1, 0), (1, 1))
    up_plane = spread_plane(place, up_line, "yx")
    down_plane = spread_plane(place, down_line, "yx")

    def feed_weights(keys):
        plan = [("zyc", [(slice(0, rows_up), slice(0, hidden_local), slice(0, hidden_local))])]
        found = []
        for plane in (up_plane, down_plane):
            pieces = spread_cores(place, {(key[1],): plane[key] for key in keys})
            found += assemble(place, pieces, "yc", plan)
        return found

    up_own, down_own = feed_weights(own_keys)
    up_other, down_other = feed_weights(other_keys)
    shift_own = up_bias.astype(f32)[None, :]
    shift_other = place.shift(up_bias, dx=1).astype(f32)[None, :]

    def line_of(value):
        return value.astype(f32)[None, :]

    buffer_lengths, buffer_buckets = lengths.reshape(-1, SLOTS), buckets.reshape(-1)
    table = jnp.pad(
        jnp.concatenate([pos_table, prompts], axis=0), ((0, 1024 - TABLE - PROMPTS), (0, 0))
    )
    gain_one, gain_two = line_of(norm1_gain), line_of(norm2_gain)
    qkv_offset = pair_major(
        jnp.concatenate([line_of(q_bias), jnp.zeros((1, D), f32), line_of(v_bias)], axis=1)
    )
    start_rows, normed, grad_branch, fq, fk, grad_down_shift = embed(
        buffer_lengths, buffer_buckets, tokens.reshape(rows, D), cotangent.reshape(rows, D), table,
        gain_one, line_of(norm1_bias),
    )

    qkv_one_rows = (dot(normed, qkv_one) + qkv_offset[:, :cut]).astype(bf16)
    attended_one, log_one = attend(qkv_one_rows, fq, fk)
    qkv_two_rows = (dot(normed, qkv_two) + qkv_offset[:, cut:]).astype(bf16)
    attended_two, log_two = attend(qkv_two_rows, fq, fk)
    first_sum, normed_two = middle(
        attended_one, attended_two, out_full, start_rows, line_of(out_bias), gain_two, line_of(norm2_bias)
    )
    *sums, grad_up_own, grad_down_own, shift_grad_own = feed(
        normed_two, grad_branch, up_own, down_own, shift_own
    )

    def parts(value, order):
        many = {"x": place.nx, "y": place.ny, "c": place.nc, "z": place.nz}
        return value.reshape(tuple(many[axis] for axis in order) + (-1, value.shape[-1]))

    send_up = Scatter(place, parts(grad_up_own, "zyc"), "zyc")
    send_down = Scatter(place, parts(grad_down_own, "zyc"), "zyc")
    cores_own = send_up.hop("c") + send_down.hop("c")
    branch, grad_normed, grad_up_other, grad_down_other, shift_grad_other = feed(
        normed_two, grad_branch, up_other, down_other, shift_other, tuple(sums)
    )
    grad_up_shift = jnp.where(
        place.x == 0,
        jnp.concatenate([shift_grad_own, shift_grad_other], axis=1),
        jnp.concatenate([shift_grad_other, shift_grad_own], axis=1),
    )
    other_up = Scatter(place, parts(grad_up_other, "zyc"), "zyc")
    other_down = Scatter(place, parts(grad_down_other, "zyc"), "zyc")
    planes_own = send_up.hop("y")
    cores = other_up.hop("c") + other_down.hop("c")
    output, grad_one, grad_attended, grad_out, early = middle_back(
        buffer_lengths, buffer_buckets, first_sum, branch, grad_normed, grad_branch, attended_one,
        attended_two, out_full, gain_two, line_of(down_bias), grad_down_shift, grad_up_shift,
    )
    grad_attended = after(grad_attended, *cores, *planes_own)
    planes_one = other_up.hop("y") + send_down.join(other_down)
    back_two = attend_back(qkv_two_rows, grad_attended, attended_two, fq, fk, log_two, FIRST)
    grad_qkv_two = dot(normed, back_two, TN).astype(bf16)
    wide = jnp.concatenate([grad_qkv_two, grad_out], axis=1)
    grad_attended = after(grad_attended, wide, *planes_one)
    send_two = Scatter(place, parts(wide, "zycx"), "zycx")
    planes_two = send_up.join(other_up) + send_down.hop("y") + send_two.hop("c")
    back_one = attend_back(qkv_one_rows, grad_attended, attended_one, fq, fk, log_one, 0)
    back_one = after(back_one, *planes_two)
    lines_one = send_up.hop("z") + send_down.hop("z") + send_two.hop("y")
    input_grad, packed = finish(
        buffer_lengths, buffer_buckets, back_one, back_two, qkv_one, qkv_two, start_rows, grad_one,
        gain_one, early,
    )
    grad_qkv_one = dot(normed, back_one, TN).astype(bf16)
    send_one = Scatter(place, parts(grad_qkv_one, "zycx"), "zycx")
    lines_one += send_one.hop("c")
    packed = after(packed, *lines_one)
    for axis in "xyz":
        send_one.hop(axis)
    for axis in "xz":
        send_two.hop(axis)
    summed = add_all(place, packed)
    part_one, part_two = send_one.total, send_two.total
    rest = 3 * D - cut
    qkv_weight_grad = pair_minor(jnp.concatenate([part_one, part_two[:, :rest]], axis=1))
    out_weight_grad = part_two[:, rest:]
    up_weight_grad = send_up.total
    down_weight_grad = send_down.total.T
    singles = [summed[PROMPTS + i] for i in range(8)]
    up_bias_grad = lax.dynamic_slice_in_dim(
        summed[PROMPTS + 8 : PROMPTS + 12].reshape(hidden), lax.axis_index("mlp") * hidden_local, hidden_local, 0
    )
    return (
        output.reshape(tokens.shape),
        input_grad.reshape(tokens.shape),
        summed[:PROMPTS],
        singles[0],
        singles[1],
        qkv_weight_grad,
        singles[2],
        singles[3],
        out_weight_grad,
        singles[4],
        singles[5],
        singles[6],
        up_weight_grad,
        up_bias_grad,
        down_weight_grad,
        singles[7],
    )


def solution(mesh):
    both = ("dp", "mlp")
    in_specs = (
        P(None, both, None),
        P(None, both, None),
        P(None, both, None),
        P(None, both),
        P(),
        P(),
        P(),
        P(),
        P(both, None),
        P(),
        P(),
        P(both, None),
        P(),
        P(),
        P(),
        P("dp", "mlp"),
        P("mlp"),
        P("mlp", "dp"),
        P(),
    )
    out_specs = (
        P(None, both, None),
        P(None, both, None),
        P(),
        P(),
        P(),
        P(both, None),
        P(),
        P(),
        P(both, None),
        P(),
        P(),
        P(),
        P("dp", "mlp"),
        P("mlp"),
        P("mlp", "dp"),
        P(),
    )
    return jax.shard_map(
        per_device, mesh=mesh, in_specs=in_specs, out_specs=out_specs, check_vma=False
    )
```

```python
import math

import jax
import jax.numpy as jnp
from jax import lax
from jax.experimental import pallas as pl
from jax.experimental.pallas import tpu as pltpu
from jax.sharding import PartitionSpec as P

D = 768
HEADS = 12
HEAD_DIM = 64
PAIRS = 6
PROMPTS = 50
LEN_LOW = 101
LEN_MID = 197
TABLE = 875
SLOTS = 4
ROWS = 640
GROUP = 3 * 128
PACK = 64
BLOCK = 320
weigh = 5
FIRST = 2
GAIN_ONE, SHIFT_ONE, OUT_BIAS, GAIN_TWO, SHIFT_TWO, DOWN_BIAS = (slice(i, i + 1) for i in range(6))

epsilon = 1e-06
bf16 = jnp.bfloat16
f32 = jnp.float32
log2_e = 1.4426950408889634
score_scale = log2_e / math.sqrt(HEAD_DIM)
erf_p = 0.3275911
erf_a = (0.254829592, -0.284496736, 1.421413741, -1.453152027, 1.061405429)

NT = (((1,), (1,)), ((), ()))
NN = (((1,), (0,)), ((), ()))
TN = (((0,), (0,)), ((), ()))


def cost(flops, bytes_accessed, transcendentals):
    return pl.CostEstimate(
        flops=weigh * flops, bytes_accessed=weigh * bytes_accessed, transcendentals=weigh * transcendentals
    )


def dot(left, right, dims=NN):
    return lax.dot_general(left, right, dims, preferred_element_type=f32)


def row_plan(lengths_ref, buckets_ref, buffer, rows):
    sequence = jnp.zeros_like(rows)
    start = jnp.zeros_like(rows)
    end = 0
    for slot in range(SLOTS):
        length = lengths_ref[buffer, slot]
        end = end + jnp.where(length > 0, length + PROMPTS, 0)
        sequence = sequence + jnp.where(end <= rows, 1, 0)
        start = jnp.where(end <= rows, end, start)
    position = rows - start
    bucket = buckets_ref[buffer]
    table = jnp.where(bucket == 0, 0, jnp.where(bucket == 1, LEN_LOW, LEN_LOW + LEN_MID))
    inside = sequence < SLOTS
    prompt = inside & (position < PROMPTS)
    image = inside & (position >= PROMPTS)
    index = jnp.where(
        prompt,
        TABLE + position,
        jnp.where(image, jnp.clip(table + position - PROMPTS, 0, TABLE - 1), -1),
    )
    return sequence, position, inside, prompt, image, index


def norm_stats(values_in):
    average = jnp.mean(values_in, axis=-1, keepdims=True)
    centred = values_in - average
    variance = jnp.mean(centred * centred, axis=-1, keepdims=True)
    inverse = lax.rsqrt(variance + epsilon)
    return centred * inverse, inverse


def norm_back(grad_normed, normal, inverse, gain):
    scaled = grad_normed * gain
    mean_one = jnp.mean(scaled, axis=-1, keepdims=True)
    mean_two = jnp.mean(scaled * normal, axis=-1, keepdims=True)
    return (scaled - mean_one - normal * mean_two) * inverse


def add_rows(ref, step, row, value):
    total = jnp.sum(value, axis=0, keepdims=True)

    @pl.when(step == 0)
    def _():
        ref[row : row + 1, :] = total

    @pl.when(step > 0)
    def _():
        ref[row : row + 1, :] += total


def block_rows(shape, axis):
    step = pl.program_id(0)
    per = ROWS // BLOCK
    ids = lax.broadcasted_iota(jnp.int32, shape, axis) + lax.rem(step, per) * BLOCK
    return lax.div(step, per), ids


def embed_kernel(
    lengths_ref, buckets_ref, tokens_ref, cot_ref, table_ref,
    h_ref, a_ref, gm_ref, fq_ref, fk_ref, sum_ref,
):
    buffer, ids = block_rows((BLOCK, 1), 0)
    lane = lax.broadcasted_iota(jnp.int32, (1, 128), 1)
    sequence, _, inside, _, image, index = row_plan(lengths_ref, buckets_ref, buffer, ids)
    places = lax.broadcasted_iota(jnp.int32, (1, table_ref.shape[0]), 1)
    hits = jnp.where(places == index, 1.0, 0.0).astype(bf16)
    start = dot(hits, table_ref[...]) + jnp.where(image, tokens_ref[...].astype(f32), 0.0)
    h_ref[...] = start
    normal, _ = norm_stats(start)
    last = TABLE + PROMPTS
    gain = table_ref[last : last + 1, :].astype(f32)
    shift = table_ref[last + 1 : last + 2, :].astype(f32)
    a_ref[...] = (normal * gain + shift).astype(bf16)
    grad = jnp.where(inside, cot_ref[...].astype(f32), 0.0)
    gm_ref[...] = grad.astype(bf16)
    same = lane == sequence
    fq_ref[...] = jnp.where(same, 1.0, 0.0).astype(bf16)
    ones = jnp.where((lane >= 8) & (lane < 11), 1.0, 0.0)
    fk_ref[...] = jnp.where((lane <= SLOTS) & ~same, -1e30, ones).astype(bf16)
    add_rows(sum_ref, pl.program_id(0), 0, grad)


def whole_spec(shape):
    return pl.BlockSpec(shape, lambda b: (0,) * len(shape), pipeline_mode=pl.Buffered(1))


def scalar_spec():
    return pl.BlockSpec(memory_space=pltpu.SMEM)


def buffer_spec(columns):
    return pl.BlockSpec((BLOCK, columns), lambda b: (b, 0))


def buffer_params():
    return pltpu.CompilerParams(dimension_semantics=("arbitrary",), vmem_limit_bytes=56 << 20)


def embed(lengths, buckets, tokens, cotangent, table):
    rows = tokens.shape[0]
    kept = whole_spec((1, D))
    return pl.pallas_call(
        embed_kernel,
        grid=(rows // BLOCK,),
        in_specs=[
            scalar_spec(), scalar_spec(), buffer_spec(D), buffer_spec(D), whole_spec(table.shape),
        ],
        out_specs=[buffer_spec(D), buffer_spec(D), buffer_spec(D), buffer_spec(128), buffer_spec(128), kept],
        out_shape=[
            jax.ShapeDtypeStruct((rows, D), f32),
            jax.ShapeDtypeStruct((rows, D), bf16),
            jax.ShapeDtypeStruct((rows, D), bf16),
            jax.ShapeDtypeStruct((rows, 128), bf16),
            jax.ShapeDtypeStruct((rows, 128), bf16),
            jax.ShapeDtypeStruct((1, D), f32),
        ],
        compiler_params=buffer_params(),
        cost_estimate=cost(
            flops=2 * rows * table.shape[0] * D, bytes_accessed=rows * D * 12, transcendentals=0
        ),
        name="embed",
    )(lengths, buckets, tokens, cotangent, table)


def middle_kernel(o1_ref, o2_ref, w_ref, h_ref, vec_ref, h1_ref, b_ref):
    cut = o1_ref.shape[1]
    mixed = dot(o1_ref[...], w_ref[:cut, :]) + dot(o2_ref[...], w_ref[cut:, :])
    total = h_ref[...] + mixed + vec_ref[OUT_BIAS]
    h1_ref[...] = total
    normal, _ = norm_stats(total)
    b_ref[...] = (normal * vec_ref[GAIN_TWO] + vec_ref[SHIFT_TWO]).astype(bf16)


def middle(o1, o2, weight, start, vectors):
    rows = start.shape[0]
    return pl.pallas_call(
        middle_kernel,
        grid=(rows // BLOCK,),
        in_specs=[
            buffer_spec(o1.shape[1]), buffer_spec(o2.shape[1]), whole_spec((D, D)), buffer_spec(D), whole_spec((8, D)),
        ],
        out_specs=[buffer_spec(D), buffer_spec(D)],
        out_shape=[jax.ShapeDtypeStruct((rows, D), f32), jax.ShapeDtypeStruct((rows, D), bf16)],
        compiler_params=buffer_params(),
        cost_estimate=cost(
            flops=2 * rows * D * D, bytes_accessed=rows * D * 12, transcendentals=0
        ),
        name="middle",
    )(o1, o2, weight, start, vectors)


def middle_back_kernel(
    lengths_ref, buckets_ref, h1_ref, branch_ref, db_ref, gm_ref, o1_ref, o2_ref, w_ref, vec_ref,
    gdown_ref, gup_ref, out_ref, g1_ref, do_ref, gw_ref, early_ref, gw_s,
):
    step = pl.program_id(0)
    cut = o1_ref.shape[1]
    buffer, ids = block_rows((BLOCK, 1), 0)
    _, _, inside, _, _, _ = row_plan(lengths_ref, buckets_ref, buffer, ids)
    h1 = h1_ref[...]
    out_ref[...] = jnp.where(inside, h1 + branch_ref[...] + vec_ref[DOWN_BIAS], 0.0).astype(bf16)
    normal, inverse = norm_stats(h1)
    db = db_ref[...]
    g1 = gm_ref[...].astype(f32) + norm_back(db, normal, inverse, vec_ref[GAIN_TWO])
    g1_ref[...] = g1
    ga = g1.astype(bf16)
    do_ref[...] = dot(ga, w_ref[...], NT).astype(bf16)
    for row, value in ((0, g1), (1, db * normal), (2, db)):
        add_rows(early_ref, step, row, value)
    first = dot(o1_ref[...], ga, TN)
    second = dot(o2_ref[...], ga, TN)

    @pl.when(step == 0)
    def _():
        gw_s[:cut, :] = first
        gw_s[cut:, :] = second

    @pl.when(step > 0)
    def _():
        gw_s[:cut, :] += first
        gw_s[cut:, :] += second

    @pl.when(step == pl.num_programs(0) - 1)
    def _():
        gw_ref[...] = gw_s[...].astype(bf16)
        early_ref[3:4, :] = gdown_ref[...]
        for i in range(gup_ref.shape[1] // D):
            early_ref[4 + i : 5 + i, :] = gup_ref[:, i * D : (i + 1) * D]


def middle_back(
    lengths, buckets, h1, branch, db, gm, o1, o2, weight, vectors, grad_down, grad_up
):
    rows = h1.shape[0]
    kept = whole_spec((1, D))
    wide = buffer_spec(D)
    square = whole_spec((D, D))
    return pl.pallas_call(
        middle_back_kernel,
        grid=(rows // BLOCK,),
        in_specs=[
            scalar_spec(), scalar_spec(), wide, wide, wide, wide, buffer_spec(o1.shape[1]),
            buffer_spec(o2.shape[1]), square, whole_spec((8, D)), kept, whole_spec(grad_up.shape),
        ],
        out_specs=[wide, wide, wide, square, whole_spec((8, D))],
        out_shape=[
            jax.ShapeDtypeStruct((rows, D), bf16),
            jax.ShapeDtypeStruct((rows, D), f32),
            jax.ShapeDtypeStruct((rows, D), bf16),
            jax.ShapeDtypeStruct((D, D), bf16),
            jax.ShapeDtypeStruct((8, D), f32),
        ],
        scratch_shapes=[pltpu.VMEM((D, D), f32)],
        compiler_params=buffer_params(),
        cost_estimate=cost(
            flops=4 * rows * D * D, bytes_accessed=rows * D * 26, transcendentals=0
        ),
        name="middle_back",
    )(lengths, buckets, h1, branch, db, gm, o1, o2, weight, vectors, grad_down, grad_up)


def finish_kernel(*refs, plan):
    lengths_ref, buckets_ref, h_ref, g1_ref, vec_ref, early_ref = refs[:6]
    grads, sums_in, weights = refs[6 : 6 + len(plan)], refs[6 + len(plan) : 6 + 2 * len(plan)], refs[6 + 2 * len(plan) : -2]
    input_ref, pack_ref = refs[-2:]
    step = pl.program_id(0)
    count = pack_ref.shape[0]
    buffer, ids = block_rows((BLOCK, 1), 0)
    _, _, _, _, image, _ = row_plan(lengths_ref, buckets_ref, buffer, ids)
    da = 0.0
    for grad, (which, at) in zip(grads, plan):
        da = da + dot(grad[...], weights[which][:, at : at + grad.shape[1]], NT)
    normal, inverse = norm_stats(h_ref[...])
    g0 = g1_ref[...] + norm_back(da, normal, inverse, vec_ref[GAIN_ONE])
    input_ref[...] = jnp.where(image, g0, 0.0)
    _, across = block_rows((1, BLOCK), 1)
    _, position, _, prompt, _, _ = row_plan(lengths_ref, buckets_ref, buffer, across)
    wanted = lax.broadcasted_iota(jnp.int32, (count, 1), 0)
    hits = jnp.where(prompt & (wanted == position), 1.0, 0.0).astype(bf16)
    sums = sum(dot(hits, part) for part in split_three(g0)[:2])
    lines = [jnp.sum(da * normal, axis=0, keepdims=True), jnp.sum(da, axis=0, keepdims=True)]
    for row, line in enumerate(lines):
        sums = jnp.where(wanted == PROMPTS + row, line, sums)

    @pl.when(step == 0)
    def _():
        pack_ref[...] = sums

    @pl.when(step > 0)
    def _():
        pack_ref[...] += sums

    @pl.when(step == pl.num_programs(0) - 1)
    def _():
        at = 0
        for ref in sums_in:
            for pair in range(ref.shape[1] // GROUP):
                to = slice(at, at + 128)
                at += 128
                for row, part in ((PROMPTS + 2, 0), (PROMPTS + 3, 2)):
                    lanes = slice(pair * GROUP + part * 128, pair * GROUP + part * 128 + 128)
                    pack_ref[row : row + 1, to] = ref[0:1, lanes]
        pack_ref[PROMPTS + 4 : PROMPTS + 12, :] = early_ref[...]


def finish(lengths, buckets, start, g1, vectors, early, grads, sums, weights, plan):
    rows = start.shape[0]
    wide = buffer_spec(D)
    return pl.pallas_call(
        lambda *refs: finish_kernel(*refs, plan=plan),
        grid=(rows // BLOCK,),
        in_specs=[scalar_spec(), scalar_spec(), wide, wide, whole_spec((8, D)), whole_spec((8, D))]
        + [buffer_spec(item.shape[1]) for item in grads]
        + [whole_spec(item.shape) for item in sums]
        + [whole_spec(item.shape) for item in weights],
        out_specs=[wide, whole_spec((PACK, D))],
        out_shape=[jax.ShapeDtypeStruct((rows, D), f32), jax.ShapeDtypeStruct((PACK, D), f32)],
        compiler_params=buffer_params(),
        cost_estimate=cost(
            flops=6 * rows * D * D, bytes_accessed=rows * D * 18, transcendentals=0
        ),
        name="finish",
    )(lengths, buckets, start, g1, vectors, early, *grads, *sums, *weights)


def attend_kernel(qkv_ref, fq_ref, fk_ref, o_ref, lse_ref, *, chunk):
    pair = pl.program_id(1)
    lane = lax.broadcasted_iota(jnp.int32, (1, 128), 1)
    keys = jnp.concatenate([qkv_ref[:, 128:256], fk_ref[...]], axis=1)
    values = jnp.concatenate([qkv_ref[:, 256:384], jnp.ones((ROWS, 128), bf16)], axis=1)
    for step in range(ROWS // chunk):
        rows = slice(step * chunk, (step + 1) * chunk)
        queries = qkv_ref[rows, 0:128]
        marks = fq_ref[rows, :]
        outs = []
        lse = lse_ref[rows, :]
        for half in range(2):
            keep = (lane < 64) if half == 0 else (lane >= 64)
            own = jnp.concatenate([jnp.where(keep, queries, jnp.zeros_like(queries)), marks], axis=1)
            scores = dot(own, keys, NT)
            top = jnp.max(scores, axis=1, keepdims=True)
            weights = jnp.exp2((scores - top) * score_scale)
            mixed = dot(weights.astype(bf16), values)
            total = mixed[:, 128:129]
            outs.append(mixed[:, :128] / total)
            log_total = top + jnp.log2(total) * (1.0 / score_scale)
            lse = jnp.where(lane == pair * 2 + half, log_total, lse)
        o_ref[rows, :] = jnp.where(lane < 64, outs[0], outs[1]).astype(bf16)
        lse_ref[rows, :] = lse


def attend(qkv, fq, fk, chunk=320):
    rows = qkv.shape[0]
    mark = pl.BlockSpec((ROWS, 128), lambda b, p: (b, 0))
    return pl.pallas_call(
        lambda *refs: attend_kernel(*refs, chunk=chunk),
        grid=(rows // ROWS, qkv.shape[1] // GROUP),
        in_specs=[pl.BlockSpec((ROWS, GROUP), lambda b, p: (b, p)), mark, mark],
        out_specs=[pl.BlockSpec((ROWS, 128), lambda b, p: (b, p)), mark],
        out_shape=[
            jax.ShapeDtypeStruct((rows, qkv.shape[1] // 3), bf16),
            jax.ShapeDtypeStruct((rows, 128), f32),
        ],
        compiler_params=pltpu.CompilerParams(
            dimension_semantics=("arbitrary", "arbitrary"), vmem_limit_bytes=40 << 20
        ),
        cost_estimate=cost(
            flops=5 * rows * ROWS * qkv.shape[1],
            bytes_accessed=rows * qkv.shape[1] * 3,
            transcendentals=rows * ROWS * qkv.shape[1] // 192,
        ),
        name="attend",
    )(qkv, fq, fk)


def split_three(value):
    first = value.astype(bf16)
    rest = value - first.astype(f32)
    second = rest.astype(bf16)
    third = (rest - second.astype(f32)).astype(bf16)
    return first, second, third


def attend_back_kernel(
    qkv_ref, do_ref, o_ref, fq_ref, fk_ref, lse_ref, dqkv_ref, sum_ref, ds_ref, *, chunk, low
):
    pair, buffer = low + pl.program_id(0), pl.program_id(1)
    lane = lax.broadcasted_iota(jnp.int32, (1, 128), 1)
    queries = qkv_ref[:, 0:128]
    grads = do_ref[...]
    marks = fq_ref[...]
    product = grads.astype(f32) * o_ref[...].astype(f32)
    lse = lse_ref[...]
    zero = jnp.zeros_like(queries)
    own_q, own_g, wide_q, wide_g = [], [], [], []
    for half in range(2):
        keep = (lane < 64) if half == 0 else (lane >= 64)
        shift = -jnp.sum(jnp.where(lane == pair * 2 + half, lse, 0.0), axis=1, keepdims=True)
        inner = -jnp.sum(jnp.where(keep, product, 0.0), axis=1, keepdims=True)
        s0, s1, s2 = split_three(shift)
        i0, i1, i2 = split_three(inner)
        mark_q = jnp.where(lane == 8, s0, jnp.where(lane == 9, s1, jnp.where(lane == 10, s2, marks)))
        mark_g = jnp.where(lane == 8, i0, jnp.where(lane == 9, i1, jnp.where(lane == 10, i2, zero)))
        q_half = jnp.where(keep, queries, zero)
        g_half = jnp.where(keep, grads, zero)
        own_q.append(q_half)
        own_g.append(g_half)
        wide_q.append(jnp.concatenate([q_half, mark_q], axis=1))
        wide_g.append(jnp.concatenate([g_half, mark_g], axis=1))
    for step in range(ROWS // chunk):
        rows = slice(step * chunk, (step + 1) * chunk)
        keys = jnp.concatenate([qkv_ref[rows, 128:256], fk_ref[rows, :]], axis=1)
        values = jnp.concatenate([qkv_ref[rows, 256:384], fk_ref[rows, :]], axis=1)
        dv = jnp.zeros((chunk, 128), f32)
        dk = jnp.zeros((chunk, 128), f32)
        for half in range(2):
            weights = jnp.exp2(dot(keys, wide_q[half], NT) * score_scale)
            ds = (weights * dot(values, wide_g[half], NT)).astype(bf16)
            ds_ref[half, rows, :] = ds
            dv = dv + dot(weights.astype(bf16), own_g[half])
            dk = dk + dot(ds, own_q[half])
        dqkv_ref[rows, 256:384] = dv.astype(bf16)
        dqkv_ref[rows, 128:256] = (dk * 0.125).astype(bf16)
        line = jnp.sum(dv, axis=0, keepdims=True)
        dv_sum = dv_sum + line if step else line
    keys_t = qkv_ref[:, 128:256].T
    parts = [dot(keys_t, ds_ref[half]).T for half in range(2)]
    dq = jnp.where(lane < 64, parts[0], parts[1]) * 0.125
    dqkv_ref[:, 0:128] = dq.astype(bf16)
    dq_sum = jnp.sum(dq, axis=0, keepdims=True)

    @pl.when(buffer == 0)
    def _():
        sum_ref[0:1, 0:128] = dq_sum
        sum_ref[0:1, 256:384] = dv_sum

    @pl.when(buffer > 0)
    def _():
        sum_ref[0:1, 0:128] += dq_sum
        sum_ref[0:1, 256:384] += dv_sum


def attend_back(qkv, do, o, fq, fk, lse, first, pairs, chunk=640):
    rows = qkv.shape[0]
    low, count = pairs[0], pairs[1] - pairs[0]
    columns = count * GROUP
    mark = pl.BlockSpec((ROWS, 128), lambda p, b: (b, 0))
    wide = pl.BlockSpec((ROWS, 128), lambda p, b: (b, first + low + p))
    part = pl.BlockSpec((ROWS, 128), lambda p, b: (b, low + p))
    return pl.pallas_call(
        lambda *refs: attend_back_kernel(*refs, chunk=chunk, low=low),
        grid=(count, rows // ROWS),
        in_specs=[pl.BlockSpec((ROWS, GROUP), lambda p, b: (b, low + p)), wide, part, mark, mark, mark],
        out_specs=[
            pl.BlockSpec((ROWS, GROUP), lambda p, b: (b, p)),
            pl.BlockSpec((8, GROUP), lambda p, b: (0, p)),
        ],
        out_shape=[
            jax.ShapeDtypeStruct((rows, columns), bf16),
            jax.ShapeDtypeStruct((8, columns), f32),
        ],
        scratch_shapes=[pltpu.VMEM((2, ROWS, ROWS), bf16)],
        compiler_params=pltpu.CompilerParams(
            dimension_semantics=("arbitrary", "arbitrary"), vmem_limit_bytes=40 << 20
        ),
        cost_estimate=cost(
            flops=12 * rows * ROWS * columns,
            bytes_accessed=rows * columns * 6,
            transcendentals=rows * ROWS * columns // 192,
        ),
        name="attend_back",
    )(qkv, do, o, fq, fk, lse)


def gelu_parts(u):
    z = jnp.abs(u) * 0.7071067811865476
    t = 1.0 / (1.0 + erf_p * z)
    e = jnp.exp2(u * u * (-0.5 * log2_e))
    series = t * (erf_a[0] + t * (erf_a[1] + t * (erf_a[2] + t * (erf_a[3] + t * erf_a[4]))))
    tail = 0.5 * series * e
    return jnp.where(u < 0, tail, 1.0 - tail), e * 0.3989422804014327


def store_halves(mine_ref, theirs_ref, value, rows):
    columns = value.shape[-1]
    grid = value.reshape(-1, 2, 2, rows, columns)
    first = lax.rem(lax.axis_index("dp"), 2) == 0
    for y in range(2):
        left, right = grid[:, y, 0].reshape(-1, columns), grid[:, y, 1].reshape(-1, columns)
        mine_ref[y] = jnp.where(first, left, right).astype(bf16)
        theirs_ref[y] = jnp.where(first, right, left).astype(bf16)


def feed_kernel(*refs, chunk, more, rows_up):
    b_ref, gm_ref, up_ref, dn_ref, ub_ref = refs[:5]
    outs = refs[5 + 2 * more : -2]
    h_ref, db_ref, gub_ref = outs[:3]
    act_s, du_s = refs[-2:]
    up, dn, ub = up_ref[...], dn_ref[...], ub_ref[...]

    @pl.when(pl.program_id(0) == 0)
    def _():
        h_ref[...] = refs[5][...] if more else jnp.zeros_like(h_ref)
        db_ref[...] = refs[6][...] if more else jnp.zeros_like(db_ref)

    sums = jnp.zeros((1, ub.shape[1]), f32)
    chunks = [slice(at, at + chunk) for at in range(0, b_ref.shape[0], chunk)]
    for rows in chunks:
        u = dot(b_ref[rows, :], up) + ub
        da = dot(gm_ref[rows, :], dn)
        cdf, pdf = gelu_parts(u)
        du = da * (cdf + u * pdf)
        sums = sums + jnp.sum(du, axis=0, keepdims=True)
        act_s[rows, :] = (u * cdf).astype(bf16)
        du_s[rows, :] = du.astype(bf16)
    for rows in chunks:
        h_ref[rows, :] += dot(act_s[rows, :], dn, NT)
        db_ref[rows, :] += dot(du_s[rows, :], up, NT)
    gub_ref[...] = sums
    for i, (left, right) in enumerate(((b_ref, du_s), (gm_ref, act_s))):
        grad = dot(left[...], right[...], TN)
        if rows_up:
            store_halves(outs[3 + 2 * i], outs[4 + 2 * i], grad, rows_up)
        else:
            outs[3 + i][...] = grad.astype(bf16)


def feed(b, gm, up, dn, ub, rows_up, before=(), block=768, chunk=320):
    rows = b.shape[0]
    hidden = up.shape[1]
    rows_up = rows_up if rows_up % 16 == 0 else 0
    full = pl.BlockSpec((rows, D), lambda j: (0, 0), pipeline_mode=pl.Buffered(1))
    weight = pl.BlockSpec((D, block), lambda j: (0, j))
    bias = pl.BlockSpec((1, block), lambda j: (0, j))
    if rows_up:
        grad = pl.BlockSpec((2, D // 4, block), lambda j: (0, 0, j))
        shapes = [jax.ShapeDtypeStruct((2, D // 4, hidden), bf16)] * 4
    else:
        grad = pl.BlockSpec((D, block), lambda j: (0, j))
        shapes = [jax.ShapeDtypeStruct((D, hidden), bf16)] * 2
    return pl.pallas_call(
        lambda *refs: feed_kernel(*refs, chunk=chunk, more=bool(before), rows_up=rows_up),
        grid=(hidden // block,),
        in_specs=[full, full, weight, weight, bias] + [full] * len(before),
        out_specs=[full, full, bias] + [grad] * len(shapes),
        out_shape=[jax.ShapeDtypeStruct((rows, D), f32)] * 2
        + [jax.ShapeDtypeStruct(ub.shape, f32)]
        + shapes,
        scratch_shapes=[pltpu.VMEM((rows, block), bf16)] * 2,
        compiler_params=pltpu.CompilerParams(
            dimension_semantics=("arbitrary",), vmem_limit_bytes=60 << 20
        ),
        cost_estimate=cost(
            flops=12 * rows * hidden * D,
            bytes_accessed=rows * D * 12 + hidden * D * 8,
            transcendentals=2 * rows * hidden,
        ),
        name="feed",
    )(b, gm, up, dn, ub, *before)


def pair_major(columns):
    lead = columns.shape[:-1]
    return columns.reshape(lead + (3, PAIRS, 128)).swapaxes(-3, -2).reshape(lead + (3 * D,))


def pair_minor(columns):
    lead = columns.shape[:-1]
    return columns.reshape(lead + (PAIRS, 3, 128)).swapaxes(-3, -2).reshape(lead + (3 * D,))


class Place:
    def __init__(self):
        dp, self.nx = lax.axis_size("dp"), lax.axis_size("mlp")
        self.ny, self.nc = 2, 2
        self.nz = dp // (self.ny * self.nc)
        index = lax.axis_index("dp")
        self.x = lax.axis_index("mlp")
        self.c = index % self.nc
        self.y = (index // self.nc) % self.ny
        self.z = index // (self.nc * self.ny)

    label = "hop"

    def send(self, value, move):
        pairs = []
        for z in range(self.nz):
            for y in range(self.ny):
                for c in range(self.nc):
                    for x in range(self.nx):
                        source = ((z * self.ny + y) * self.nc + c) * self.nx + x
                        z2, y2, c2, x2 = move(z, y, c, x)
                        pairs.append((source, ((z2 * self.ny + y2) * self.nc + c2) * self.nx + x2))
        with jax.named_scope(self.label):
            return lax.ppermute(value, ("dp", "mlp"), pairs)

    def shift(self, value, dz=0, dy=0, dc=0, dx=0):
        return self.send(
            value,
            lambda z, y, c, x: (
                (z + dz) % self.nz,
                (y + dy) % self.ny,
                (c + dc) % self.nc,
                (x + dx) % self.nx,
            ),
        )


def spread_z(place, shard):
    return {k: place.shift(shard, dz=k) if k else shard for k in range(place.nz)}


def line_up(place, pieces):
    ids = jnp.arange(place.nz).reshape((place.nz,) + (1,) * pieces[0].ndim)
    whole = jnp.broadcast_to(pieces[0][None], (place.nz,) + pieces[0].shape)
    for k in range(1, place.nz):
        whole = jnp.where(ids == (place.z - k) % place.nz, pieces[k][None], whole)
    return whole


def spread_plane(place, line):
    over_x = place.shift(line, dx=1)
    over_y = place.shift(line, dy=1)
    return {(0, 0): line, (1, 0): over_x, (0, 1): over_y, (1, 1): place.shift(over_y, dx=1)}


def spread_plane_halves(place, line):
    half = line.shape[-1] // 2
    over_x = place.shift(line, dx=1)
    over_y = place.shift(line, dy=1)
    return {
        (0, 0, 0): line,
        (1, 0, 0): over_x,
        (0, 1, 0): over_y,
        (1, 1, 0): place.shift(over_x[..., :half], dy=1),
        (1, 1, half): place.shift(over_y[..., half:], dx=1),
    }


def spread_cores(place, pieces):
    whole = {key[:-1] + (0,) + key[-1:]: piece for key, piece in pieces.items()}
    for key, piece in pieces.items():
        whole[key[:-1] + (1,) + key[-1:]] = place.shift(piece, dc=1)
    return whole


def assemble_kernel(*refs, keys, plan, nx):
    sources, targets = refs[: len(keys)], refs[len(keys) :]
    index = lax.axis_index("dp")
    here = {"x": lax.axis_index("mlp"), "c": index % 2, "y": (index // 2) % 2}
    many = {"x": nx, "c": 2, "y": 2}
    for source, (key, low) in zip(sources, keys):
        spot = {axis: lax.rem(here[axis] + many[axis] - key[axis], many[axis]) for axis in key}
        spot["z"] = slice(None)
        high = low + source.shape[-1]
        for target, (order, picks, first, columns) in zip(targets, plan):
            left, right = max(low, first), min(high, first + columns)
            if left >= right:
                continue
            take = (slice(None),) + picks + (slice(None), slice(left - low, right - low))
            place = tuple(spot[axis] for axis in order)
            target[place + (slice(None), slice(left - first, right - first))] = source[take]


def assemble(place, pieces, names, plan):
    keys = [(dict(zip(names, key[:-1])), key[-1]) for key in pieces]
    arrays = list(pieces.values())
    many = {"x": place.nx, "y": place.ny, "c": place.nc, "z": place.nz}
    rows = arrays[0].shape[-2]
    shapes = [tuple(many[axis] for axis in order) + (rows, columns) for order, _, _, columns in plan]
    size = sum(math.prod(shape) for shape in shapes)
    out = pl.pallas_call(
        lambda *refs: assemble_kernel(*refs, keys=keys, plan=plan, nx=place.nx),
        in_specs=[pl.BlockSpec(memory_space=pltpu.VMEM)] * len(arrays),
        out_specs=[pl.BlockSpec(memory_space=pltpu.VMEM)] * len(plan),
        out_shape=[jax.ShapeDtypeStruct(shape, bf16) for shape in shapes],
        compiler_params=pltpu.CompilerParams(vmem_limit_bytes=40 << 20),
        cost_estimate=cost(flops=0, bytes_accessed=4 * size, transcendentals=0),
        name="assemble",
    )(*arrays)
    return [item.reshape(-1, item.shape[-1]) for item in out]


def after(value, *others):
    return lax.optimization_barrier((value,) + others)[0]


def cover(values, scatters=(), arrays=()):
    moved = [[scatter.terms[i] for i in scatter.fresh] for scatter in scatters]
    values, moved, arrays = lax.optimization_barrier((list(values), moved, list(arrays)))
    for scatter, new in zip(scatters, moved):
        for i, term in zip(scatter.fresh, new):
            scatter.terms[i] = term
    return list(values) + list(arrays)


class Scatter:
    def __init__(self, place, terms, axes):
        self.place, self.terms, self.axes = place, list(terms), axes

    def take(self, axis, index):
        at = self.axes.index(axis)
        return [lax.dynamic_index_in_dim(term, index, at, keepdims=False) for term in self.terms]

    def hop(self, axis):
        place = self.place
        here, many = getattr(place, axis), getattr(place, "n" + axis)
        moved = []
        for k in range(1, many):
            theirs = add_up(self.take(axis, (here + k) % many)).astype(bf16)
            moved.append(place.shift(theirs, **{"d" + axis: k}))
        terms = self.take(axis, here)
        self.fresh = range(len(terms), len(terms) + len(moved))
        self.terms = terms + moved
        self.axes = self.axes.replace(axis, "")
        return self

    def hop_plane(self):
        place = self.place
        moved = []
        for dx, dy in ((1, 0), (0, 1), (1, 1)):
            part = Scatter(place, self.terms, self.axes)
            part.terms, part.axes = part.take("x", (place.x + dx) % place.nx), part.axes.replace("x", "")
            theirs = add_up(part.take("y", (place.y + dy) % place.ny)).astype(bf16)
            moved.append(place.shift(theirs, dx=dx, dy=dy))
        for axis in "xy":
            self.terms = self.take(axis, getattr(place, axis))
            self.axes = self.axes.replace(axis, "")
        self.fresh = range(len(self.terms), len(self.terms) + 3)
        self.terms = self.terms + moved
        return self

    def add(self, theirs, **move):
        self.fresh = range(len(self.terms), len(self.terms) + 1)
        self.terms = self.terms + [self.place.shift(theirs, **move)]
        return self

    def join(self, other):
        return self.add(add_up(other.terms).astype(bf16), dx=1)

    @property
    def total(self):
        return add_up(self.terms)


def add_up(terms):
    return sum(term.astype(f32) for term in terms)


def per_device(
    tokens,
    cotangent,
    lengths,
    buckets,
    pos_table,
    prompts,
    norm1_gain,
    norm1_bias,
    qkv_weight,
    q_bias,
    v_bias,
    out_weight,
    out_bias,
    norm2_gain,
    norm2_bias,
    up_weight,
    up_bias,
    down_weight,
    down_bias,
):
    mlp_size = lax.axis_size("mlp")
    micro_count, local_rows = tokens.shape[:2]
    rows = micro_count * local_rows
    hidden_local = up_weight.shape[1]
    hidden = hidden_local * mlp_size

    place = Place()
    rows_up = up_weight.shape[0]
    qkv_shard = pair_major(qkv_weight)
    cut = FIRST * GROUP
    pieces = spread_z(place, jnp.concatenate([qkv_shard, out_weight], axis=1))
    buffer_lengths, buffer_buckets = lengths.reshape(-1, SLOTS), buckets.reshape(-1)
    table = jnp.pad(
        jnp.concatenate([pos_table, prompts, norm1_gain[None], norm1_bias[None]], axis=0),
        ((0, 1024 - TABLE - PROMPTS - 2), (0, 0)),
    )
    vectors = jnp.stack(
        [norm1_gain, norm1_bias, out_bias, norm2_gain, norm2_bias, down_bias, q_bias, v_bias]
    ).astype(f32)
    qkv_offset = pair_major(
        jnp.concatenate([vectors[6:7], jnp.zeros((1, D), f32), vectors[7:8]], axis=1)
    )
    start_rows, normed, grad_branch, fq, fk, grad_down_shift = embed(
        buffer_lengths, buffer_buckets, tokens.reshape(rows, D), cotangent.reshape(rows, D), table
    )
    feed_pack = jnp.stack([up_weight, down_weight.T])
    shift_other = place.shift(up_bias, dx=1)
    pieces, feed_pack, shift_other, normed = lax.optimization_barrier(
        (pieces, feed_pack, shift_other, normed)
    )
    plane = spread_plane_halves(place, line_up(place, pieces))
    qkv_one, qkv_two, out_full = assemble(
        place,
        spread_cores(place, plane),
        "xyc",
        [("zycx", (), 0, cut), ("zycx", (), cut, 3 * D - cut), ("zycx", (), 3 * D, D)],
    )

    feed_line = line_up(place, spread_z(place, feed_pack))
    over_x = place.shift(feed_line, dx=1)

    def feed_weights(pieces):
        plan = [("zyc", (which,), 0, hidden_local) for which in range(2)]
        return assemble(place, pieces, "yc", plan)

    shift_own = up_bias.astype(f32)[None, :]
    shift_other = shift_other.astype(f32)[None, :]

    normed = after(normed, feed_line)
    qkv_one_rows = (dot(normed, qkv_one) + qkv_offset[:, :cut]).astype(bf16)
    attended_one, log_one = attend(qkv_one_rows, fq, fk)
    qkv_two_rows = (dot(after(normed, attended_one), qkv_two) + qkv_offset[:, cut:]).astype(bf16)
    over_y = place.shift(feed_line, dy=1)
    attended_two, log_two, over_x, over_y = cover(
        attend(qkv_two_rows, fq, fk), arrays=[over_x, over_y]
    )
    own_pieces = spread_cores(place, {(0, 0): feed_line, (1, 0): over_y})
    first_sum, normed_two = middle(attended_one, attended_two, out_full, start_rows, vectors)

    def parts(value, order):
        many = {"x": place.nx, "y": place.ny, "c": place.nc, "z": place.nz}
        return value.reshape(tuple(many[axis] for axis in order) + (-1, value.shape[-1]))

    def feed_scatter(grads):
        made = []
        for which in range(2):
            if len(grads) == 4:
                mine, theirs = (
                    item.reshape(2, place.nz, -1, hidden_local) for item in grads[2 * which : 2 * which + 2]
                )
                made.append(Scatter(place, [mine], "yz").add(theirs, dc=1))
            else:
                made.append(Scatter(place, [parts(grads[which], "zyc")], "zyc").hop("c"))
        return made

    up_own, down_own = feed_weights(own_pieces)
    *results, over_both = cover(
        feed(normed_two, grad_branch, up_own, down_own, shift_own, rows_up),
        arrays=[place.shift(over_y, dx=1)],
    )
    sum_h, sum_db, shift_grad_own, *grads = results
    own_up, own_down = feed_scatter(grads)
    up_other, down_other = feed_weights(spread_cores(place, {(0, 0): over_x, (1, 0): over_both}))
    normed_two, _ = cover([normed_two], [own_up, own_down], [up_other])
    branch, grad_normed, shift_grad_other, *grads = cover(
        feed(normed_two, grad_branch, up_other, down_other, shift_other, rows_up, (sum_h, sum_db)),
        [own_up.hop("y")],
    )
    grad_up_shift = jnp.where(
        place.x == 0,
        jnp.concatenate([shift_grad_own, shift_grad_other], axis=1),
        jnp.concatenate([shift_grad_other, shift_grad_own], axis=1),
    )
    other_up, other_down = feed_scatter(grads)
    (first_sum,) = cover([first_sum], [other_up, other_down])
    output, grad_one, grad_attended, grad_out, early = middle_back(
        buffer_lengths, buffer_buckets, first_sum, branch, grad_normed, grad_branch,
        attended_one, attended_two, out_full, vectors, grad_down_shift, grad_up_shift,
    )
    half = (PAIRS - FIRST) // 2
    back_two, sums_two = cover(
        attend_back(qkv_two_rows, grad_attended, attended_two, fq, fk, log_two, FIRST, (0, half)),
        [other_up.hop("y"), own_down.join(other_down)],
    )
    grad_attended = after(grad_attended, back_two)
    back_three, sums_three = cover(
        attend_back(
            qkv_two_rows, grad_attended, attended_two, fq, fk, log_two, FIRST, (half, PAIRS - FIRST)
        ),
        [own_up.join(other_up), own_down.hop("y")],
    )
    wide = jnp.concatenate(
        [dot(normed, back_two, TN).astype(bf16), dot(normed, back_three, TN).astype(bf16), grad_out], axis=1
    )
    grad_attended = after(grad_attended, wide)
    send_own = Scatter(place, [jnp.stack([own_up.total, own_down.total])], "uz").hop("z")
    send_two = Scatter(place, [parts(wide, "zycx")], "zycx").hop("c")
    back_one, sums_one = cover(
        attend_back(qkv_one_rows, grad_attended, attended_one, fq, fk, log_one, 0, (0, FIRST)),
        [send_two],
    )
    send_two.hop("x")
    grad_qkv_one = dot(normed, back_one, TN).astype(bf16)
    send_one = Scatter(place, [parts(grad_qkv_one, "zycx")], "zycx").hop("c")
    input_grad, packed = cover(
        finish(
            buffer_lengths, buffer_buckets, start_rows, grad_one, vectors, early,
            [after(back_one, grad_qkv_one), back_two, back_three], [sums_one, sums_two, sums_three],
            [qkv_one, qkv_two], [(0, 0), (1, 0), (1, half * GROUP)],
        ),
        [send_own, send_two, send_one],
    )

    packed = packed.reshape(place.nc, PACK // place.nc, D)
    own = lax.dynamic_index_in_dim(packed, place.c, 0, keepdims=False)
    other = lax.dynamic_index_in_dim(packed, 1 - place.c, 0, keepdims=False)
    send_two.hop("y")
    send_one.hop("x")
    own = own + place.shift(other, dc=1)
    near = {(0, 0): own, (1, 0): place.shift(own, dx=1), (0, 1): place.shift(own, dy=1)}
    near[1, 1] = place.shift(own, dx=1, dy=1)
    own = 0.0
    for x in range(2):
        for y in range(2):
            line = [jnp.where(place.x == x, near[0, dy], near[1, dy]) for dy in range(2)]
            own = own + jnp.where(place.y == y, line[0], line[1])
    send_one.hop("y")
    send_two.terms = [jnp.concatenate([send_one.total, send_two.total], axis=-1)]
    send_two.hop("z")
    bit = 1
    while bit < place.nz:
        own = own + place.send(own, lambda z, y, c, x, bit=bit: (z ^ bit, y, c, x))
        bit *= 2
    other = place.shift(own, dc=1)
    summed = jnp.where(
        place.c == 0, jnp.concatenate([own, other], 0), jnp.concatenate([other, own], 0)
    )
    qkv_weight_grad = pair_minor(add_up([term[:, : 3 * D] for term in send_two.terms]))
    out_weight_grad = add_up([term[:, 3 * D :] for term in send_two.terms])
    up_weight_grad = send_own.total[0]
    down_weight_grad = send_own.total[1].T
    singles = [summed[PROMPTS + i] for i in range(8)]
    up_bias_grad = lax.dynamic_slice_in_dim(
        summed[PROMPTS + 8 : PROMPTS + 12].reshape(hidden), lax.axis_index("mlp") * hidden_local, hidden_local, 0
    )
    return (
        output.reshape(tokens.shape),
        input_grad.reshape(tokens.shape),
        summed[:PROMPTS],
        singles[0],
        singles[1],
        qkv_weight_grad,
        singles[2],
        singles[3],
        out_weight_grad,
        singles[4],
        singles[5],
        singles[6],
        up_weight_grad,
        up_bias_grad,
        down_weight_grad,
        singles[7],
    )


def solution(mesh):
    both = ("dp", "mlp")
    in_specs = (
        P(None, both, None),
        P(None, both, None),
        P(None, both, None),
        P(None, both),
        P(),
        P(),
        P(),
        P(),
        P(both, None),
        P(),
        P(),
        P(both, None),
        P(),
        P(),
        P(),
        P("dp", "mlp"),
        P("mlp"),
        P("mlp", "dp"),
        P(),
    )
    out_specs = (
        P(None, both, None),
        P(None, both, None),
        P(),
        P(),
        P(),
        P(both, None),
        P(),
        P(),
        P(both, None),
        P(),
        P(),
        P(),
        P("dp", "mlp"),
        P("mlp"),
        P("mlp", "dp"),
        P(),
    )
    return jax.shard_map(
        per_device, mesh=mesh, in_specs=in_specs, out_specs=out_specs, check_vma=False
    )
```

```python
import math

import jax
import jax.numpy as jnp
from jax import lax
from jax.experimental import pallas as pl
from jax.experimental.pallas import tpu as pltpu
from jax.sharding import PartitionSpec as P

D = 768
HEADS = 12
HEAD_DIM = 64
PAIRS = 6
PROMPTS = 50
LEN_LOW = 101
LEN_MID = 197
TABLE = 875
SLOTS = 4
ROWS = 640
GROUP = 3 * 128
PACK = 64
BLOCK = 320
weigh = 5
FIRST = 2
GAIN_ONE, SHIFT_ONE, OUT_BIAS, GAIN_TWO, SHIFT_TWO, DOWN_BIAS = (slice(i, i + 1) for i in range(6))

epsilon = 1e-06
bf16 = jnp.bfloat16
f32 = jnp.float32
log2_e = 1.4426950408889634
score_scale = log2_e / math.sqrt(HEAD_DIM)
erf_p = 0.3275911
erf_a = (0.254829592, -0.284496736, 1.421413741, -1.453152027, 1.061405429)

NT = (((1,), (1,)), ((), ()))
NN = (((1,), (0,)), ((), ()))
TN = (((0,), (0,)), ((), ()))


def cost(flops, bytes_accessed, transcendentals):
    return pl.CostEstimate(
        flops=weigh * flops, bytes_accessed=weigh * bytes_accessed, transcendentals=weigh * transcendentals
    )


def dot(left, right, dims=NN):
    return lax.dot_general(left, right, dims, preferred_element_type=f32)


def row_plan(lengths_ref, buckets_ref, buffer, rows):
    sequence = jnp.zeros_like(rows)
    start = jnp.zeros_like(rows)
    end = 0
    for slot in range(SLOTS):
        length = lengths_ref[buffer, slot]
        end = end + jnp.where(length > 0, length + PROMPTS, 0)
        sequence = sequence + jnp.where(end <= rows, 1, 0)
        start = jnp.where(end <= rows, end, start)
    position = rows - start
    bucket = buckets_ref[buffer]
    table = jnp.where(bucket == 0, 0, jnp.where(bucket == 1, LEN_LOW, LEN_LOW + LEN_MID))
    inside = sequence < SLOTS
    prompt = inside & (position < PROMPTS)
    image = inside & (position >= PROMPTS)
    index = jnp.where(
        prompt,
        TABLE + position,
        jnp.where(image, jnp.clip(table + position - PROMPTS, 0, TABLE - 1), -1),
    )
    return sequence, position, inside, prompt, image, index


def norm_stats(values_in):
    average = jnp.mean(values_in, axis=-1, keepdims=True)
    centred = values_in - average
    variance = jnp.mean(centred * centred, axis=-1, keepdims=True)
    inverse = lax.rsqrt(variance + epsilon)
    return centred * inverse, inverse


def norm_back(grad_normed, normal, inverse, gain):
    scaled = grad_normed * gain
    mean_one = jnp.mean(scaled, axis=-1, keepdims=True)
    mean_two = jnp.mean(scaled * normal, axis=-1, keepdims=True)
    return (scaled - mean_one - normal * mean_two) * inverse


def add_rows(ref, step, row, value):
    total = jnp.sum(value, axis=0, keepdims=True)

    @pl.when(step == 0)
    def _():
        ref[row : row + 1, :] = total

    @pl.when(step > 0)
    def _():
        ref[row : row + 1, :] += total


def add_product(ref, step, value):
    @pl.when(step == 0)
    def _():
        ref[...] = value

    @pl.when(step > 0)
    def _():
        ref[...] += value


def weight_shapes(columns, rows_in):
    wide = 2 * rows_in
    if wide % 16 == 0:
        return [jax.ShapeDtypeStruct((D // (2 * wide), wide, columns), bf16)] * 2
    return [jax.ShapeDtypeStruct((D, columns), bf16)]


def store_weight(refs, value, rows_in):
    if len(refs) == 1:
        refs[0][...] = value.astype(bf16)
        return
    grid = value.reshape(-1, 2, 2 * rows_in, value.shape[-1])
    first = lax.rem(lax.axis_index("dp"), 2) == 0
    refs[0][...] = jnp.where(first, grid[:, 0], grid[:, 1]).astype(bf16)
    refs[1][...] = jnp.where(first, grid[:, 1], grid[:, 0]).astype(bf16)


def block_rows(shape, axis):
    step = pl.program_id(0)
    per = ROWS // BLOCK
    ids = lax.broadcasted_iota(jnp.int32, shape, axis) + lax.rem(step, per) * BLOCK
    return lax.div(step, per), ids


def embed_kernel(
    lengths_ref, buckets_ref, tokens_ref, cot_ref, table_ref,
    h_ref, a_ref, gm_ref, fq_ref, fk_ref, sum_ref,
):
    buffer, ids = block_rows((BLOCK, 1), 0)
    lane = lax.broadcasted_iota(jnp.int32, (1, 128), 1)
    sequence, _, inside, _, image, index = row_plan(lengths_ref, buckets_ref, buffer, ids)
    places = lax.broadcasted_iota(jnp.int32, (1, table_ref.shape[0]), 1)
    hits = jnp.where(places == index, 1.0, 0.0).astype(bf16)
    start = dot(hits, table_ref[...]) + jnp.where(image, tokens_ref[...].astype(f32), 0.0)
    h_ref[...] = start
    normal, _ = norm_stats(start)
    last = TABLE + PROMPTS
    gain = table_ref[last : last + 1, :].astype(f32)
    shift = table_ref[last + 1 : last + 2, :].astype(f32)
    a_ref[...] = (normal * gain + shift).astype(bf16)
    grad = jnp.where(inside, cot_ref[...].astype(f32), 0.0)
    gm_ref[...] = grad.astype(bf16)
    same = lane == sequence
    fq_ref[...] = jnp.where(same, 1.0, 0.0).astype(bf16)
    ones = jnp.where((lane >= 8) & (lane < 11), 1.0, 0.0)
    fk_ref[...] = jnp.where((lane <= SLOTS) & ~same, -1e30, ones).astype(bf16)
    add_rows(sum_ref, pl.program_id(0), 0, grad)


def whole_spec(shape):
    return pl.BlockSpec(shape, lambda b: (0,) * len(shape), pipeline_mode=pl.Buffered(1))


def scalar_spec():
    return pl.BlockSpec(memory_space=pltpu.SMEM)


def buffer_spec(columns):
    return pl.BlockSpec((BLOCK, columns), lambda b: (b, 0))


def buffer_params(mib=28):
    return pltpu.CompilerParams(dimension_semantics=("arbitrary",), vmem_limit_bytes=mib << 20)


def embed(lengths, buckets, tokens, cotangent, table):
    rows = tokens.shape[0]
    kept = whole_spec((1, D))
    return pl.pallas_call(
        embed_kernel,
        grid=(rows // BLOCK,),
        in_specs=[
            scalar_spec(), scalar_spec(), buffer_spec(D), buffer_spec(D), whole_spec(table.shape),
        ],
        out_specs=[buffer_spec(D), buffer_spec(D), buffer_spec(D), buffer_spec(128), buffer_spec(128), kept],
        out_shape=[
            jax.ShapeDtypeStruct((rows, D), f32),
            jax.ShapeDtypeStruct((rows, D), bf16),
            jax.ShapeDtypeStruct((rows, D), bf16),
            jax.ShapeDtypeStruct((rows, 128), bf16),
            jax.ShapeDtypeStruct((rows, 128), bf16),
            jax.ShapeDtypeStruct((1, D), f32),
        ],
        compiler_params=buffer_params(56),
        cost_estimate=cost(
            flops=2 * rows * table.shape[0] * D, bytes_accessed=rows * D * 12, transcendentals=0
        ),
        name="embed",
    )(lengths, buckets, tokens, cotangent, table)


def middle_kernel(o_ref, w_ref, h_ref, vec_ref, h1_ref, b_ref):
    total = h_ref[...] + dot(o_ref[...], w_ref[...]) + vec_ref[OUT_BIAS]
    h1_ref[...] = total
    normal, _ = norm_stats(total)
    b_ref[...] = (normal * vec_ref[GAIN_TWO] + vec_ref[SHIFT_TWO]).astype(bf16)


def middle(o, weight, start, vectors):
    rows = start.shape[0]
    return pl.pallas_call(
        middle_kernel,
        grid=(rows // BLOCK,),
        in_specs=[
            buffer_spec(D), whole_spec((D, D)), buffer_spec(D), whole_spec((8, D)),
        ],
        out_specs=[buffer_spec(D), buffer_spec(D)],
        out_shape=[jax.ShapeDtypeStruct((rows, D), f32), jax.ShapeDtypeStruct((rows, D), bf16)],
        compiler_params=buffer_params(),
        cost_estimate=cost(
            flops=2 * rows * D * D, bytes_accessed=rows * D * 12, transcendentals=0
        ),
        name="middle",
    )(o, weight, start, vectors)


def middle_back_kernel(
    lengths_ref, buckets_ref, h1_ref, branch_ref, db_ref, gm_ref, o_ref, w_ref, vec_ref,
    gdown_ref, gup_ref, out_ref, g1_ref, do_ref, early_ref, *gw_refs, rows_in,
):
    *gw_refs, gw_s = gw_refs
    step = pl.program_id(0)
    buffer, ids = block_rows((BLOCK, 1), 0)
    _, _, inside, _, _, _ = row_plan(lengths_ref, buckets_ref, buffer, ids)
    h1 = h1_ref[...]
    out_ref[...] = jnp.where(inside, h1 + branch_ref[...].astype(f32) + vec_ref[DOWN_BIAS], 0.0).astype(bf16)
    normal, inverse = norm_stats(h1)
    db = db_ref[...].astype(f32)
    g1 = gm_ref[...].astype(f32) + norm_back(db, normal, inverse, vec_ref[GAIN_TWO])
    g1_ref[...] = g1
    ga = g1.astype(bf16)
    do_ref[...] = dot(ga, w_ref[...], NT).astype(bf16)
    for row, value in ((0, g1), (1, db * normal), (2, db)):
        add_rows(early_ref, step, row, value)
    add_product(gw_s, step, dot(o_ref[...], ga, TN))

    @pl.when(step == pl.num_programs(0) - 1)
    def _():
        store_weight(gw_refs, gw_s[...], rows_in)
        early_ref[3:4, :] = gdown_ref[...]
        for i in range(gup_ref.shape[1] // D):
            early_ref[4 + i : 5 + i, :] = gup_ref[:, i * D : (i + 1) * D]


def middle_back(
    lengths, buckets, h1, branch, db, gm, o, weight, vectors, grad_down, grad_up, rows_in
):
    rows = h1.shape[0]
    wide = buffer_spec(D)
    grads = weight_shapes(D, rows_in)
    return pl.pallas_call(
        lambda *refs: middle_back_kernel(*refs, rows_in=rows_in),
        grid=(rows // BLOCK,),
        in_specs=[
            scalar_spec(), scalar_spec(), wide, wide, wide, wide, wide, whole_spec((D, D)),
            whole_spec((8, D)), whole_spec((1, D)), whole_spec(grad_up.shape),
        ],
        out_specs=[wide, wide, wide, whole_spec((8, D))] + [whole_spec(item.shape) for item in grads],
        out_shape=[
            jax.ShapeDtypeStruct((rows, D), bf16),
            jax.ShapeDtypeStruct((rows, D), f32),
            jax.ShapeDtypeStruct((rows, D), bf16),
            jax.ShapeDtypeStruct((8, D), f32),
        ]
        + grads,
        scratch_shapes=[pltpu.VMEM((D, D), f32)],
        compiler_params=buffer_params(56),
        cost_estimate=cost(
            flops=4 * rows * D * D, bytes_accessed=rows * D * 26, transcendentals=0
        ),
        name="middle_back",
    )(lengths, buckets, h1, branch, db, gm, o, weight, vectors, grad_down, grad_up)


def finish_kernel(*refs, plan):
    lengths_ref, buckets_ref, h_ref, g1_ref, vec_ref, early_ref = refs[:6]
    grads, sums_in, weights = refs[6 : 6 + len(plan)], refs[6 + len(plan) : 6 + 2 * len(plan)], refs[6 + 2 * len(plan) : -2]
    input_ref, pack_ref = refs[-2:]
    step = pl.program_id(0)
    count = pack_ref.shape[0]
    buffer, ids = block_rows((BLOCK, 1), 0)
    _, _, _, _, image, _ = row_plan(lengths_ref, buckets_ref, buffer, ids)
    da = 0.0
    for grad, (which, at) in zip(grads, plan):
        da = da + dot(grad[...], weights[which][:, at : at + grad.shape[1]], NT)
    normal, inverse = norm_stats(h_ref[...])
    g0 = g1_ref[...] + norm_back(da, normal, inverse, vec_ref[GAIN_ONE])
    input_ref[...] = jnp.where(image, g0, 0.0)
    _, across = block_rows((1, BLOCK), 1)
    _, position, _, prompt, _, _ = row_plan(lengths_ref, buckets_ref, buffer, across)
    wanted = lax.broadcasted_iota(jnp.int32, (count, 1), 0)
    hits = jnp.where(prompt & (wanted == position), 1.0, 0.0).astype(bf16)
    sums = sum(dot(hits, part) for part in split_three(g0)[:2])
    lines = [jnp.sum(da * normal, axis=0, keepdims=True), jnp.sum(da, axis=0, keepdims=True)]
    for row, line in enumerate(lines):
        sums = jnp.where(wanted == PROMPTS + row, line, sums)

    @pl.when(step == 0)
    def _():
        pack_ref[...] = sums

    @pl.when(step > 0)
    def _():
        pack_ref[...] += sums

    @pl.when(step == pl.num_programs(0) - 1)
    def _():
        at = 0
        for ref in sums_in:
            for pair in range(ref.shape[1] // GROUP):
                to = slice(at, at + 128)
                at += 128
                for row, part in ((PROMPTS + 2, 0), (PROMPTS + 3, 2)):
                    lanes = slice(pair * GROUP + part * 128, pair * GROUP + part * 128 + 128)
                    pack_ref[row : row + 1, to] = ref[0:1, lanes]
        pack_ref[PROMPTS + 4 : PROMPTS + 12, :] = early_ref[...]


def finish(lengths, buckets, start, g1, vectors, early, grads, sums, weights, plan):
    rows = start.shape[0]
    wide = buffer_spec(D)
    return pl.pallas_call(
        lambda *refs: finish_kernel(*refs, plan=plan),
        grid=(rows // BLOCK,),
        in_specs=[scalar_spec(), scalar_spec(), wide, wide, whole_spec((8, D)), whole_spec((8, D))]
        + [buffer_spec(item.shape[1]) for item in grads]
        + [whole_spec(item.shape) for item in sums]
        + [whole_spec(item.shape) for item in weights],
        out_specs=[wide, whole_spec((PACK, D))],
        out_shape=[jax.ShapeDtypeStruct((rows, D), f32), jax.ShapeDtypeStruct((PACK, D), f32)],
        compiler_params=buffer_params(),
        cost_estimate=cost(
            flops=6 * rows * D * D, bytes_accessed=rows * D * 18, transcendentals=0
        ),
        name="finish",
    )(lengths, buckets, start, g1, vectors, early, *grads, *sums, *weights)


def attend_kernel(qkv_ref, fq_ref, fk_ref, o_ref, lse_ref, *, chunk):
    pair = pl.program_id(1)
    lane = lax.broadcasted_iota(jnp.int32, (1, 128), 1)
    keys = jnp.concatenate([qkv_ref[:, 128:256], fk_ref[...]], axis=1)
    values = jnp.concatenate([qkv_ref[:, 256:384], jnp.ones((ROWS, 128), bf16)], axis=1)
    for step in range(ROWS // chunk):
        rows = slice(step * chunk, (step + 1) * chunk)
        queries = qkv_ref[rows, 0:128]
        marks = fq_ref[rows, :]
        outs = []
        lse = lse_ref[rows, :]
        for half in range(2):
            keep = (lane < 64) if half == 0 else (lane >= 64)
            own = jnp.concatenate([jnp.where(keep, queries, jnp.zeros_like(queries)), marks], axis=1)
            scores = dot(own, keys, NT)
            top = jnp.max(scores, axis=1, keepdims=True)
            weights = jnp.exp2((scores - top) * score_scale)
            mixed = dot(weights.astype(bf16), values)
            total = mixed[:, 128:129]
            outs.append(mixed[:, :128] / total)
            log_total = top + jnp.log2(total) * (1.0 / score_scale)
            lse = jnp.where(lane == pair * 2 + half, log_total, lse)
        o_ref[rows, :] = jnp.where(lane < 64, outs[0], outs[1]).astype(bf16)
        lse_ref[rows, :] = lse


def attend(qkv, fq, fk, chunk=320):
    rows = qkv.shape[0]
    mark = pl.BlockSpec((ROWS, 128), lambda b, p: (b, 0))
    return pl.pallas_call(
        lambda *refs: attend_kernel(*refs, chunk=chunk),
        grid=(rows // ROWS, qkv.shape[1] // GROUP),
        in_specs=[pl.BlockSpec((ROWS, GROUP), lambda b, p: (b, p)), mark, mark],
        out_specs=[pl.BlockSpec((ROWS, 128), lambda b, p: (b, p)), mark],
        out_shape=[
            jax.ShapeDtypeStruct((rows, qkv.shape[1] // 3), bf16),
            jax.ShapeDtypeStruct((rows, 128), f32),
        ],
        compiler_params=pltpu.CompilerParams(
            dimension_semantics=("arbitrary", "arbitrary"), vmem_limit_bytes=24 << 20
        ),
        cost_estimate=cost(
            flops=5 * rows * ROWS * qkv.shape[1],
            bytes_accessed=rows * qkv.shape[1] * 3,
            transcendentals=rows * ROWS * qkv.shape[1] // 192,
        ),
        name="attend",
    )(qkv, fq, fk)


def split_three(value):
    first = value.astype(bf16)
    rest = value - first.astype(f32)
    second = rest.astype(bf16)
    third = (rest - second.astype(f32)).astype(bf16)
    return first, second, third


def attend_back_kernel(
    qkv_ref, do_ref, o_ref, fq_ref, fk_ref, lse_ref, dqkv_ref, sum_ref, ds_ref, *, chunk, low
):
    pair, buffer = low + pl.program_id(0), pl.program_id(1)
    lane = lax.broadcasted_iota(jnp.int32, (1, 128), 1)
    queries = qkv_ref[:, 0:128]
    grads = do_ref[...]
    marks = fq_ref[...]
    product = grads.astype(f32) * o_ref[...].astype(f32)
    lse = lse_ref[...]
    zero = jnp.zeros_like(queries)
    own_q, own_g, wide_q, wide_g = [], [], [], []
    for half in range(2):
        keep = (lane < 64) if half == 0 else (lane >= 64)
        shift = -jnp.sum(jnp.where(lane == pair * 2 + half, lse, 0.0), axis=1, keepdims=True)
        inner = -jnp.sum(jnp.where(keep, product, 0.0), axis=1, keepdims=True)
        s0, s1, s2 = split_three(shift)
        i0, i1, i2 = split_three(inner)
        mark_q = jnp.where(lane == 8, s0, jnp.where(lane == 9, s1, jnp.where(lane == 10, s2, marks)))
        mark_g = jnp.where(lane == 8, i0, jnp.where(lane == 9, i1, jnp.where(lane == 10, i2, zero)))
        q_half = jnp.where(keep, queries, zero)
        g_half = jnp.where(keep, grads, zero)
        own_q.append(q_half)
        own_g.append(g_half)
        wide_q.append(jnp.concatenate([q_half, mark_q], axis=1))
        wide_g.append(jnp.concatenate([g_half, mark_g], axis=1))
    for step in range(ROWS // chunk):
        rows = slice(step * chunk, (step + 1) * chunk)
        keys = jnp.concatenate([qkv_ref[rows, 128:256], fk_ref[rows, :]], axis=1)
        values = jnp.concatenate([qkv_ref[rows, 256:384], fk_ref[rows, :]], axis=1)
        dv = jnp.zeros((chunk, 128), f32)
        dk = jnp.zeros((chunk, 128), f32)
        for half in range(2):
            weights = jnp.exp2(dot(keys, wide_q[half], NT) * score_scale)
            ds = (weights * dot(values, wide_g[half], NT)).astype(bf16)
            ds_ref[half, rows, :] = ds
            dv = dv + dot(weights.astype(bf16), own_g[half])
            dk = dk + dot(ds, own_q[half])
        dqkv_ref[rows, 256:384] = dv.astype(bf16)
        dqkv_ref[rows, 128:256] = (dk * 0.125).astype(bf16)
        line = jnp.sum(dv, axis=0, keepdims=True)
        dv_sum = dv_sum + line if step else line
    keys_t = qkv_ref[:, 128:256].T
    parts = [dot(keys_t, ds_ref[half]).T for half in range(2)]
    dq = jnp.where(lane < 64, parts[0], parts[1]) * 0.125
    dqkv_ref[:, 0:128] = dq.astype(bf16)
    dq_sum = jnp.sum(dq, axis=0, keepdims=True)

    @pl.when(buffer == 0)
    def _():
        sum_ref[0:1, 0:128] = dq_sum
        sum_ref[0:1, 256:384] = dv_sum

    @pl.when(buffer > 0)
    def _():
        sum_ref[0:1, 0:128] += dq_sum
        sum_ref[0:1, 256:384] += dv_sum


def attend_back(qkv, do, o, fq, fk, lse, pairs, chunk=640):
    rows = qkv.shape[0]
    low, count = pairs[0], pairs[1] - pairs[0]
    columns = count * GROUP
    mark = pl.BlockSpec((ROWS, 128), lambda p, b: (b, 0))
    part = pl.BlockSpec((ROWS, 128), lambda p, b: (b, low + p))
    return pl.pallas_call(
        lambda *refs: attend_back_kernel(*refs, chunk=chunk, low=low),
        grid=(count, rows // ROWS),
        in_specs=[
            pl.BlockSpec((ROWS, GROUP), lambda p, b: (b, low + p)), part, part, mark, mark, mark,
        ],
        out_specs=[
            pl.BlockSpec((ROWS, GROUP), lambda p, b: (b, p)),
            pl.BlockSpec((8, GROUP), lambda p, b: (0, p)),
        ],
        out_shape=[
            jax.ShapeDtypeStruct((rows, columns), bf16),
            jax.ShapeDtypeStruct((8, columns), f32),
        ],
        scratch_shapes=[pltpu.VMEM((2, ROWS, ROWS), bf16)],
        compiler_params=pltpu.CompilerParams(
            dimension_semantics=("arbitrary", "arbitrary"), vmem_limit_bytes=24 << 20
        ),
        cost_estimate=cost(
            flops=12 * rows * ROWS * columns,
            bytes_accessed=rows * columns * 6,
            transcendentals=rows * ROWS * columns // 192,
        ),
        name="attend_back",
    )(qkv, do, o, fq, fk, lse)


def gelu_parts(u):
    z = jnp.abs(u) * 0.7071067811865476
    t = 1.0 / (1.0 + erf_p * z)
    e = jnp.exp2(u * u * (-0.5 * log2_e))
    series = t * (erf_a[0] + t * (erf_a[1] + t * (erf_a[2] + t * (erf_a[3] + t * erf_a[4]))))
    tail = 0.5 * series * e
    return jnp.where(u < 0, tail, 1.0 - tail), e * 0.3989422804014327


def store_halves(mine_ref, theirs_ref, value, rows):
    columns = value.shape[-1]
    grid = value.reshape(-1, 2, 2, rows, columns)
    first = lax.rem(lax.axis_index("dp"), 2) == 0
    for y in range(2):
        left, right = grid[:, y, 0].reshape(-1, columns), grid[:, y, 1].reshape(-1, columns)
        mine_ref[y] = jnp.where(first, left, right).astype(bf16)
        theirs_ref[y] = jnp.where(first, right, left).astype(bf16)


def feed_kernel(*refs, chunk, more, rows_up):
    b_ref, gm_ref, up_ref, dn_ref, ub_ref = refs[:5]
    outs = refs[5 + 2 * more : -2]
    h_ref, db_ref, gub_ref = outs[:3]
    act_s, du_s = refs[-2:]
    up, dn, ub = up_ref[...], dn_ref[...], ub_ref[...]

    @pl.when(pl.program_id(0) == 0)
    def _():
        h_ref[...] = refs[5][...] if more else jnp.zeros_like(h_ref)
        db_ref[...] = refs[6][...] if more else jnp.zeros_like(db_ref)

    sums = jnp.zeros((1, ub.shape[1]), f32)
    chunks = [slice(at, at + chunk) for at in range(0, b_ref.shape[0], chunk)]
    for rows in chunks:
        u = dot(b_ref[rows, :], up) + ub
        da = dot(gm_ref[rows, :], dn)
        cdf, pdf = gelu_parts(u)
        du = da * (cdf + u * pdf)
        sums = sums + jnp.sum(du, axis=0, keepdims=True)
        act_s[rows, :] = (u * cdf).astype(bf16)
        du_s[rows, :] = du.astype(bf16)
    for rows in chunks:
        h_ref[rows, :] += dot(act_s[rows, :], dn, NT)
        db_ref[rows, :] += dot(du_s[rows, :], up, NT)
    gub_ref[...] = sums
    for i, (left, right) in enumerate(((b_ref, du_s), (gm_ref, act_s))):
        grad = dot(left[...], right[...], TN)
        if rows_up:
            store_halves(outs[3 + 2 * i], outs[4 + 2 * i], grad, rows_up)
        else:
            outs[3 + i][...] = grad.astype(bf16)


def feed(b, gm, up, dn, ub, rows_up, before=(), block=768, chunk=320):
    rows = b.shape[0]
    hidden = up.shape[1]
    rows_up = rows_up if rows_up % 16 == 0 else 0
    full = pl.BlockSpec((rows, D), lambda j: (0, 0), pipeline_mode=pl.Buffered(1))
    weight = pl.BlockSpec((D, block), lambda j: (0, j))
    bias = pl.BlockSpec((1, block), lambda j: (0, j))
    if rows_up:
        grad = pl.BlockSpec((2, D // 4, block), lambda j: (0, 0, j))
        shapes = [jax.ShapeDtypeStruct((2, D // 4, hidden), bf16)] * 4
    else:
        grad = pl.BlockSpec((D, block), lambda j: (0, j))
        shapes = [jax.ShapeDtypeStruct((D, hidden), bf16)] * 2
    return pl.pallas_call(
        lambda *refs: feed_kernel(*refs, chunk=chunk, more=bool(before), rows_up=rows_up),
        grid=(hidden // block,),
        in_specs=[full, full, weight, weight, bias] + [full] * len(before),
        out_specs=[full, full, bias] + [grad] * len(shapes),
        out_shape=[jax.ShapeDtypeStruct((rows, D), f32)] * 2
        + [jax.ShapeDtypeStruct(ub.shape, f32)]
        + shapes,
        scratch_shapes=[pltpu.VMEM((rows, block), bf16)] * 2,
        compiler_params=pltpu.CompilerParams(
            dimension_semantics=("arbitrary",), vmem_limit_bytes=(46 if before else 38) << 20
        ),
        cost_estimate=cost(
            flops=12 * rows * hidden * D,
            bytes_accessed=rows * D * 12 + hidden * D * 8,
            transcendentals=2 * rows * hidden,
        ),
        name="feed",
    )(b, gm, up, dn, ub, *before)


def pair_major(columns):
    lead = columns.shape[:-1]
    return columns.reshape(lead + (3, PAIRS, 128)).swapaxes(-3, -2).reshape(lead + (3 * D,))


def pair_minor(columns):
    lead = columns.shape[:-1]
    return columns.reshape(lead + (PAIRS, 3, 128)).swapaxes(-3, -2).reshape(lead + (3 * D,))


class Place:
    def __init__(self):
        dp, self.nx = lax.axis_size("dp"), lax.axis_size("mlp")
        self.ny, self.nc = 2, 2
        self.nz = dp // (self.ny * self.nc)
        index = lax.axis_index("dp")
        self.x = lax.axis_index("mlp")
        self.c = index % self.nc
        self.y = (index // self.nc) % self.ny
        self.z = index // (self.nc * self.ny)

    label = "hop"

    def send(self, value, move):
        pairs = []
        for z in range(self.nz):
            for y in range(self.ny):
                for c in range(self.nc):
                    for x in range(self.nx):
                        source = ((z * self.ny + y) * self.nc + c) * self.nx + x
                        z2, y2, c2, x2 = move(z, y, c, x)
                        pairs.append((source, ((z2 * self.ny + y2) * self.nc + c2) * self.nx + x2))
        with jax.named_scope(self.label):
            return lax.ppermute(value, ("dp", "mlp"), pairs)

    def shift(self, value, dz=0, dy=0, dc=0, dx=0):
        return self.send(
            value,
            lambda z, y, c, x: (
                (z + dz) % self.nz,
                (y + dy) % self.ny,
                (c + dc) % self.nc,
                (x + dx) % self.nx,
            ),
        )


def spread_z(place, shard):
    return {k: place.shift(shard, dz=k) if k else shard for k in range(place.nz)}


def line_up(place, pieces):
    ids = jnp.arange(place.nz).reshape((place.nz,) + (1,) * pieces[0].ndim)
    whole = jnp.broadcast_to(pieces[0][None], (place.nz,) + pieces[0].shape)
    for k in range(1, place.nz):
        whole = jnp.where(ids == (place.z - k) % place.nz, pieces[k][None], whole)
    return whole


def spread_plane(place, line):
    over_x = place.shift(line, dx=1)
    over_y = place.shift(line, dy=1)
    return {(0, 0): line, (1, 0): over_x, (0, 1): over_y, (1, 1): place.shift(over_y, dx=1)}


def spread_plane_halves(place, line, other):
    half = line.shape[-1] // 2
    over_x = place.shift(line, dx=1)
    over_y = place.shift(line, dy=1)
    over_x, over_y, other = lax.optimization_barrier((over_x, over_y, other))
    pieces = {
        (0, 0, 0): line,
        (1, 0, 0): over_x,
        (0, 1, 0): over_y,
        (1, 1, 0): place.shift(over_x[..., :half], dy=1),
        (1, 1, half): place.shift(over_y[..., half:], dx=1),
    }
    return pieces, other


def spread_cores(place, pieces):
    whole = {key[:-1] + (0,) + key[-1:]: piece for key, piece in pieces.items()}
    for key, piece in pieces.items():
        whole[key[:-1] + (1,) + key[-1:]] = place.shift(piece, dc=1)
    return whole


def assemble_kernel(*refs, keys, plan, nx):
    sources, targets = refs[: len(keys)], refs[len(keys) :]
    index = lax.axis_index("dp")
    here = {"x": lax.axis_index("mlp"), "c": index % 2, "y": (index // 2) % 2}
    many = {"x": nx, "c": 2, "y": 2}
    for source, (key, low) in zip(sources, keys):
        spot = {axis: lax.rem(here[axis] + many[axis] - key[axis], many[axis]) for axis in key}
        spot["z"] = slice(None)
        high = low + source.shape[-1]
        for target, (order, picks, first, columns) in zip(targets, plan):
            left, right = max(low, first), min(high, first + columns)
            if left >= right:
                continue
            take = (slice(None),) + picks + (slice(None), slice(left - low, right - low))
            place = tuple(spot[axis] for axis in order)
            target[place + (slice(None), slice(left - first, right - first))] = source[take]


def assemble(place, pieces, names, plan):
    keys = [(dict(zip(names, key[:-1])), key[-1]) for key in pieces]
    arrays = list(pieces.values())
    many = {"x": place.nx, "y": place.ny, "c": place.nc, "z": place.nz}
    rows = arrays[0].shape[-2]
    shapes = [tuple(many[axis] for axis in order) + (rows, columns) for order, _, _, columns in plan]
    size = sum(math.prod(shape) for shape in shapes)
    out = pl.pallas_call(
        lambda *refs: assemble_kernel(*refs, keys=keys, plan=plan, nx=place.nx),
        in_specs=[pl.BlockSpec(memory_space=pltpu.VMEM)] * len(arrays),
        out_specs=[pl.BlockSpec(memory_space=pltpu.VMEM)] * len(plan),
        out_shape=[jax.ShapeDtypeStruct(shape, bf16) for shape in shapes],
        compiler_params=pltpu.CompilerParams(vmem_limit_bytes=4 << 20),
        cost_estimate=cost(flops=0, bytes_accessed=4 * size, transcendentals=0),
        name="assemble",
    )(*arrays)
    return [item.reshape(-1, item.shape[-1]) for item in out]


def after(value, *others):
    return lax.optimization_barrier((value,) + others)[0]


def cover(values, scatters=(), arrays=()):
    picked = []
    for item in scatters:
        scatter, picks = item if isinstance(item, tuple) else (item, range(len(item.fresh)))
        picked += [(scatter, scatter.fresh[i]) for i in picks]
    moved = [scatter.terms[i] for scatter, i in picked]
    values, moved, arrays = lax.optimization_barrier((list(values), moved, list(arrays)))
    for (scatter, i), term in zip(picked, moved):
        scatter.terms[i] = term
    return list(values) + list(arrays)


class Scatter:
    def __init__(self, place, terms, axes):
        self.place, self.terms, self.axes = place, list(terms), axes

    def take(self, axis, index):
        at = self.axes.index(axis)
        return [lax.dynamic_index_in_dim(term, index, at, keepdims=False) for term in self.terms]

    def hop(self, axis):
        place = self.place
        here, many = getattr(place, axis), getattr(place, "n" + axis)
        moved = []
        for k in range(1, many):
            theirs = add_up(self.take(axis, (here + k) % many)).astype(bf16)
            moved.append(place.shift(theirs, **{"d" + axis: k}))
        terms = self.take(axis, here)
        self.fresh = range(len(terms), len(terms) + len(moved))
        self.terms = terms + moved
        self.axes = self.axes.replace(axis, "")
        return self

    def hop_plane(self):
        place = self.place
        moved = []
        for dx, dy in ((1, 0), (0, 1), (1, 1)):
            part = Scatter(place, self.terms, self.axes)
            part.terms, part.axes = part.take("x", (place.x + dx) % place.nx), part.axes.replace("x", "")
            theirs = add_up(part.take("y", (place.y + dy) % place.ny)).astype(bf16)
            moved.append(place.shift(theirs, dx=dx, dy=dy))
        for axis in "xy":
            self.terms = self.take(axis, getattr(place, axis))
            self.axes = self.axes.replace(axis, "")
        self.fresh = range(len(self.terms), len(self.terms) + 3)
        self.terms = self.terms + moved
        return self

    def add(self, theirs, **move):
        self.fresh = range(len(self.terms), len(self.terms) + 1)
        self.terms = self.terms + [self.place.shift(theirs, **move)]
        return self

    def join(self, other):
        return self.add(add_up(other.terms).astype(bf16), dx=1)

    @property
    def total(self):
        return add_up(self.terms)


def add_up(terms):
    return sum(term.astype(f32) for term in terms)


def per_device(
    tokens,
    cotangent,
    lengths,
    buckets,
    pos_table,
    prompts,
    norm1_gain,
    norm1_bias,
    qkv_weight,
    q_bias,
    v_bias,
    out_weight,
    out_bias,
    norm2_gain,
    norm2_bias,
    up_weight,
    up_bias,
    down_weight,
    down_bias,
):
    mlp_size = lax.axis_size("mlp")
    micro_count, local_rows = tokens.shape[:2]
    rows = micro_count * local_rows
    hidden_local = up_weight.shape[1]
    hidden = hidden_local * mlp_size

    place = Place()
    rows_up = up_weight.shape[0]
    qkv_shard = pair_major(qkv_weight)
    rows_in = qkv_weight.shape[0]
    pieces = spread_z(place, jnp.concatenate([qkv_shard, out_weight], axis=1))
    buffer_lengths, buffer_buckets = lengths.reshape(-1, SLOTS), buckets.reshape(-1)
    table = jnp.pad(
        jnp.concatenate([pos_table, prompts, norm1_gain[None], norm1_bias[None]], axis=0),
        ((0, 1024 - TABLE - PROMPTS - 2), (0, 0)),
    )
    start_rows, normed, grad_branch, fq, fk, grad_down_shift = embed(
        buffer_lengths, buffer_buckets, tokens.reshape(rows, D), cotangent.reshape(rows, D), table
    )
    feed_pack = jnp.stack([up_weight, down_weight.T])
    shift_other = place.shift(up_bias, dx=1)
    pieces, feed_pack, shift_other, normed = lax.optimization_barrier(
        (pieces, feed_pack, shift_other, normed)
    )
    line = line_up(place, pieces)
    small = [norm1_gain, norm1_bias, out_bias, norm2_gain, norm2_bias, down_bias, q_bias, v_bias]
    small, line = lax.optimization_barrier((small, line))
    vectors = jnp.stack(small).astype(f32)
    qkv_offset = pair_major(
        jnp.concatenate([vectors[6:7], jnp.zeros((1, D), f32), vectors[7:8]], axis=1)
    )
    plane, (qkv_offset, vectors) = spread_plane_halves(place, line, (qkv_offset, vectors))
    qkv_full, out_full = assemble(
        place, spread_cores(place, plane), "xyc", [("zycx", (), 0, 3 * D), ("zycx", (), 3 * D, D)]
    )

    feed_line = line_up(place, spread_z(place, feed_pack))
    over_x = place.shift(feed_line, dx=1)

    def feed_weights(pieces):
        plan = [("zyc", (which,), 0, hidden_local) for which in range(2)]
        return assemble(place, pieces, "yc", plan)

    shift_own = up_bias.astype(f32)[None, :]
    shift_other = shift_other.astype(f32)[None, :]

    normed = after(normed, feed_line)
    qkv_rows = (dot(normed, qkv_full) + qkv_offset).astype(bf16)
    over_y = place.shift(feed_line, dy=1)
    attended, log_total, over_x, over_y = cover(attend(qkv_rows, fq, fk), arrays=[over_x, over_y])
    own_pieces = spread_cores(place, {(0, 0): feed_line, (1, 0): over_y})
    first_sum, normed_two = middle(attended, out_full, start_rows, vectors)

    def parts(value, order):
        many = {"x": place.nx, "y": place.ny, "c": place.nc, "z": place.nz}
        return value.reshape(tuple(many[axis] for axis in order) + (-1, value.shape[-1]))

    def feed_scatter(grads):
        made = []
        for which in range(2):
            if len(grads) == 4:
                mine, theirs = (
                    item.reshape(2, place.nz, -1, hidden_local) for item in grads[2 * which : 2 * which + 2]
                )
                made.append(Scatter(place, [mine], "yz").add(theirs, dc=1))
            else:
                made.append(Scatter(place, [parts(grads[which], "zyc")], "zyc").hop("c"))
        return made

    up_own, down_own = feed_weights(own_pieces)
    *results, over_both = cover(
        feed(normed_two, grad_branch, up_own, down_own, shift_own, rows_up),
        arrays=[place.shift(over_y, dx=1)],
    )
    sum_h, sum_db, shift_grad_own, *grads = results
    own_up, own_down = feed_scatter(grads)
    up_other, down_other = feed_weights(spread_cores(place, {(0, 0): over_x, (1, 0): over_both}))
    normed_two, _ = cover([normed_two], [own_up, own_down], [up_other])
    branch, grad_normed, shift_grad_other, *grads = cover(
        feed(normed_two, grad_branch, up_other, down_other, shift_other, rows_up, (sum_h, sum_db)),
        [own_up.hop("y")],
    )
    grad_up_shift = jnp.where(
        place.x == 0,
        jnp.concatenate([shift_grad_own, shift_grad_other], axis=1),
        jnp.concatenate([shift_grad_other, shift_grad_own], axis=1),
    )
    other_up, other_down = feed_scatter(grads)
    (first_sum,) = cover([first_sum], [other_up, other_down])
    output, grad_one, grad_attended, early, *grads = middle_back(
        buffer_lengths, buffer_buckets, first_sum, branch, grad_normed, grad_branch,
        attended, out_full, vectors, grad_down_shift, grad_up_shift, rows_in,
    )

    def weight_scatter(grads):
        if len(grads) == 2:
            mine, theirs = (parts(item.reshape(D // 2, -1), "zyx") for item in grads)
            return Scatter(place, [mine], "zyx").add(theirs, dc=1)
        return Scatter(place, [parts(grads[0], "zycx")], "zycx").hop("c")

    def back(pairs, covered):
        values = attend_back(qkv_rows, grad_attended, attended, fq, fk, log_total, pairs)
        rows_grad, sums = cover(values, covered)
        return rows_grad, sums, dot(normed, rows_grad, TN).astype(bf16)

    cuts = [0, FIRST, FIRST + (PAIRS - FIRST) // 2, PAIRS]
    send_out = weight_scatter(grads)
    back_two, sums_two, weight_two = back(
        (cuts[1], cuts[2]), [other_up.hop("y"), own_down.join(other_down), send_out]
    )
    grad_attended = after(grad_attended, weight_two)
    send_two = weight_scatter([weight_two])
    back_three, sums_three, weight_three = back(
        (cuts[2], cuts[3]), [own_up.join(other_up), own_down.hop("y"), send_two]
    )
    grad_attended = after(grad_attended, weight_three)
    send_three = weight_scatter([weight_three])
    send_own = Scatter(place, [jnp.stack([own_up.total, own_down.total])], "uz").hop("z")
    far = [k - 1 for k in range(1, place.nz) if 2 * k == place.nz]
    near = [k for k in range(place.nz - 1) if k not in far]
    back_one, sums_one, weight_one = back(
        (cuts[0], cuts[1]), [send_three, send_two.hop("x"), (send_own, far)]
    )
    back_one = after(back_one, weight_one)
    send_one = weight_scatter([weight_one])
    send_three = Scatter(
        place, [jnp.concatenate([send_three.total, send_out.total], axis=-1)], send_out.axes
    ).hop("x")
    input_grad, packed = cover(
        finish(
            buffer_lengths, buffer_buckets, start_rows, grad_one, vectors, early,
            [back_one, back_two, back_three], [sums_one, sums_two, sums_three],
            [qkv_full], [(0, at * GROUP) for at in cuts[:3]],
        ),
        [(send_own, near), send_three, send_two.hop("y"), send_one],
    )

    packed = packed.reshape(place.nc, PACK // place.nc, D)
    own = lax.dynamic_index_in_dim(packed, place.c, 0, keepdims=False)
    other = lax.dynamic_index_in_dim(packed, 1 - place.c, 0, keepdims=False)
    send_three.hop("y")
    send_one.hop("x")
    own = own + place.shift(other, dc=1)
    seen = {(0, 0): own, (1, 0): place.shift(own, dx=1), (0, 1): place.shift(own, dy=1)}
    seen[1, 1] = place.shift(own, dx=1, dy=1)
    own = 0.0
    for x in range(2):
        for y in range(2):
            line = [jnp.where(place.x == x, seen[0, dy], seen[1, dy]) for dy in range(2)]
            own = own + jnp.where(place.y == y, line[0], line[1])
    (own,) = cover([own], [send_one, send_three])
    send_one.hop("y")
    bit = 1
    while bit < place.nz:
        own = own + place.send(own, lambda z, y, c, x, bit=bit: (z ^ bit, y, c, x))
        if bit == 1:
            (own,) = cover([own], [send_one])
            send_all = Scatter(
                place,
                [jnp.concatenate([send_one.total, send_two.total, send_three.total], axis=-1)],
                send_one.axes,
            ).hop("z")
        bit *= 2
    other = place.shift(own, dc=1)
    summed = jnp.where(
        place.c == 0, jnp.concatenate([own, other], 0), jnp.concatenate([other, own], 0)
    )
    prompts_grad = summed[:PROMPTS]
    singles = [summed[PROMPTS + i] for i in range(8)]
    up_bias_grad = lax.dynamic_slice_in_dim(
        summed[PROMPTS + 8 : PROMPTS + 12].reshape(hidden), place.x * hidden_local, hidden_local, 0
    )
    prompts_grad, up_bias_grad, *singles = cover([prompts_grad, up_bias_grad] + singles, [send_all])
    qkv_weight_grad = pair_minor(add_up([term[:, : 3 * D] for term in send_all.terms]))
    out_weight_grad = add_up([term[:, 3 * D :] for term in send_all.terms])
    up_weight_grad = send_own.total[0]
    down_weight_grad = send_own.total[1].T
    return (
        output.reshape(tokens.shape),
        input_grad.reshape(tokens.shape),
        prompts_grad,
        singles[0],
        singles[1],
        qkv_weight_grad,
        singles[2],
        singles[3],
        out_weight_grad,
        singles[4],
        singles[5],
        singles[6],
        up_weight_grad,
        up_bias_grad,
        down_weight_grad,
        singles[7],
    )


def solution(mesh):
    both = ("dp", "mlp")
    in_specs = (
        P(None, both, None),
        P(None, both, None),
        P(None, both, None),
        P(None, both),
        P(),
        P(),
        P(),
        P(),
        P(both, None),
        P(),
        P(),
        P(both, None),
        P(),
        P(),
        P(),
        P("dp", "mlp"),
        P("mlp"),
        P("mlp", "dp"),
        P(),
    )
    out_specs = (
        P(None, both, None),
        P(None, both, None),
        P(),
        P(),
        P(),
        P(both, None),
        P(),
        P(),
        P(both, None),
        P(),
        P(),
        P(),
        P("dp", "mlp"),
        P("mlp"),
        P("mlp", "dp"),
        P(),
    )
    return jax.shard_map(
        per_device, mesh=mesh, in_specs=in_specs, out_specs=out_specs, check_vma=False
    )
```

```python
import math

import jax
import jax.numpy as jnp
from jax import lax
from jax.experimental import pallas as pl
from jax.experimental.pallas import tpu as pltpu
from jax.sharding import PartitionSpec as P

D = 768
HEADS = 12
HEAD_DIM = 64
PAIRS = 6
PROMPTS = 50
LEN_LOW = 101
LEN_MID = 197
TABLE = 875
SLOTS = 4
ROWS = 640
GROUP = 3 * 128
PACK = 64
BLOCK = 320
weigh = 5
FIRST = 2
MIDDLE = 40
GAIN_ONE, SHIFT_ONE, OUT_BIAS, GAIN_TWO, SHIFT_TWO, DOWN_BIAS = (slice(i, i + 1) for i in range(6))

epsilon = 1e-06
bf16 = jnp.bfloat16
f32 = jnp.float32
log2_e = 1.4426950408889634
score_scale = log2_e / math.sqrt(HEAD_DIM)
erf_p = 0.3275911
erf_a = (0.254829592, -0.284496736, 1.421413741, -1.453152027, 1.061405429)

NT = (((1,), (1,)), ((), ()))
NN = (((1,), (0,)), ((), ()))
TN = (((0,), (0,)), ((), ()))


def cost(flops, bytes_accessed, transcendentals):
    return pl.CostEstimate(
        flops=weigh * flops, bytes_accessed=weigh * bytes_accessed, transcendentals=weigh * transcendentals
    )


def dot(left, right, dims=NN):
    return lax.dot_general(left, right, dims, preferred_element_type=f32)


def row_plan(lengths_ref, buckets_ref, buffer, rows):
    sequence = jnp.zeros_like(rows)
    start = jnp.zeros_like(rows)
    end = 0
    for slot in range(SLOTS):
        length = lengths_ref[buffer, slot]
        end = end + jnp.where(length > 0, length + PROMPTS, 0)
        sequence = sequence + jnp.where(end <= rows, 1, 0)
        start = jnp.where(end <= rows, end, start)
    position = rows - start
    bucket = buckets_ref[buffer]
    table = jnp.where(bucket == 0, 0, jnp.where(bucket == 1, LEN_LOW, LEN_LOW + LEN_MID))
    inside = sequence < SLOTS
    prompt = inside & (position < PROMPTS)
    image = inside & (position >= PROMPTS)
    index = jnp.where(
        prompt,
        TABLE + position,
        jnp.where(image, jnp.clip(table + position - PROMPTS, 0, TABLE - 1), -1),
    )
    return sequence, position, inside, prompt, image, index


def norm_stats(values_in):
    average = jnp.mean(values_in, axis=-1, keepdims=True)
    centred = values_in - average
    variance = jnp.mean(centred * centred, axis=-1, keepdims=True)
    inverse = lax.rsqrt(variance + epsilon)
    return centred * inverse, inverse


def norm_back(grad_normed, normal, inverse, gain):
    scaled = grad_normed * gain
    mean_one = jnp.mean(scaled, axis=-1, keepdims=True)
    mean_two = jnp.mean(scaled * normal, axis=-1, keepdims=True)
    return (scaled - mean_one - normal * mean_two) * inverse


def add_rows(ref, step, row, value):
    total = jnp.sum(value, axis=0, keepdims=True)

    @pl.when(step == 0)
    def _():
        ref[row : row + 1, :] = total

    @pl.when(step > 0)
    def _():
        ref[row : row + 1, :] += total


def add_product(ref, step, value):
    @pl.when(step == 0)
    def _():
        ref[...] = value

    @pl.when(step > 0)
    def _():
        ref[...] += value


def weight_shapes(columns, rows_in):
    wide = 2 * rows_in
    if wide % 16 == 0:
        return [jax.ShapeDtypeStruct((D // (2 * wide), wide, columns), bf16)] * 2
    return [jax.ShapeDtypeStruct((D, columns), bf16)]


def store_weight(refs, value, rows_in):
    if len(refs) == 1:
        refs[0][...] = value.astype(bf16)
        return
    grid = value.reshape(-1, 2, 2 * rows_in, value.shape[-1])
    first = lax.rem(lax.axis_index("dp"), 2) == 0
    refs[0][...] = jnp.where(first, grid[:, 0], grid[:, 1]).astype(bf16)
    refs[1][...] = jnp.where(first, grid[:, 1], grid[:, 0]).astype(bf16)


def block_rows(shape, axis):
    step = pl.program_id(0)
    per = ROWS // BLOCK
    ids = lax.broadcasted_iota(jnp.int32, shape, axis) + lax.rem(step, per) * BLOCK
    return lax.div(step, per), ids


def embed_kernel(
    lengths_ref, buckets_ref, tokens_ref, cot_ref, table_ref,
    h_ref, a_ref, gm_ref, fq_ref, fk_ref, sum_ref,
):
    buffer, ids = block_rows((BLOCK, 1), 0)
    lane = lax.broadcasted_iota(jnp.int32, (1, 128), 1)
    sequence, _, inside, _, image, index = row_plan(lengths_ref, buckets_ref, buffer, ids)
    places = lax.broadcasted_iota(jnp.int32, (1, table_ref.shape[0]), 1)
    hits = jnp.where(places == index, 1.0, 0.0).astype(bf16)
    start = dot(hits, table_ref[...]) + jnp.where(image, tokens_ref[...].astype(f32), 0.0)
    h_ref[...] = start
    normal, _ = norm_stats(start)
    last = TABLE + PROMPTS
    gain = table_ref[last : last + 1, :].astype(f32)
    shift = table_ref[last + 1 : last + 2, :].astype(f32)
    a_ref[...] = (normal * gain + shift).astype(bf16)
    grad = jnp.where(inside, cot_ref[...].astype(f32), 0.0)
    gm_ref[...] = grad.astype(bf16)
    same = lane == sequence
    fq_ref[...] = jnp.where(same, 1.0, 0.0).astype(bf16)
    ones = jnp.where((lane >= 8) & (lane < 11), 1.0, 0.0)
    fk_ref[...] = jnp.where((lane <= SLOTS) & ~same, -1e30, ones).astype(bf16)
    add_rows(sum_ref, pl.program_id(0), 0, grad)


def whole_spec(shape):
    return pl.BlockSpec(shape, lambda b: (0,) * len(shape), pipeline_mode=pl.Buffered(1))


def scalar_spec():
    return pl.BlockSpec(memory_space=pltpu.SMEM)


def buffer_spec(columns):
    return pl.BlockSpec((BLOCK, columns), lambda b: (b, 0))


def buffer_params(mib=28):
    return pltpu.CompilerParams(dimension_semantics=("arbitrary",), vmem_limit_bytes=mib << 20)


def embed(lengths, buckets, tokens, cotangent, table):
    rows = tokens.shape[0]
    kept = whole_spec((1, D))
    return pl.pallas_call(
        embed_kernel,
        grid=(rows // BLOCK,),
        in_specs=[
            scalar_spec(), scalar_spec(), buffer_spec(D), buffer_spec(D), whole_spec(table.shape),
        ],
        out_specs=[buffer_spec(D), buffer_spec(D), buffer_spec(D), buffer_spec(128), buffer_spec(128), kept],
        out_shape=[
            jax.ShapeDtypeStruct((rows, D), f32),
            jax.ShapeDtypeStruct((rows, D), bf16),
            jax.ShapeDtypeStruct((rows, D), bf16),
            jax.ShapeDtypeStruct((rows, 128), bf16),
            jax.ShapeDtypeStruct((rows, 128), bf16),
            jax.ShapeDtypeStruct((1, D), f32),
        ],
        compiler_params=buffer_params(56),
        cost_estimate=cost(
            flops=2 * rows * table.shape[0] * D, bytes_accessed=rows * D * 12, transcendentals=0
        ),
        name="embed",
    )(lengths, buckets, tokens, cotangent, table)


def middle_kernel(o_ref, w_ref, h_ref, vec_ref, h1_ref, b_ref):
    total = h_ref[...] + dot(o_ref[...], w_ref[...]) + vec_ref[OUT_BIAS]
    h1_ref[...] = total
    normal, _ = norm_stats(total)
    b_ref[...] = (normal * vec_ref[GAIN_TWO] + vec_ref[SHIFT_TWO]).astype(bf16)


def middle(o, weight, start, vectors):
    rows = start.shape[0]
    return pl.pallas_call(
        middle_kernel,
        grid=(rows // BLOCK,),
        in_specs=[
            buffer_spec(D), whole_spec((D, D)), buffer_spec(D), whole_spec((8, D)),
        ],
        out_specs=[buffer_spec(D), buffer_spec(D)],
        out_shape=[jax.ShapeDtypeStruct((rows, D), f32), jax.ShapeDtypeStruct((rows, D), bf16)],
        compiler_params=buffer_params(),
        cost_estimate=cost(
            flops=2 * rows * D * D, bytes_accessed=rows * D * 12, transcendentals=0
        ),
        name="middle",
    )(o, weight, start, vectors)


def middle_back_kernel(
    h1_ref, db_ref, gm_ref, o_ref, w_ref, vec_ref, gdown_ref, gup_ref, g1_ref, do_ref, early_ref,
    *gw_refs, rows_in,
):
    *gw_refs, gw_s = gw_refs
    step = pl.program_id(0)
    normal, inverse = norm_stats(h1_ref[...])
    db = db_ref[...]
    g1 = gm_ref[...].astype(f32) + norm_back(db, normal, inverse, vec_ref[GAIN_TWO])
    g1_ref[...] = g1
    ga = g1.astype(bf16)
    do_ref[...] = dot(ga, w_ref[...], NT).astype(bf16)
    for row, value in ((0, g1), (1, db * normal), (2, db)):
        add_rows(early_ref, step, row, value)
    add_product(gw_s, step, dot(o_ref[...], ga, TN))

    @pl.when(step == pl.num_programs(0) - 1)
    def _():
        store_weight(gw_refs, gw_s[...], rows_in)
        early_ref[3:4, :] = gdown_ref[...]
        for i in range(gup_ref.shape[1] // D):
            early_ref[4 + i : 5 + i, :] = gup_ref[:, i * D : (i + 1) * D]


def middle_back(h1, db, gm, o, weight, vectors, grad_down, grad_up, rows_in):
    rows = h1.shape[0]
    wide = buffer_spec(D)
    grads = weight_shapes(D, rows_in)
    return pl.pallas_call(
        lambda *refs: middle_back_kernel(*refs, rows_in=rows_in),
        grid=(rows // BLOCK,),
        in_specs=[
            wide, wide, wide, wide, whole_spec((D, D)),
            whole_spec((8, D)), whole_spec((1, D)), whole_spec(grad_up.shape),
        ],
        out_specs=[wide, wide, whole_spec((8, D))] + [whole_spec(item.shape) for item in grads],
        out_shape=[
            jax.ShapeDtypeStruct((rows, D), f32),
            jax.ShapeDtypeStruct((rows, D), bf16),
            jax.ShapeDtypeStruct((8, D), f32),
        ]
        + grads,
        scratch_shapes=[pltpu.VMEM((D, D), f32)],
        compiler_params=buffer_params(MIDDLE),
        cost_estimate=cost(
            flops=4 * rows * D * D, bytes_accessed=rows * D * 18, transcendentals=0
        ),
        name="middle_back",
    )(h1, db, gm, o, weight, vectors, grad_down, grad_up)


def finish_kernel(*refs, plan):
    lengths_ref, buckets_ref, h_ref, g1_ref, vec_ref, early_ref = refs[:6]
    grads, sums_in, weights = refs[6 : 6 + len(plan)], refs[6 + len(plan) : 6 + 2 * len(plan)], refs[6 + 2 * len(plan) : -2]
    input_ref, pack_ref = refs[-2:]
    step = pl.program_id(0)
    count = pack_ref.shape[0]
    buffer, ids = block_rows((BLOCK, 1), 0)
    _, _, _, _, image, _ = row_plan(lengths_ref, buckets_ref, buffer, ids)
    da = 0.0
    for grad, (which, at) in zip(grads, plan):
        da = da + dot(grad[...], weights[which][:, at : at + grad.shape[1]], NT)
    normal, inverse = norm_stats(h_ref[...])
    g0 = g1_ref[...] + norm_back(da, normal, inverse, vec_ref[GAIN_ONE])
    input_ref[...] = jnp.where(image, g0, 0.0)
    _, across = block_rows((1, BLOCK), 1)
    _, position, _, prompt, _, _ = row_plan(lengths_ref, buckets_ref, buffer, across)
    wanted = lax.broadcasted_iota(jnp.int32, (count, 1), 0)
    hits = jnp.where(prompt & (wanted == position), 1.0, 0.0).astype(bf16)
    sums = sum(dot(hits, part) for part in split_three(g0)[:2])
    lines = [jnp.sum(da * normal, axis=0, keepdims=True), jnp.sum(da, axis=0, keepdims=True)]
    for row, line in enumerate(lines):
        sums = jnp.where(wanted == PROMPTS + row, line, sums)

    @pl.when(step == 0)
    def _():
        pack_ref[...] = sums

    @pl.when(step > 0)
    def _():
        pack_ref[...] += sums

    @pl.when(step == pl.num_programs(0) - 1)
    def _():
        at = 0
        for ref in sums_in:
            for pair in range(ref.shape[1] // GROUP):
                to = slice(at, at + 128)
                at += 128
                for row, part in ((PROMPTS + 2, 0), (PROMPTS + 3, 2)):
                    lanes = slice(pair * GROUP + part * 128, pair * GROUP + part * 128 + 128)
                    pack_ref[row : row + 1, to] = ref[0:1, lanes]
        pack_ref[PROMPTS + 4 : PROMPTS + 12, :] = early_ref[...]


def finish(lengths, buckets, start, g1, vectors, early, grads, sums, weights, plan):
    rows = start.shape[0]
    wide = buffer_spec(D)
    return pl.pallas_call(
        lambda *refs: finish_kernel(*refs, plan=plan),
        grid=(rows // BLOCK,),
        in_specs=[scalar_spec(), scalar_spec(), wide, wide, whole_spec((8, D)), whole_spec((8, D))]
        + [buffer_spec(item.shape[1]) for item in grads]
        + [whole_spec(item.shape) for item in sums]
        + [whole_spec(item.shape) for item in weights],
        out_specs=[wide, whole_spec((PACK, D))],
        out_shape=[jax.ShapeDtypeStruct((rows, D), f32), jax.ShapeDtypeStruct((PACK, D), f32)],
        compiler_params=buffer_params(),
        cost_estimate=cost(
            flops=6 * rows * D * D, bytes_accessed=rows * D * 18, transcendentals=0
        ),
        name="finish",
    )(lengths, buckets, start, g1, vectors, early, *grads, *sums, *weights)


def attend_kernel(qkv_ref, fq_ref, fk_ref, o_ref, lse_ref, *, chunk):
    pair = pl.program_id(1)
    lane = lax.broadcasted_iota(jnp.int32, (1, 128), 1)
    keys = jnp.concatenate([qkv_ref[:, 128:256], fk_ref[...]], axis=1)
    values = jnp.concatenate([qkv_ref[:, 256:384], jnp.ones((ROWS, 128), bf16)], axis=1)
    for step in range(ROWS // chunk):
        rows = slice(step * chunk, (step + 1) * chunk)
        queries = qkv_ref[rows, 0:128]
        marks = fq_ref[rows, :]
        outs = []
        lse = lse_ref[rows, :]
        for half in range(2):
            keep = (lane < 64) if half == 0 else (lane >= 64)
            own = jnp.concatenate([jnp.where(keep, queries, jnp.zeros_like(queries)), marks], axis=1)
            scores = dot(own, keys, NT)
            top = jnp.max(scores, axis=1, keepdims=True)
            weights = jnp.exp2((scores - top) * score_scale)
            mixed = dot(weights.astype(bf16), values)
            total = mixed[:, 128:129]
            outs.append(mixed[:, :128] / total)
            log_total = top + jnp.log2(total) * (1.0 / score_scale)
            lse = jnp.where(lane == pair * 2 + half, log_total, lse)
        o_ref[rows, :] = jnp.where(lane < 64, outs[0], outs[1]).astype(bf16)
        lse_ref[rows, :] = lse


def attend(qkv, fq, fk, chunk=320):
    rows = qkv.shape[0]
    mark = pl.BlockSpec((ROWS, 128), lambda b, p: (b, 0))
    return pl.pallas_call(
        lambda *refs: attend_kernel(*refs, chunk=chunk),
        grid=(rows // ROWS, qkv.shape[1] // GROUP),
        in_specs=[pl.BlockSpec((ROWS, GROUP), lambda b, p: (b, p)), mark, mark],
        out_specs=[pl.BlockSpec((ROWS, 128), lambda b, p: (b, p)), mark],
        out_shape=[
            jax.ShapeDtypeStruct((rows, qkv.shape[1] // 3), bf16),
            jax.ShapeDtypeStruct((rows, 128), f32),
        ],
        compiler_params=pltpu.CompilerParams(
            dimension_semantics=("arbitrary", "arbitrary"), vmem_limit_bytes=24 << 20
        ),
        cost_estimate=cost(
            flops=5 * rows * ROWS * qkv.shape[1],
            bytes_accessed=rows * qkv.shape[1] * 3,
            transcendentals=rows * ROWS * qkv.shape[1] // 192,
        ),
        name="attend",
    )(qkv, fq, fk)


def split_three(value):
    first = value.astype(bf16)
    rest = value - first.astype(f32)
    second = rest.astype(bf16)
    third = (rest - second.astype(f32)).astype(bf16)
    return first, second, third


def attend_back_kernel(
    qkv_ref, do_ref, o_ref, fq_ref, fk_ref, lse_ref, dqkv_ref, sum_ref, ds_ref, *, chunk, low
):
    pair, buffer = low + pl.program_id(0), pl.program_id(1)
    lane = lax.broadcasted_iota(jnp.int32, (1, 128), 1)
    queries = qkv_ref[:, 0:128]
    grads = do_ref[...]
    marks = fq_ref[...]
    product = grads.astype(f32) * o_ref[...].astype(f32)
    lse = lse_ref[...]
    zero = jnp.zeros_like(queries)
    own_q, own_g, wide_q, wide_g = [], [], [], []
    for half in range(2):
        keep = (lane < 64) if half == 0 else (lane >= 64)
        shift = -jnp.sum(jnp.where(lane == pair * 2 + half, lse, 0.0), axis=1, keepdims=True)
        inner = -jnp.sum(jnp.where(keep, product, 0.0), axis=1, keepdims=True)
        s0, s1, s2 = split_three(shift)
        i0, i1, i2 = split_three(inner)
        mark_q = jnp.where(lane == 8, s0, jnp.where(lane == 9, s1, jnp.where(lane == 10, s2, marks)))
        mark_g = jnp.where(lane == 8, i0, jnp.where(lane == 9, i1, jnp.where(lane == 10, i2, zero)))
        q_half = jnp.where(keep, queries, zero)
        g_half = jnp.where(keep, grads, zero)
        own_q.append(q_half)
        own_g.append(g_half)
        wide_q.append(jnp.concatenate([q_half, mark_q], axis=1))
        wide_g.append(jnp.concatenate([g_half, mark_g], axis=1))
    for step in range(ROWS // chunk):
        rows = slice(step * chunk, (step + 1) * chunk)
        keys = jnp.concatenate([qkv_ref[rows, 128:256], fk_ref[rows, :]], axis=1)
        values = jnp.concatenate([qkv_ref[rows, 256:384], fk_ref[rows, :]], axis=1)
        dv = jnp.zeros((chunk, 128), f32)
        dk = jnp.zeros((chunk, 128), f32)
        for half in range(2):
            weights = jnp.exp2(dot(keys, wide_q[half], NT) * score_scale)
            ds = (weights * dot(values, wide_g[half], NT)).astype(bf16)
            ds_ref[half, rows, :] = ds
            dv = dv + dot(weights.astype(bf16), own_g[half])
            dk = dk + dot(ds, own_q[half])
        dqkv_ref[rows, 256:384] = dv.astype(bf16)
        dqkv_ref[rows, 128:256] = (dk * 0.125).astype(bf16)
        line = jnp.sum(dv, axis=0, keepdims=True)
        dv_sum = dv_sum + line if step else line
    keys_t = qkv_ref[:, 128:256].T
    parts = [dot(keys_t, ds_ref[half]).T for half in range(2)]
    dq = jnp.where(lane < 64, parts[0], parts[1]) * 0.125
    dqkv_ref[:, 0:128] = dq.astype(bf16)
    dq_sum = jnp.sum(dq, axis=0, keepdims=True)

    @pl.when(buffer == 0)
    def _():
        sum_ref[0:1, 0:128] = dq_sum
        sum_ref[0:1, 256:384] = dv_sum

    @pl.when(buffer > 0)
    def _():
        sum_ref[0:1, 0:128] += dq_sum
        sum_ref[0:1, 256:384] += dv_sum


def attend_back(qkv, do, o, fq, fk, lse, pairs, chunk=640):
    rows = qkv.shape[0]
    low, count = pairs[0], pairs[1] - pairs[0]
    columns = count * GROUP
    mark = pl.BlockSpec((ROWS, 128), lambda p, b: (b, 0))
    part = pl.BlockSpec((ROWS, 128), lambda p, b: (b, low + p))
    return pl.pallas_call(
        lambda *refs: attend_back_kernel(*refs, chunk=chunk, low=low),
        grid=(count, rows // ROWS),
        in_specs=[
            pl.BlockSpec((ROWS, GROUP), lambda p, b: (b, low + p)), part, part, mark, mark, mark,
        ],
        out_specs=[
            pl.BlockSpec((ROWS, GROUP), lambda p, b: (b, p)),
            pl.BlockSpec((8, GROUP), lambda p, b: (0, p)),
        ],
        out_shape=[
            jax.ShapeDtypeStruct((rows, columns), bf16),
            jax.ShapeDtypeStruct((8, columns), f32),
        ],
        scratch_shapes=[pltpu.VMEM((2, ROWS, ROWS), bf16)],
        compiler_params=pltpu.CompilerParams(
            dimension_semantics=("arbitrary", "arbitrary"), vmem_limit_bytes=24 << 20
        ),
        cost_estimate=cost(
            flops=12 * rows * ROWS * columns,
            bytes_accessed=rows * columns * 6,
            transcendentals=rows * ROWS * columns // 192,
        ),
        name="attend_back",
    )(qkv, do, o, fq, fk, lse)


def gelu_parts(u):
    z = jnp.abs(u) * 0.7071067811865476
    t = 1.0 / (1.0 + erf_p * z)
    e = jnp.exp2(u * u * (-0.5 * log2_e))
    series = t * (erf_a[0] + t * (erf_a[1] + t * (erf_a[2] + t * (erf_a[3] + t * erf_a[4]))))
    tail = 0.5 * series * e
    return jnp.where(u < 0, tail, 1.0 - tail), e * 0.3989422804014327


def store_halves(mine_ref, theirs_ref, value, rows):
    columns = value.shape[-1]
    grid = value.reshape(-1, 2, 2, rows, columns)
    first = lax.rem(lax.axis_index("dp"), 2) == 0
    for y in range(2):
        left, right = grid[:, y, 0].reshape(-1, columns), grid[:, y, 1].reshape(-1, columns)
        mine_ref[y] = jnp.where(first, left, right).astype(bf16)
        theirs_ref[y] = jnp.where(first, right, left).astype(bf16)


def feed_kernel(*refs, chunk, more, rows_up):
    b_ref, gm_ref, up_ref, dn_ref, ub_ref = refs[:5]
    outs = refs[5 + 2 * more : -2]
    h_ref, db_ref, gub_ref = outs[:3]
    act_s, du_s = refs[-2:]
    up, dn, ub = up_ref[...], dn_ref[...], ub_ref[...]

    @pl.when(pl.program_id(0) == 0)
    def _():
        h_ref[...] = refs[5][...] if more else jnp.zeros_like(h_ref)
        db_ref[...] = refs[6][...] if more else jnp.zeros_like(db_ref)

    sums = jnp.zeros((1, ub.shape[1]), f32)
    chunks = [slice(at, at + chunk) for at in range(0, b_ref.shape[0], chunk)]
    for rows in chunks:
        u = dot(b_ref[rows, :], up) + ub
        da = dot(gm_ref[rows, :], dn)
        cdf, pdf = gelu_parts(u)
        du = da * (cdf + u * pdf)
        sums = sums + jnp.sum(du, axis=0, keepdims=True)
        act_s[rows, :] = (u * cdf).astype(bf16)
        du_s[rows, :] = du.astype(bf16)
    for rows in chunks:
        h_ref[rows, :] += dot(act_s[rows, :], dn, NT)
        db_ref[rows, :] += dot(du_s[rows, :], up, NT)
    gub_ref[...] = sums
    for i, (left, right) in enumerate(((b_ref, du_s), (gm_ref, act_s))):
        grad = dot(left[...], right[...], TN)
        if rows_up:
            store_halves(outs[3 + 2 * i], outs[4 + 2 * i], grad, rows_up)
        else:
            outs[3 + i][...] = grad.astype(bf16)


def feed(b, gm, up, dn, ub, rows_up, before=(), block=768, chunk=320):
    rows = b.shape[0]
    hidden = up.shape[1]
    rows_up = rows_up if rows_up % 16 == 0 else 0
    full = pl.BlockSpec((rows, D), lambda j: (0, 0), pipeline_mode=pl.Buffered(1))
    weight = pl.BlockSpec((D, block), lambda j: (0, j))
    bias = pl.BlockSpec((1, block), lambda j: (0, j))
    if rows_up:
        grad = pl.BlockSpec((2, D // 4, block), lambda j: (0, 0, j))
        shapes = [jax.ShapeDtypeStruct((2, D // 4, hidden), bf16)] * 4
    else:
        grad = pl.BlockSpec((D, block), lambda j: (0, j))
        shapes = [jax.ShapeDtypeStruct((D, hidden), bf16)] * 2
    return pl.pallas_call(
        lambda *refs: feed_kernel(*refs, chunk=chunk, more=bool(before), rows_up=rows_up),
        grid=(hidden // block,),
        in_specs=[full, full, weight, weight, bias] + [full] * len(before),
        out_specs=[full, full, bias] + [grad] * len(shapes),
        out_shape=[jax.ShapeDtypeStruct((rows, D), f32)] * 2
        + [jax.ShapeDtypeStruct(ub.shape, f32)]
        + shapes,
        scratch_shapes=[pltpu.VMEM((rows, block), bf16)] * 2,
        compiler_params=pltpu.CompilerParams(
            dimension_semantics=("arbitrary",), vmem_limit_bytes=(46 if before else 38) << 20
        ),
        cost_estimate=cost(
            flops=12 * rows * hidden * D,
            bytes_accessed=rows * D * 12 + hidden * D * 8,
            transcendentals=2 * rows * hidden,
        ),
        name="feed",
    )(b, gm, up, dn, ub, *before)


def pair_major(columns):
    lead = columns.shape[:-1]
    return columns.reshape(lead + (3, PAIRS, 128)).swapaxes(-3, -2).reshape(lead + (3 * D,))


def pair_minor(columns):
    lead = columns.shape[:-1]
    return columns.reshape(lead + (PAIRS, 3, 128)).swapaxes(-3, -2).reshape(lead + (3 * D,))


class Place:
    def __init__(self):
        dp, self.nx = lax.axis_size("dp"), lax.axis_size("mlp")
        self.ny, self.nc = 2, 2
        self.nz = dp // (self.ny * self.nc)
        index = lax.axis_index("dp")
        self.x = lax.axis_index("mlp")
        self.c = index % self.nc
        self.y = (index // self.nc) % self.ny
        self.z = index // (self.nc * self.ny)

    label = "hop"

    def send(self, value, move):
        pairs = []
        for z in range(self.nz):
            for y in range(self.ny):
                for c in range(self.nc):
                    for x in range(self.nx):
                        source = ((z * self.ny + y) * self.nc + c) * self.nx + x
                        z2, y2, c2, x2 = move(z, y, c, x)
                        pairs.append((source, ((z2 * self.ny + y2) * self.nc + c2) * self.nx + x2))
        with jax.named_scope(self.label):
            return lax.ppermute(value, ("dp", "mlp"), pairs)

    def shift(self, value, dz=0, dy=0, dc=0, dx=0):
        return self.send(
            value,
            lambda z, y, c, x: (
                (z + dz) % self.nz,
                (y + dy) % self.ny,
                (c + dc) % self.nc,
                (x + dx) % self.nx,
            ),
        )


def spread_z(place, shard):
    return {k: place.shift(shard, dz=k) if k else shard for k in range(place.nz)}


def line_up(place, pieces):
    ids = jnp.arange(place.nz).reshape((place.nz,) + (1,) * pieces[0].ndim)
    whole = jnp.broadcast_to(pieces[0][None], (place.nz,) + pieces[0].shape)
    for k in range(1, place.nz):
        whole = jnp.where(ids == (place.z - k) % place.nz, pieces[k][None], whole)
    return whole


def spread_plane(place, line):
    over_x = place.shift(line, dx=1)
    over_y = place.shift(line, dy=1)
    return {(0, 0): line, (1, 0): over_x, (0, 1): over_y, (1, 1): place.shift(over_y, dx=1)}


def spread_plane_halves(place, line, other):
    half = line.shape[-1] // 2
    over_x = place.shift(line, dx=1)
    over_y = place.shift(line, dy=1)
    over_x, over_y, other = lax.optimization_barrier((over_x, over_y, other))
    pieces = {
        (0, 0, 0): line,
        (1, 0, 0): over_x,
        (0, 1, 0): over_y,
        (1, 1, 0): place.shift(over_x[..., :half], dy=1),
        (1, 1, half): place.shift(over_y[..., half:], dx=1),
    }
    return pieces, other


def spread_cores(place, pieces):
    whole = {key[:-1] + (0,) + key[-1:]: piece for key, piece in pieces.items()}
    for key, piece in pieces.items():
        whole[key[:-1] + (1,) + key[-1:]] = place.shift(piece, dc=1)
    return whole


def assemble_kernel(*refs, keys, plan, nx):
    sources, targets = refs[: len(keys)], refs[len(keys) :]
    index = lax.axis_index("dp")
    here = {"x": lax.axis_index("mlp"), "c": index % 2, "y": (index // 2) % 2}
    many = {"x": nx, "c": 2, "y": 2}
    for source, (key, low) in zip(sources, keys):
        spot = {axis: lax.rem(here[axis] + many[axis] - key[axis], many[axis]) for axis in key}
        spot["z"] = slice(None)
        high = low + source.shape[-1]
        for target, (order, picks, first, columns) in zip(targets, plan):
            left, right = max(low, first), min(high, first + columns)
            if left >= right:
                continue
            take = (slice(None),) + picks + (slice(None), slice(left - low, right - low))
            place = tuple(spot[axis] for axis in order)
            target[place + (slice(None), slice(left - first, right - first))] = source[take]


def assemble(place, pieces, names, plan):
    keys = [(dict(zip(names, key[:-1])), key[-1]) for key in pieces]
    arrays = list(pieces.values())
    many = {"x": place.nx, "y": place.ny, "c": place.nc, "z": place.nz}
    rows = arrays[0].shape[-2]
    shapes = [tuple(many[axis] for axis in order) + (rows, columns) for order, _, _, columns in plan]
    size = sum(math.prod(shape) for shape in shapes)
    out = pl.pallas_call(
        lambda *refs: assemble_kernel(*refs, keys=keys, plan=plan, nx=place.nx),
        in_specs=[pl.BlockSpec(memory_space=pltpu.VMEM)] * len(arrays),
        out_specs=[pl.BlockSpec(memory_space=pltpu.VMEM)] * len(plan),
        out_shape=[jax.ShapeDtypeStruct(shape, bf16) for shape in shapes],
        compiler_params=pltpu.CompilerParams(vmem_limit_bytes=4 << 20),
        cost_estimate=cost(flops=0, bytes_accessed=4 * size, transcendentals=0),
        name="assemble",
    )(*arrays)
    return [item.reshape(-1, item.shape[-1]) for item in out]


def after(value, *others):
    return lax.optimization_barrier((value,) + others)[0]


def cover(values, scatters=(), arrays=()):
    picked = []
    for item in scatters:
        scatter, picks = item if isinstance(item, tuple) else (item, range(len(item.fresh)))
        picked += [(scatter, scatter.fresh[i]) for i in picks]
    moved = [scatter.terms[i] for scatter, i in picked]
    values, moved, arrays = lax.optimization_barrier((list(values), moved, list(arrays)))
    for (scatter, i), term in zip(picked, moved):
        scatter.terms[i] = term
    return list(values) + list(arrays)


class Scatter:
    def __init__(self, place, terms, axes):
        self.place, self.terms, self.axes = place, list(terms), axes

    def take(self, axis, index):
        at = self.axes.index(axis)
        return [lax.dynamic_index_in_dim(term, index, at, keepdims=False) for term in self.terms]

    def hop(self, axis):
        place = self.place
        here, many = getattr(place, axis), getattr(place, "n" + axis)
        moved = []
        for k in range(1, many):
            theirs = add_up(self.take(axis, (here + k) % many)).astype(bf16)
            moved.append(place.shift(theirs, **{"d" + axis: k}))
        terms = self.take(axis, here)
        self.fresh = range(len(terms), len(terms) + len(moved))
        self.terms = terms + moved
        self.axes = self.axes.replace(axis, "")
        return self

    def hop_plane(self):
        place = self.place
        moved = []
        for dx, dy in ((1, 0), (0, 1), (1, 1)):
            part = Scatter(place, self.terms, self.axes)
            part.terms, part.axes = part.take("x", (place.x + dx) % place.nx), part.axes.replace("x", "")
            theirs = add_up(part.take("y", (place.y + dy) % place.ny)).astype(bf16)
            moved.append(place.shift(theirs, dx=dx, dy=dy))
        for axis in "xy":
            self.terms = self.take(axis, getattr(place, axis))
            self.axes = self.axes.replace(axis, "")
        self.fresh = range(len(self.terms), len(self.terms) + 3)
        self.terms = self.terms + moved
        return self

    def add(self, theirs, **move):
        self.fresh = range(len(self.terms), len(self.terms) + 1)
        self.terms = self.terms + [self.place.shift(theirs, **move)]
        return self

    def join(self, other):
        return self.add(add_up(other.terms).astype(bf16), dx=1)

    @property
    def total(self):
        return add_up(self.terms)


def add_up(terms):
    return sum(term.astype(f32) for term in terms)


def per_device(
    tokens,
    cotangent,
    lengths,
    buckets,
    pos_table,
    prompts,
    norm1_gain,
    norm1_bias,
    qkv_weight,
    q_bias,
    v_bias,
    out_weight,
    out_bias,
    norm2_gain,
    norm2_bias,
    up_weight,
    up_bias,
    down_weight,
    down_bias,
):
    mlp_size = lax.axis_size("mlp")
    micro_count, local_rows = tokens.shape[:2]
    rows = micro_count * local_rows
    hidden_local = up_weight.shape[1]
    hidden = hidden_local * mlp_size

    place = Place()
    rows_up = up_weight.shape[0]
    qkv_shard = pair_major(qkv_weight)
    rows_in = qkv_weight.shape[0]
    pieces = spread_z(place, jnp.concatenate([qkv_shard, out_weight], axis=1))
    buffer_lengths, buffer_buckets = lengths.reshape(-1, SLOTS), buckets.reshape(-1)
    table = jnp.pad(
        jnp.concatenate([pos_table, prompts, norm1_gain[None], norm1_bias[None]], axis=0),
        ((0, 1024 - TABLE - PROMPTS - 2), (0, 0)),
    )
    start_rows, normed, grad_branch, fq, fk, grad_down_shift = embed(
        buffer_lengths, buffer_buckets, tokens.reshape(rows, D), cotangent.reshape(rows, D), table
    )
    feed_pack = jnp.stack([up_weight, down_weight.T])
    shift_other = place.shift(up_bias, dx=1)
    pieces, feed_pack, shift_other, normed = lax.optimization_barrier(
        (pieces, feed_pack, shift_other, normed)
    )
    line = line_up(place, pieces)
    small = [norm1_gain, norm1_bias, out_bias, norm2_gain, norm2_bias, down_bias, q_bias, v_bias]
    small, line = lax.optimization_barrier((small, line))
    vectors = jnp.stack(small).astype(f32)
    qkv_offset = pair_major(
        jnp.concatenate([vectors[6:7], jnp.zeros((1, D), f32), vectors[7:8]], axis=1)
    )
    plane, (qkv_offset, vectors) = spread_plane_halves(place, line, (qkv_offset, vectors))
    qkv_full, out_full = assemble(
        place, spread_cores(place, plane), "xyc", [("zycx", (), 0, 3 * D), ("zycx", (), 3 * D, D)]
    )

    feed_line = line_up(place, spread_z(place, feed_pack))
    over_x = place.shift(feed_line, dx=1)

    def feed_weights(pieces):
        plan = [("zyc", (which,), 0, hidden_local) for which in range(2)]
        return assemble(place, pieces, "yc", plan)

    shift_own = up_bias.astype(f32)[None, :]
    shift_other = shift_other.astype(f32)[None, :]

    normed = after(normed, feed_line)
    qkv_rows = (dot(normed, qkv_full) + qkv_offset).astype(bf16)
    over_y = place.shift(feed_line, dy=1)
    attended, log_total, over_x, over_y = cover(attend(qkv_rows, fq, fk), arrays=[over_x, over_y])
    own_pieces = spread_cores(place, {(0, 0): feed_line, (1, 0): over_y})
    first_sum, normed_two = middle(attended, out_full, start_rows, vectors)

    def parts(value, order):
        many = {"x": place.nx, "y": place.ny, "c": place.nc, "z": place.nz}
        return value.reshape(tuple(many[axis] for axis in order) + (-1, value.shape[-1]))

    def feed_scatter(grads):
        made = []
        for which in range(2):
            if len(grads) == 4:
                mine, theirs = (
                    item.reshape(2, place.nz, -1, hidden_local) for item in grads[2 * which : 2 * which + 2]
                )
                made.append(Scatter(place, [mine], "yz").add(theirs, dc=1))
            else:
                made.append(Scatter(place, [parts(grads[which], "zyc")], "zyc").hop("c"))
        return made

    up_own, down_own = feed_weights(own_pieces)
    *results, over_both = cover(
        feed(normed_two, grad_branch, up_own, down_own, shift_own, rows_up),
        arrays=[place.shift(over_y, dx=1)],
    )
    sum_h, sum_db, shift_grad_own, *grads = results
    own_up, own_down = feed_scatter(grads)
    up_other, down_other = feed_weights(spread_cores(place, {(0, 0): over_x, (1, 0): over_both}))
    normed_two, _ = cover([normed_two], [own_up, own_down], [up_other])
    branch, grad_normed, shift_grad_other, *grads = cover(
        feed(normed_two, grad_branch, up_other, down_other, shift_other, rows_up, (sum_h, sum_db)),
        [own_up.hop("y")],
    )
    grad_up_shift = jnp.where(
        place.x == 0,
        jnp.concatenate([shift_grad_own, shift_grad_other], axis=1),
        jnp.concatenate([shift_grad_other, shift_grad_own], axis=1),
    )
    other_up, other_down = feed_scatter(grads)
    (first_sum,) = cover([first_sum], [other_up, other_down])
    grad_one, grad_attended, early, *grads = middle_back(
        first_sum, grad_normed, grad_branch, attended, out_full, vectors, grad_down_shift,
        grad_up_shift, rows_in,
    )

    def weight_scatter(grads):
        if len(grads) == 2:
            mine, theirs = (parts(item.reshape(D // 2, -1), "zyx") for item in grads)
            return Scatter(place, [mine], "zyx").add(theirs, dc=1)
        return Scatter(place, [parts(grads[0], "zycx")], "zycx").hop("c")

    def back(pairs, covered):
        values = attend_back(qkv_rows, grad_attended, attended, fq, fk, log_total, pairs)
        rows_grad, sums = cover(values, covered)
        return rows_grad, sums, dot(normed, rows_grad, TN).astype(bf16)

    cuts = [0, FIRST, FIRST + (PAIRS - FIRST) // 2, PAIRS]
    send_out = weight_scatter(grads)
    back_two, sums_two, weight_two = back(
        (cuts[1], cuts[2]), [other_up.hop("y"), own_down.join(other_down), send_out]
    )
    grad_attended = after(grad_attended, weight_two)
    send_two = weight_scatter([weight_two])
    back_three, sums_three, weight_three = back(
        (cuts[2], cuts[3]), [own_up.join(other_up), own_down.hop("y"), send_two]
    )
    grad_attended = after(grad_attended, weight_three)
    send_three = weight_scatter([weight_three])
    send_own = Scatter(place, [jnp.stack([own_up.total, own_down.total])], "uz").hop("z")
    far = [k - 1 for k in range(1, place.nz) if 2 * k == place.nz]
    near = [k for k in range(place.nz - 1) if k not in far]
    back_one, sums_one, weight_one = back(
        (cuts[0], cuts[1]), [send_three, send_two.hop("x"), (send_own, far)]
    )
    back_one = after(back_one, weight_one)
    send_one = weight_scatter([weight_one])
    send_three = Scatter(
        place, [jnp.concatenate([send_three.total, send_out.total], axis=-1)], send_out.axes
    ).hop("x")
    input_grad, packed = cover(
        finish(
            buffer_lengths, buffer_buckets, start_rows, grad_one, vectors, early,
            [back_one, back_two, back_three], [sums_one, sums_two, sums_three],
            [qkv_full], [(0, at * GROUP) for at in cuts[:3]],
        ),
        [(send_own, near), send_three, send_two.hop("y"), send_one],
    )

    packed = packed.reshape(place.nc, PACK // place.nc, D)
    own = lax.dynamic_index_in_dim(packed, place.c, 0, keepdims=False)
    other = lax.dynamic_index_in_dim(packed, 1 - place.c, 0, keepdims=False)
    send_three.hop("y")
    send_one.hop("x")
    own = own + place.shift(other, dc=1)
    (own,) = cover([own], [send_one, send_three])
    send_rest = Scatter(
        place, [jnp.concatenate([send_two.total, send_three.total], axis=-1)], send_three.axes
    ).hop("z")
    send_one.hop("y")
    seen = {(0, 0): own, (1, 0): place.shift(own, dx=1), (0, 1): place.shift(own, dy=1)}
    seen[1, 1] = place.shift(own, dx=1, dy=1)
    own = 0.0
    for x in range(2):
        for y in range(2):
            line = [jnp.where(place.x == x, seen[0, dy], seen[1, dy]) for dy in range(2)]
            own = own + jnp.where(place.y == y, line[0], line[1])
    (own,) = cover([own], [send_one])
    send_one.hop("z")
    first_sum, branch, _ = lax.optimization_barrier((first_sum, branch, own))
    outside = fq[:, SLOTS : SLOTS + 1].astype(f32) > 0.0
    output = jnp.where(outside, 0.0, first_sum + branch + vectors[5:6]).astype(bf16)
    bit = 1
    while bit < place.nz:
        own = own + place.send(own, lambda z, y, c, x, bit=bit: (z ^ bit, y, c, x))
        if bit == 1:
            (own,) = cover([own], [send_rest])
        bit *= 2
    (own,) = cover([own], [send_one])
    other = place.shift(own, dc=1)
    summed = jnp.where(
        place.c == 0, jnp.concatenate([own, other], 0), jnp.concatenate([other, own], 0)
    )
    prompts_grad = summed[:PROMPTS]
    singles = [summed[PROMPTS + i] for i in range(8)]
    up_bias_grad = lax.dynamic_slice_in_dim(
        summed[PROMPTS + 8 : PROMPTS + 12].reshape(hidden), place.x * hidden_local, hidden_local, 0
    )
    rest = 3 * D - FIRST * GROUP
    qkv_weight_grad = pair_minor(
        jnp.concatenate([send_one.total, add_up([term[:, :rest] for term in send_rest.terms])], axis=1)
    )
    out_weight_grad = add_up([term[:, rest:] for term in send_rest.terms])
    up_weight_grad = send_own.total[0]
    down_weight_grad = send_own.total[1].T
    return (
        output.reshape(tokens.shape),
        input_grad.reshape(tokens.shape),
        prompts_grad,
        singles[0],
        singles[1],
        qkv_weight_grad,
        singles[2],
        singles[3],
        out_weight_grad,
        singles[4],
        singles[5],
        singles[6],
        up_weight_grad,
        up_bias_grad,
        down_weight_grad,
        singles[7],
    )


def solution(mesh):
    both = ("dp", "mlp")
    in_specs = (
        P(None, both, None),
        P(None, both, None),
        P(None, both, None),
        P(None, both),
        P(),
        P(),
        P(),
        P(),
        P(both, None),
        P(),
        P(),
        P(both, None),
        P(),
        P(),
        P(),
        P("dp", "mlp"),
        P("mlp"),
        P("mlp", "dp"),
        P(),
    )
    out_specs = (
        P(None, both, None),
        P(None, both, None),
        P(),
        P(),
        P(),
        P(both, None),
        P(),
        P(),
        P(both, None),
        P(),
        P(),
        P(),
        P("dp", "mlp"),
        P("mlp"),
        P("mlp", "dp"),
        P(),
    )
    return jax.shard_map(
        per_device, mesh=mesh, in_specs=in_specs, out_specs=out_specs, check_vma=False
    )
```

```python
import math

import jax
import jax.numpy as jnp
from jax import lax
from jax.experimental import pallas as pl
from jax.experimental.pallas import tpu as pltpu
from jax.sharding import PartitionSpec as P

D = 768
HEADS = 12
HEAD_DIM = 64
PAIRS = 6
PROMPTS = 50
LEN_LOW = 101
LEN_MID = 197
TABLE = 875
SLOTS = 4
ROWS = 640
GROUP = 3 * 128
PACK = 64
BLOCK = 640
weigh = 2
FIRST = 2
MIDDLE = 40
GAIN_ONE, SHIFT_ONE, OUT_BIAS, GAIN_TWO, SHIFT_TWO, DOWN_BIAS = (slice(i, i + 1) for i in range(6))

epsilon = 1e-06
bf16 = jnp.bfloat16
f32 = jnp.float32
log2_e = 1.4426950408889634
score_scale = log2_e / math.sqrt(HEAD_DIM)
erf_p = 0.3275911
erf_a = (0.254829592, -0.284496736, 1.421413741, -1.453152027, 1.061405429)

NT = (((1,), (1,)), ((), ()))
NN = (((1,), (0,)), ((), ()))
TN = (((0,), (0,)), ((), ()))


def cost(flops, bytes_accessed, transcendentals):
    return pl.CostEstimate(
        flops=weigh * flops, bytes_accessed=weigh * bytes_accessed, transcendentals=weigh * transcendentals
    )


def dot(left, right, dims=NN):
    return lax.dot_general(left, right, dims, preferred_element_type=f32)


def row_plan(lengths_ref, buckets_ref, buffer, rows):
    sequence = jnp.zeros_like(rows)
    start = jnp.zeros_like(rows)
    end = 0
    for slot in range(SLOTS):
        length = lengths_ref[buffer, slot]
        end = end + jnp.where(length > 0, length + PROMPTS, 0)
        sequence = sequence + jnp.where(end <= rows, 1, 0)
        start = jnp.where(end <= rows, end, start)
    position = rows - start
    bucket = buckets_ref[buffer]
    table = jnp.where(bucket == 0, 0, jnp.where(bucket == 1, LEN_LOW, LEN_LOW + LEN_MID))
    inside = sequence < SLOTS
    prompt = inside & (position < PROMPTS)
    image = inside & (position >= PROMPTS)
    index = jnp.where(
        prompt,
        TABLE + position,
        jnp.where(image, jnp.clip(table + position - PROMPTS, 0, TABLE - 1), -1),
    )
    return sequence, position, inside, prompt, image, index


def norm_stats(values_in):
    average = jnp.mean(values_in, axis=-1, keepdims=True)
    centred = values_in - average
    variance = jnp.mean(centred * centred, axis=-1, keepdims=True)
    inverse = lax.rsqrt(variance + epsilon)
    return centred * inverse, inverse


def norm_back(grad_normed, normal, inverse, gain):
    scaled = grad_normed * gain
    mean_one = jnp.mean(scaled, axis=-1, keepdims=True)
    mean_two = jnp.mean(scaled * normal, axis=-1, keepdims=True)
    return (scaled - mean_one - normal * mean_two) * inverse


def add_rows(ref, step, row, value):
    total = jnp.sum(value, axis=0, keepdims=True)

    @pl.when(step == 0)
    def _():
        ref[row : row + 1, :] = total

    @pl.when(step > 0)
    def _():
        ref[row : row + 1, :] += total


def add_product(ref, step, value):
    @pl.when(step == 0)
    def _():
        ref[...] = value

    @pl.when(step > 0)
    def _():
        ref[...] += value


def weight_shapes(columns, rows_in):
    wide = 2 * rows_in
    if wide % 16 == 0:
        return [jax.ShapeDtypeStruct((D // (2 * wide), wide, columns), bf16)] * 2
    return [jax.ShapeDtypeStruct((D, columns), bf16)]


def store_weight(refs, value, rows_in):
    if len(refs) == 1:
        refs[0][...] = value.astype(bf16)
        return
    grid = value.reshape(-1, 2, 2 * rows_in, value.shape[-1])
    first = lax.rem(lax.axis_index("dp"), 2) == 0
    refs[0][...] = jnp.where(first, grid[:, 0], grid[:, 1]).astype(bf16)
    refs[1][...] = jnp.where(first, grid[:, 1], grid[:, 0]).astype(bf16)


def block_rows(shape, axis):
    step = pl.program_id(0)
    per = ROWS // BLOCK
    ids = lax.broadcasted_iota(jnp.int32, shape, axis) + lax.rem(step, per) * BLOCK
    return lax.div(step, per), ids


def embed_kernel(
    lengths_ref, buckets_ref, tokens_ref, cot_ref, table_ref,
    h_ref, a_ref, gm_ref, fq_ref, fk_ref, sum_ref,
):
    buffer, ids = block_rows((BLOCK, 1), 0)
    lane = lax.broadcasted_iota(jnp.int32, (1, 128), 1)
    sequence, _, inside, _, image, index = row_plan(lengths_ref, buckets_ref, buffer, ids)
    places = lax.broadcasted_iota(jnp.int32, (1, table_ref.shape[0]), 1)
    hits = jnp.where(places == index, 1.0, 0.0).astype(bf16)
    start = dot(hits, table_ref[...]) + jnp.where(image, tokens_ref[...].astype(f32), 0.0)
    h_ref[...] = start
    normal, _ = norm_stats(start)
    last = TABLE + PROMPTS
    gain = table_ref[last : last + 1, :].astype(f32)
    shift = table_ref[last + 1 : last + 2, :].astype(f32)
    a_ref[...] = (normal * gain + shift).astype(bf16)
    grad = jnp.where(inside, cot_ref[...].astype(f32), 0.0)
    gm_ref[...] = grad.astype(bf16)
    same = lane == sequence
    fq_ref[...] = jnp.where(same, 1.0, 0.0).astype(bf16)
    ones = jnp.where((lane >= 8) & (lane < 11), 1.0, 0.0)
    fk_ref[...] = jnp.where((lane <= SLOTS) & ~same, -1e30, ones).astype(bf16)
    add_rows(sum_ref, pl.program_id(0), 0, grad)


def whole_spec(shape):
    return pl.BlockSpec(shape, lambda b: (0,) * len(shape), pipeline_mode=pl.Buffered(1))


def scalar_spec():
    return pl.BlockSpec(memory_space=pltpu.SMEM)


def buffer_spec(columns):
    return pl.BlockSpec((BLOCK, columns), lambda b: (b, 0))


def buffer_params(mib=28):
    return pltpu.CompilerParams(dimension_semantics=("arbitrary",), vmem_limit_bytes=mib << 20)


def embed(lengths, buckets, tokens, cotangent, table):
    rows = tokens.shape[0]
    kept = whole_spec((1, D))
    return pl.pallas_call(
        embed_kernel,
        grid=(rows // BLOCK,),
        in_specs=[
            scalar_spec(), scalar_spec(), buffer_spec(D), buffer_spec(D), whole_spec(table.shape),
        ],
        out_specs=[buffer_spec(D), buffer_spec(D), buffer_spec(D), buffer_spec(128), buffer_spec(128), kept],
        out_shape=[
            jax.ShapeDtypeStruct((rows, D), f32),
            jax.ShapeDtypeStruct((rows, D), bf16),
            jax.ShapeDtypeStruct((rows, D), bf16),
            jax.ShapeDtypeStruct((rows, 128), bf16),
            jax.ShapeDtypeStruct((rows, 128), bf16),
            jax.ShapeDtypeStruct((1, D), f32),
        ],
        compiler_params=buffer_params(56),
        cost_estimate=cost(
            flops=2 * rows * table.shape[0] * D, bytes_accessed=rows * D * 12, transcendentals=0
        ),
        name="embed",
    )(lengths, buckets, tokens, cotangent, table)


def middle_kernel(o_ref, w_ref, h_ref, vec_ref, h1_ref, b_ref):
    total = h_ref[...] + dot(o_ref[...], w_ref[...]) + vec_ref[OUT_BIAS]
    h1_ref[...] = total
    normal, _ = norm_stats(total)
    b_ref[...] = (normal * vec_ref[GAIN_TWO] + vec_ref[SHIFT_TWO]).astype(bf16)


def middle(o, weight, start, vectors):
    rows = start.shape[0]
    return pl.pallas_call(
        middle_kernel,
        grid=(rows // BLOCK,),
        in_specs=[
            buffer_spec(D), whole_spec((D, D)), buffer_spec(D), whole_spec((8, D)),
        ],
        out_specs=[buffer_spec(D), buffer_spec(D)],
        out_shape=[jax.ShapeDtypeStruct((rows, D), f32), jax.ShapeDtypeStruct((rows, D), bf16)],
        compiler_params=buffer_params(),
        cost_estimate=cost(
            flops=2 * rows * D * D, bytes_accessed=rows * D * 12, transcendentals=0
        ),
        name="middle",
    )(o, weight, start, vectors)


def middle_back_kernel(
    h1_ref, db_ref, gm_ref, o_ref, w_ref, vec_ref, gdown_ref, gup_ref, g1_ref, do_ref, early_ref,
    *gw_refs, rows_in,
):
    *gw_refs, gw_s = gw_refs
    step = pl.program_id(0)
    normal, inverse = norm_stats(h1_ref[...])
    db = db_ref[...]
    g1 = gm_ref[...].astype(f32) + norm_back(db, normal, inverse, vec_ref[GAIN_TWO])
    g1_ref[...] = g1
    ga = g1.astype(bf16)
    do_ref[...] = dot(ga, w_ref[...], NT).astype(bf16)
    for row, value in ((0, g1), (1, db * normal), (2, db)):
        add_rows(early_ref, step, row, value)
    add_product(gw_s, step, dot(o_ref[...], ga, TN))

    @pl.when(step == pl.num_programs(0) - 1)
    def _():
        store_weight(gw_refs, gw_s[...], rows_in)
        early_ref[3:4, :] = gdown_ref[...]
        for i in range(gup_ref.shape[1] // D):
            early_ref[4 + i : 5 + i, :] = gup_ref[:, i * D : (i + 1) * D]


def middle_back(h1, db, gm, o, weight, vectors, grad_down, grad_up, rows_in):
    rows = h1.shape[0]
    wide = buffer_spec(D)
    grads = weight_shapes(D, rows_in)
    return pl.pallas_call(
        lambda *refs: middle_back_kernel(*refs, rows_in=rows_in),
        grid=(rows // BLOCK,),
        in_specs=[
            wide, wide, wide, wide, whole_spec((D, D)),
            whole_spec((8, D)), whole_spec((1, D)), whole_spec(grad_up.shape),
        ],
        out_specs=[wide, wide, whole_spec((8, D))] + [whole_spec(item.shape) for item in grads],
        out_shape=[
            jax.ShapeDtypeStruct((rows, D), f32),
            jax.ShapeDtypeStruct((rows, D), bf16),
            jax.ShapeDtypeStruct((8, D), f32),
        ]
        + grads,
        scratch_shapes=[pltpu.VMEM((D, D), f32)],
        compiler_params=buffer_params(MIDDLE),
        cost_estimate=cost(
            flops=4 * rows * D * D, bytes_accessed=rows * D * 18, transcendentals=0
        ),
        name="middle_back",
    )(h1, db, gm, o, weight, vectors, grad_down, grad_up)


def finish_kernel(*refs, plan):
    lengths_ref, buckets_ref, h_ref, g1_ref, vec_ref, early_ref = refs[:6]
    grads, sums_in, weights = refs[6 : 6 + len(plan)], refs[6 + len(plan) : 6 + 2 * len(plan)], refs[6 + 2 * len(plan) : -2]
    input_ref, pack_ref = refs[-2:]
    step = pl.program_id(0)
    count = pack_ref.shape[0]
    buffer, ids = block_rows((BLOCK, 1), 0)
    _, _, _, _, image, _ = row_plan(lengths_ref, buckets_ref, buffer, ids)
    da = 0.0
    for grad, (which, at) in zip(grads, plan):
        da = da + dot(grad[...], weights[which][:, at : at + grad.shape[1]], NT)
    normal, inverse = norm_stats(h_ref[...])
    g0 = g1_ref[...] + norm_back(da, normal, inverse, vec_ref[GAIN_ONE])
    input_ref[...] = jnp.where(image, g0, 0.0)
    _, across = block_rows((1, BLOCK), 1)
    _, position, _, prompt, _, _ = row_plan(lengths_ref, buckets_ref, buffer, across)
    wanted = lax.broadcasted_iota(jnp.int32, (count, 1), 0)
    hits = jnp.where(prompt & (wanted == position), 1.0, 0.0).astype(bf16)
    sums = sum(dot(hits, part) for part in split_three(g0)[:2])
    lines = [jnp.sum(da * normal, axis=0, keepdims=True), jnp.sum(da, axis=0, keepdims=True)]
    for row, line in enumerate(lines):
        sums = jnp.where(wanted == PROMPTS + row, line, sums)

    @pl.when(step == 0)
    def _():
        pack_ref[...] = sums

    @pl.when(step > 0)
    def _():
        pack_ref[...] += sums

    @pl.when(step == pl.num_programs(0) - 1)
    def _():
        at = 0
        for ref in sums_in:
            for pair in range(ref.shape[1] // GROUP):
                to = slice(at, at + 128)
                at += 128
                for row, part in ((PROMPTS + 2, 0), (PROMPTS + 3, 2)):
                    lanes = slice(pair * GROUP + part * 128, pair * GROUP + part * 128 + 128)
                    pack_ref[row : row + 1, to] = ref[0:1, lanes]
        pack_ref[PROMPTS + 4 : PROMPTS + 12, :] = early_ref[...]


def finish(lengths, buckets, start, g1, vectors, early, grads, sums, weights, plan):
    rows = start.shape[0]
    wide = buffer_spec(D)
    return pl.pallas_call(
        lambda *refs: finish_kernel(*refs, plan=plan),
        grid=(rows // BLOCK,),
        in_specs=[scalar_spec(), scalar_spec(), wide, wide, whole_spec((8, D)), whole_spec((8, D))]
        + [buffer_spec(item.shape[1]) for item in grads]
        + [whole_spec(item.shape) for item in sums]
        + [whole_spec(item.shape) for item in weights],
        out_specs=[wide, whole_spec((PACK, D))],
        out_shape=[jax.ShapeDtypeStruct((rows, D), f32), jax.ShapeDtypeStruct((PACK, D), f32)],
        compiler_params=buffer_params(),
        cost_estimate=cost(
            flops=6 * rows * D * D, bytes_accessed=rows * D * 18, transcendentals=0
        ),
        name="finish",
    )(lengths, buckets, start, g1, vectors, early, *grads, *sums, *weights)


def attend_kernel(qkv_ref, fq_ref, fk_ref, o_ref, lse_ref, *, chunk):
    pair = pl.program_id(1)
    lane = lax.broadcasted_iota(jnp.int32, (1, 128), 1)
    keys = jnp.concatenate([qkv_ref[:, 128:256], fk_ref[...]], axis=1)
    values = jnp.concatenate([qkv_ref[:, 256:384], jnp.ones((ROWS, 128), bf16)], axis=1)
    for step in range(ROWS // chunk):
        rows = slice(step * chunk, (step + 1) * chunk)
        queries = qkv_ref[rows, 0:128]
        marks = fq_ref[rows, :]
        outs = []
        lse = lse_ref[rows, :]
        for half in range(2):
            keep = (lane < 64) if half == 0 else (lane >= 64)
            own = jnp.concatenate([jnp.where(keep, queries, jnp.zeros_like(queries)), marks], axis=1)
            scores = dot(own, keys, NT)
            top = jnp.max(scores, axis=1, keepdims=True)
            weights = jnp.exp2((scores - top) * score_scale)
            mixed = dot(weights.astype(bf16), values)
            total = mixed[:, 128:129]
            outs.append(mixed[:, :128] / total)
            log_total = top + jnp.log2(total) * (1.0 / score_scale)
            lse = jnp.where(lane == pair * 2 + half, log_total, lse)
        o_ref[rows, :] = jnp.where(lane < 64, outs[0], outs[1]).astype(bf16)
        lse_ref[rows, :] = lse


def attend(qkv, fq, fk, chunk=320):
    rows = qkv.shape[0]
    mark = pl.BlockSpec((ROWS, 128), lambda b, p: (b, 0))
    return pl.pallas_call(
        lambda *refs: attend_kernel(*refs, chunk=chunk),
        grid=(rows // ROWS, qkv.shape[1] // GROUP),
        in_specs=[pl.BlockSpec((ROWS, GROUP), lambda b, p: (b, p)), mark, mark],
        out_specs=[pl.BlockSpec((ROWS, 128), lambda b, p: (b, p)), mark],
        out_shape=[
            jax.ShapeDtypeStruct((rows, qkv.shape[1] // 3), bf16),
            jax.ShapeDtypeStruct((rows, 128), f32),
        ],
        compiler_params=pltpu.CompilerParams(
            dimension_semantics=("arbitrary", "arbitrary"), vmem_limit_bytes=24 << 20
        ),
        cost_estimate=cost(
            flops=5 * rows * ROWS * qkv.shape[1],
            bytes_accessed=rows * qkv.shape[1] * 3,
            transcendentals=rows * ROWS * qkv.shape[1] // 192,
        ),
        name="attend",
    )(qkv, fq, fk)


def split_three(value):
    first = value.astype(bf16)
    rest = value - first.astype(f32)
    second = rest.astype(bf16)
    third = (rest - second.astype(f32)).astype(bf16)
    return first, second, third


def attend_back_kernel(
    qkv_ref, do_ref, o_ref, fq_ref, fk_ref, lse_ref, dqkv_ref, sum_ref, ds_ref, *, chunk, low
):
    pair, buffer = low + pl.program_id(0), pl.program_id(1)
    lane = lax.broadcasted_iota(jnp.int32, (1, 128), 1)
    queries = qkv_ref[:, 0:128]
    grads = do_ref[...]
    marks = fq_ref[...]
    product = grads.astype(f32) * o_ref[...].astype(f32)
    lse = lse_ref[...]
    zero = jnp.zeros_like(queries)
    own_q, own_g, wide_q, wide_g = [], [], [], []
    for half in range(2):
        keep = (lane < 64) if half == 0 else (lane >= 64)
        shift = -jnp.sum(jnp.where(lane == pair * 2 + half, lse, 0.0), axis=1, keepdims=True)
        inner = -jnp.sum(jnp.where(keep, product, 0.0), axis=1, keepdims=True)
        s0, s1, s2 = split_three(shift)
        i0, i1, i2 = split_three(inner)
        mark_q = jnp.where(lane == 8, s0, jnp.where(lane == 9, s1, jnp.where(lane == 10, s2, marks)))
        mark_g = jnp.where(lane == 8, i0, jnp.where(lane == 9, i1, jnp.where(lane == 10, i2, zero)))
        q_half = jnp.where(keep, queries, zero)
        g_half = jnp.where(keep, grads, zero)
        own_q.append(q_half)
        own_g.append(g_half)
        wide_q.append(jnp.concatenate([q_half, mark_q], axis=1))
        wide_g.append(jnp.concatenate([g_half, mark_g], axis=1))
    for step in range(ROWS // chunk):
        rows = slice(step * chunk, (step + 1) * chunk)
        keys = jnp.concatenate([qkv_ref[rows, 128:256], fk_ref[rows, :]], axis=1)
        values = jnp.concatenate([qkv_ref[rows, 256:384], fk_ref[rows, :]], axis=1)
        dv = jnp.zeros((chunk, 128), f32)
        dk = jnp.zeros((chunk, 128), f32)
        for half in range(2):
            weights = jnp.exp2(dot(keys, wide_q[half], NT) * score_scale)
            ds = (weights * dot(values, wide_g[half], NT)).astype(bf16)
            ds_ref[half, rows, :] = ds
            dv = dv + dot(weights.astype(bf16), own_g[half])
            dk = dk + dot(ds, own_q[half])
        dqkv_ref[rows, 256:384] = dv.astype(bf16)
        dqkv_ref[rows, 128:256] = (dk * 0.125).astype(bf16)
        line = jnp.sum(dv, axis=0, keepdims=True)
        dv_sum = dv_sum + line if step else line
    keys_t = qkv_ref[:, 128:256].T
    parts = [dot(keys_t, ds_ref[half]).T for half in range(2)]
    dq = jnp.where(lane < 64, parts[0], parts[1]) * 0.125
    dqkv_ref[:, 0:128] = dq.astype(bf16)
    dq_sum = jnp.sum(dq, axis=0, keepdims=True)

    @pl.when(buffer == 0)
    def _():
        sum_ref[0:1, 0:128] = dq_sum
        sum_ref[0:1, 256:384] = dv_sum

    @pl.when(buffer > 0)
    def _():
        sum_ref[0:1, 0:128] += dq_sum
        sum_ref[0:1, 256:384] += dv_sum


def attend_back(qkv, do, o, fq, fk, lse, pairs, chunk=640):
    rows = qkv.shape[0]
    low, count = pairs[0], pairs[1] - pairs[0]
    columns = count * GROUP
    mark = pl.BlockSpec((ROWS, 128), lambda p, b: (b, 0))
    part = pl.BlockSpec((ROWS, 128), lambda p, b: (b, low + p))
    return pl.pallas_call(
        lambda *refs: attend_back_kernel(*refs, chunk=chunk, low=low),
        grid=(count, rows // ROWS),
        in_specs=[
            pl.BlockSpec((ROWS, GROUP), lambda p, b: (b, low + p)), part, part, mark, mark, mark,
        ],
        out_specs=[
            pl.BlockSpec((ROWS, GROUP), lambda p, b: (b, p)),
            pl.BlockSpec((8, GROUP), lambda p, b: (0, p)),
        ],
        out_shape=[
            jax.ShapeDtypeStruct((rows, columns), bf16),
            jax.ShapeDtypeStruct((8, columns), f32),
        ],
        scratch_shapes=[pltpu.VMEM((2, ROWS, ROWS), bf16)],
        compiler_params=pltpu.CompilerParams(
            dimension_semantics=("arbitrary", "arbitrary"), vmem_limit_bytes=24 << 20
        ),
        cost_estimate=cost(
            flops=12 * rows * ROWS * columns,
            bytes_accessed=rows * columns * 6,
            transcendentals=rows * ROWS * columns // 192,
        ),
        name="attend_back",
    )(qkv, do, o, fq, fk, lse)


def gelu_parts(u):
    z = jnp.abs(u) * 0.7071067811865476
    t = 1.0 / (1.0 + erf_p * z)
    e = jnp.exp2(u * u * (-0.5 * log2_e))
    series = t * (erf_a[0] + t * (erf_a[1] + t * (erf_a[2] + t * (erf_a[3] + t * erf_a[4]))))
    tail = 0.5 * series * e
    return jnp.where(u < 0, tail, 1.0 - tail), e * 0.3989422804014327


def store_halves(mine_ref, theirs_ref, value, rows):
    columns = value.shape[-1]
    grid = value.reshape(-1, 2, 2, rows, columns)
    first = lax.rem(lax.axis_index("dp"), 2) == 0
    for y in range(2):
        left, right = grid[:, y, 0].reshape(-1, columns), grid[:, y, 1].reshape(-1, columns)
        mine_ref[y] = jnp.where(first, left, right).astype(bf16)
        theirs_ref[y] = jnp.where(first, right, left).astype(bf16)


def feed_kernel(*refs, chunk, more, rows_up):
    b_ref, gm_ref, up_ref, dn_ref, ub_ref = refs[:5]
    outs = refs[5 + 2 * more : -2]
    h_ref, db_ref, gub_ref = outs[:3]
    act_s, du_s = refs[-2:]
    up, dn, ub = up_ref[...], dn_ref[...], ub_ref[...]

    @pl.when(pl.program_id(0) == 0)
    def _():
        h_ref[...] = refs[5][...] if more else jnp.zeros_like(h_ref)
        db_ref[...] = refs[6][...] if more else jnp.zeros_like(db_ref)

    sums = jnp.zeros((1, ub.shape[1]), f32)
    chunks = [slice(at, at + chunk) for at in range(0, b_ref.shape[0], chunk)]
    for rows in chunks:
        u = dot(b_ref[rows, :], up) + ub
        da = dot(gm_ref[rows, :], dn)
        cdf, pdf = gelu_parts(u)
        du = da * (cdf + u * pdf)
        sums = sums + jnp.sum(du, axis=0, keepdims=True)
        act_s[rows, :] = (u * cdf).astype(bf16)
        du_s[rows, :] = du.astype(bf16)
    for rows in chunks:
        h_ref[rows, :] += dot(act_s[rows, :], dn, NT)
        db_ref[rows, :] += dot(du_s[rows, :], up, NT)
    gub_ref[...] = sums
    for i, (left, right) in enumerate(((b_ref, du_s), (gm_ref, act_s))):
        grad = dot(left[...], right[...], TN)
        if rows_up:
            store_halves(outs[3 + 2 * i], outs[4 + 2 * i], grad, rows_up)
        else:
            outs[3 + i][...] = grad.astype(bf16)


def feed(b, gm, up, dn, ub, rows_up, before=(), block=768, chunk=320):
    rows = b.shape[0]
    hidden = up.shape[1]
    rows_up = rows_up if rows_up % 16 == 0 else 0
    full = pl.BlockSpec((rows, D), lambda j: (0, 0), pipeline_mode=pl.Buffered(1))
    weight = pl.BlockSpec((D, block), lambda j: (0, j))
    bias = pl.BlockSpec((1, block), lambda j: (0, j))
    if rows_up:
        grad = pl.BlockSpec((2, D // 4, block), lambda j: (0, 0, j))
        shapes = [jax.ShapeDtypeStruct((2, D // 4, hidden), bf16)] * 4
    else:
        grad = pl.BlockSpec((D, block), lambda j: (0, j))
        shapes = [jax.ShapeDtypeStruct((D, hidden), bf16)] * 2
    return pl.pallas_call(
        lambda *refs: feed_kernel(*refs, chunk=chunk, more=bool(before), rows_up=rows_up),
        grid=(hidden // block,),
        in_specs=[full, full, weight, weight, bias] + [full] * len(before),
        out_specs=[full, full, bias] + [grad] * len(shapes),
        out_shape=[jax.ShapeDtypeStruct((rows, D), f32)] * 2
        + [jax.ShapeDtypeStruct(ub.shape, f32)]
        + shapes,
        scratch_shapes=[pltpu.VMEM((rows, block), bf16)] * 2,
        compiler_params=pltpu.CompilerParams(
            dimension_semantics=("arbitrary",), vmem_limit_bytes=(46 if before else 38) << 20
        ),
        cost_estimate=cost(
            flops=12 * rows * hidden * D,
            bytes_accessed=rows * D * 12 + hidden * D * 8,
            transcendentals=2 * rows * hidden,
        ),
        name="feed",
    )(b, gm, up, dn, ub, *before)


def pair_major(columns):
    lead = columns.shape[:-1]
    return columns.reshape(lead + (3, PAIRS, 128)).swapaxes(-3, -2).reshape(lead + (3 * D,))


def pair_minor(columns):
    lead = columns.shape[:-1]
    return columns.reshape(lead + (PAIRS, 3, 128)).swapaxes(-3, -2).reshape(lead + (3 * D,))


class Place:
    def __init__(self):
        dp, self.nx = lax.axis_size("dp"), lax.axis_size("mlp")
        self.ny, self.nc = 2, 2
        self.nz = dp // (self.ny * self.nc)
        index = lax.axis_index("dp")
        self.x = lax.axis_index("mlp")
        self.c = index % self.nc
        self.y = (index // self.nc) % self.ny
        self.z = index // (self.nc * self.ny)

    label = "hop"

    def send(self, value, move):
        pairs = []
        for z in range(self.nz):
            for y in range(self.ny):
                for c in range(self.nc):
                    for x in range(self.nx):
                        source = ((z * self.ny + y) * self.nc + c) * self.nx + x
                        z2, y2, c2, x2 = move(z, y, c, x)
                        pairs.append((source, ((z2 * self.ny + y2) * self.nc + c2) * self.nx + x2))
        with jax.named_scope(self.label):
            return lax.ppermute(value, ("dp", "mlp"), pairs)

    def shift(self, value, dz=0, dy=0, dc=0, dx=0):
        return self.send(
            value,
            lambda z, y, c, x: (
                (z + dz) % self.nz,
                (y + dy) % self.ny,
                (c + dc) % self.nc,
                (x + dx) % self.nx,
            ),
        )


def spread_z(place, shard):
    return {k: place.shift(shard, dz=k) if k else shard for k in range(place.nz)}


def line_up(place, pieces):
    ids = jnp.arange(place.nz).reshape((place.nz,) + (1,) * pieces[0].ndim)
    whole = jnp.broadcast_to(pieces[0][None], (place.nz,) + pieces[0].shape)
    for k in range(1, place.nz):
        whole = jnp.where(ids == (place.z - k) % place.nz, pieces[k][None], whole)
    return whole


def spread_plane(place, line):
    over_x = place.shift(line, dx=1)
    over_y = place.shift(line, dy=1)
    return {(0, 0): line, (1, 0): over_x, (0, 1): over_y, (1, 1): place.shift(over_y, dx=1)}


def spread_plane_halves(place, line, other):
    half = line.shape[-1] // 2
    over_x = place.shift(line, dx=1)
    over_y = place.shift(line, dy=1)
    over_x, over_y, other = lax.optimization_barrier((over_x, over_y, other))
    pieces = {
        (0, 0, 0): line,
        (1, 0, 0): over_x,
        (0, 1, 0): over_y,
        (1, 1, 0): place.shift(over_x[..., :half], dy=1),
        (1, 1, half): place.shift(over_y[..., half:], dx=1),
    }
    return pieces, other


def spread_cores(place, pieces):
    whole = {key[:-1] + (0,) + key[-1:]: piece for key, piece in pieces.items()}
    for key, piece in pieces.items():
        whole[key[:-1] + (1,) + key[-1:]] = place.shift(piece, dc=1)
    return whole


def assemble_kernel(*refs, keys, plan, nx):
    sources, targets = refs[: len(keys)], refs[len(keys) :]
    index = lax.axis_index("dp")
    here = {"x": lax.axis_index("mlp"), "c": index % 2, "y": (index // 2) % 2}
    many = {"x": nx, "c": 2, "y": 2}
    for source, (key, low) in zip(sources, keys):
        spot = {axis: lax.rem(here[axis] + many[axis] - key[axis], many[axis]) for axis in key}
        spot["z"] = slice(None)
        high = low + source.shape[-1]
        for target, (order, picks, first, columns) in zip(targets, plan):
            left, right = max(low, first), min(high, first + columns)
            if left >= right:
                continue
            take = (slice(None),) + picks + (slice(None), slice(left - low, right - low))
            place = tuple(spot[axis] for axis in order)
            target[place + (slice(None), slice(left - first, right - first))] = source[take]


def assemble(place, pieces, names, plan):
    keys = [(dict(zip(names, key[:-1])), key[-1]) for key in pieces]
    arrays = list(pieces.values())
    many = {"x": place.nx, "y": place.ny, "c": place.nc, "z": place.nz}
    rows = arrays[0].shape[-2]
    shapes = [tuple(many[axis] for axis in order) + (rows, columns) for order, _, _, columns in plan]
    size = sum(math.prod(shape) for shape in shapes)
    out = pl.pallas_call(
        lambda *refs: assemble_kernel(*refs, keys=keys, plan=plan, nx=place.nx),
        in_specs=[pl.BlockSpec(memory_space=pltpu.VMEM)] * len(arrays),
        out_specs=[pl.BlockSpec(memory_space=pltpu.VMEM)] * len(plan),
        out_shape=[jax.ShapeDtypeStruct(shape, bf16) for shape in shapes],
        compiler_params=pltpu.CompilerParams(vmem_limit_bytes=4 << 20),
        cost_estimate=cost(flops=0, bytes_accessed=4 * size, transcendentals=0),
        name="assemble",
    )(*arrays)
    return [item.reshape(-1, item.shape[-1]) for item in out]


def after(value, *others):
    return lax.optimization_barrier((value,) + others)[0]


def cover(values, scatters=(), arrays=()):
    picked = []
    for item in scatters:
        scatter, picks = item if isinstance(item, tuple) else (item, range(len(item.fresh)))
        picked += [(scatter, scatter.fresh[i]) for i in picks]
    moved = [scatter.terms[i] for scatter, i in picked]
    values, moved, arrays = lax.optimization_barrier((list(values), moved, list(arrays)))
    for (scatter, i), term in zip(picked, moved):
        scatter.terms[i] = term
    return list(values) + list(arrays)


class Scatter:
    def __init__(self, place, terms, axes):
        self.place, self.terms, self.axes = place, list(terms), axes

    def take(self, axis, index):
        at = self.axes.index(axis)
        return [lax.dynamic_index_in_dim(term, index, at, keepdims=False) for term in self.terms]

    def hop(self, axis):
        place = self.place
        here, many = getattr(place, axis), getattr(place, "n" + axis)
        moved = []
        for k in range(1, many):
            theirs = add_up(self.take(axis, (here + k) % many)).astype(bf16)
            moved.append(place.shift(theirs, **{"d" + axis: k}))
        terms = self.take(axis, here)
        self.fresh = range(len(terms), len(terms) + len(moved))
        self.terms = terms + moved
        self.axes = self.axes.replace(axis, "")
        return self

    def hop_plane(self):
        place = self.place
        moved = []
        for dx, dy in ((1, 0), (0, 1), (1, 1)):
            part = Scatter(place, self.terms, self.axes)
            part.terms, part.axes = part.take("x", (place.x + dx) % place.nx), part.axes.replace("x", "")
            theirs = add_up(part.take("y", (place.y + dy) % place.ny)).astype(bf16)
            moved.append(place.shift(theirs, dx=dx, dy=dy))
        for axis in "xy":
            self.terms = self.take(axis, getattr(place, axis))
            self.axes = self.axes.replace(axis, "")
        self.fresh = range(len(self.terms), len(self.terms) + 3)
        self.terms = self.terms + moved
        return self

    def add(self, theirs, **move):
        self.fresh = range(len(self.terms), len(self.terms) + 1)
        self.terms = self.terms + [self.place.shift(theirs, **move)]
        return self

    def join(self, other):
        return self.add(add_up(other.terms).astype(bf16), dx=1)

    @property
    def total(self):
        return add_up(self.terms)


def add_up(terms):
    return sum(term.astype(f32) for term in terms)


def per_device(
    tokens,
    cotangent,
    lengths,
    buckets,
    pos_table,
    prompts,
    norm1_gain,
    norm1_bias,
    qkv_weight,
    q_bias,
    v_bias,
    out_weight,
    out_bias,
    norm2_gain,
    norm2_bias,
    up_weight,
    up_bias,
    down_weight,
    down_bias,
):
    mlp_size = lax.axis_size("mlp")
    micro_count, local_rows = tokens.shape[:2]
    rows = micro_count * local_rows
    hidden_local = up_weight.shape[1]
    hidden = hidden_local * mlp_size

    place = Place()
    rows_up = up_weight.shape[0]
    qkv_shard = pair_major(qkv_weight)
    rows_in = qkv_weight.shape[0]
    pieces = spread_z(place, jnp.concatenate([qkv_shard, out_weight], axis=1))
    buffer_lengths, buffer_buckets = lengths.reshape(-1, SLOTS), buckets.reshape(-1)
    table = jnp.pad(
        jnp.concatenate([pos_table, prompts, norm1_gain[None], norm1_bias[None]], axis=0),
        ((0, 1024 - TABLE - PROMPTS - 2), (0, 0)),
    )
    start_rows, normed, grad_branch, fq, fk, grad_down_shift = embed(
        buffer_lengths, buffer_buckets, tokens.reshape(rows, D), cotangent.reshape(rows, D), table
    )
    feed_pack = jnp.stack([up_weight, down_weight.T])
    shift_other = place.shift(up_bias, dx=1)
    pieces, feed_pack, shift_other, normed = lax.optimization_barrier(
        (pieces, feed_pack, shift_other, normed)
    )
    line = line_up(place, pieces)
    small = [norm1_gain, norm1_bias, out_bias, norm2_gain, norm2_bias, down_bias, q_bias, v_bias]
    small, line = lax.optimization_barrier((small, line))
    vectors = jnp.stack(small).astype(f32)
    qkv_offset = pair_major(
        jnp.concatenate([vectors[6:7], jnp.zeros((1, D), f32), vectors[7:8]], axis=1)
    )
    plane, (qkv_offset, vectors) = spread_plane_halves(place, line, (qkv_offset, vectors))
    qkv_full, out_full = assemble(
        place, spread_cores(place, plane), "xyc", [("zycx", (), 0, 3 * D), ("zycx", (), 3 * D, D)]
    )

    feed_line = line_up(place, spread_z(place, feed_pack))
    over_x = place.shift(feed_line, dx=1)

    def feed_weights(pieces):
        plan = [("zyc", (which,), 0, hidden_local) for which in range(2)]
        return assemble(place, pieces, "yc", plan)

    shift_own = up_bias.astype(f32)[None, :]
    shift_other = shift_other.astype(f32)[None, :]

    normed = after(normed, feed_line)
    qkv_rows = (dot(normed, qkv_full) + qkv_offset).astype(bf16)
    over_y = place.shift(feed_line, dy=1)
    attended, log_total, over_x, over_y = cover(attend(qkv_rows, fq, fk), arrays=[over_x, over_y])
    own_pieces = spread_cores(place, {(0, 0): feed_line, (1, 0): over_y})
    first_sum, normed_two = middle(attended, out_full, start_rows, vectors)

    def parts(value, order):
        many = {"x": place.nx, "y": place.ny, "c": place.nc, "z": place.nz}
        return value.reshape(tuple(many[axis] for axis in order) + (-1, value.shape[-1]))

    def feed_scatter(grads):
        made = []
        for which in range(2):
            if len(grads) == 4:
                mine, theirs = (
                    item.reshape(2, place.nz, -1, hidden_local) for item in grads[2 * which : 2 * which + 2]
                )
                made.append(Scatter(place, [mine], "yz").add(theirs, dc=1))
            else:
                made.append(Scatter(place, [parts(grads[which], "zyc")], "zyc").hop("c"))
        return made

    up_own, down_own = feed_weights(own_pieces)
    *results, over_both = cover(
        feed(normed_two, grad_branch, up_own, down_own, shift_own, rows_up),
        arrays=[place.shift(over_y, dx=1)],
    )
    sum_h, sum_db, shift_grad_own, *grads = results
    own_up, own_down = feed_scatter(grads)
    up_other, down_other = feed_weights(spread_cores(place, {(0, 0): over_x, (1, 0): over_both}))
    normed_two, _ = cover([normed_two], [own_up, own_down], [up_other])
    branch, grad_normed, shift_grad_other, *grads = cover(
        feed(normed_two, grad_branch, up_other, down_other, shift_other, rows_up, (sum_h, sum_db)),
        [own_up.hop("y")],
    )
    grad_up_shift = jnp.where(
        place.x == 0,
        jnp.concatenate([shift_grad_own, shift_grad_other], axis=1),
        jnp.concatenate([shift_grad_other, shift_grad_own], axis=1),
    )
    other_up, other_down = feed_scatter(grads)
    (first_sum,) = cover([first_sum], [other_up, other_down])
    grad_one, grad_attended, early, *grads = middle_back(
        first_sum, grad_normed, grad_branch, attended, out_full, vectors, grad_down_shift,
        grad_up_shift, rows_in,
    )

    def weight_scatter(grads):
        if len(grads) == 2:
            mine, theirs = (parts(item.reshape(D // 2, -1), "zyx") for item in grads)
            return Scatter(place, [mine], "zyx").add(theirs, dc=1)
        return Scatter(place, [parts(grads[0], "zycx")], "zycx").hop("c")

    def back(pairs, covered):
        values = attend_back(qkv_rows, grad_attended, attended, fq, fk, log_total, pairs)
        rows_grad, sums = cover(values, covered)
        return rows_grad, sums, dot(normed, rows_grad, TN).astype(bf16)

    cuts = [0, FIRST, FIRST + (PAIRS - FIRST) // 2, PAIRS]
    send_out = weight_scatter(grads)
    back_two, sums_two, weight_two = back(
        (cuts[1], cuts[2]), [other_up.hop("y"), own_down.join(other_down), send_out]
    )
    grad_attended = after(grad_attended, weight_two)
    send_two = weight_scatter([weight_two])
    back_three, sums_three, weight_three = back(
        (cuts[2], cuts[3]), [own_up.join(other_up), own_down.hop("y"), send_two]
    )
    grad_attended = after(grad_attended, weight_three)
    send_three = weight_scatter([weight_three])
    send_own = Scatter(place, [jnp.stack([own_up.total, own_down.total])], "uz").hop("z")
    far = [k - 1 for k in range(1, place.nz) if 2 * k == place.nz]
    near = [k for k in range(place.nz - 1) if k not in far]
    back_one, sums_one, weight_one = back(
        (cuts[0], cuts[1]), [send_three, send_two.hop("x"), (send_own, far)]
    )
    back_one = after(back_one, weight_one)
    send_one = weight_scatter([weight_one])
    send_three = Scatter(
        place, [jnp.concatenate([send_three.total, send_out.total], axis=-1)], send_out.axes
    ).hop("x")
    input_grad, packed = cover(
        finish(
            buffer_lengths, buffer_buckets, start_rows, grad_one, vectors, early,
            [back_one, back_two, back_three], [sums_one, sums_two, sums_three],
            [qkv_full], [(0, at * GROUP) for at in cuts[:3]],
        ),
        [(send_own, near), send_three, send_two.hop("y"), send_one],
    )

    packed = packed.reshape(place.nc, PACK // place.nc, D)
    own = lax.dynamic_index_in_dim(packed, place.c, 0, keepdims=False)
    other = lax.dynamic_index_in_dim(packed, 1 - place.c, 0, keepdims=False)
    send_three.hop("y")
    send_one.hop("x")
    own = own + place.shift(other, dc=1)
    (own,) = cover([own], [send_one, send_three])
    send_rest = Scatter(
        place, [jnp.concatenate([send_two.total, send_three.total], axis=-1)], send_three.axes
    ).hop("z")
    send_one.hop("y")
    seen = {(0, 0): own, (1, 0): place.shift(own, dx=1), (0, 1): place.shift(own, dy=1)}
    seen[1, 1] = place.shift(own, dx=1, dy=1)
    own = 0.0
    for x in range(2):
        for y in range(2):
            line = [jnp.where(place.x == x, seen[0, dy], seen[1, dy]) for dy in range(2)]
            own = own + jnp.where(place.y == y, line[0], line[1])
    (own,) = cover([own], [send_one])
    send_one.hop("z")
    first_sum, branch, _ = lax.optimization_barrier((first_sum, branch, own))
    outside = fq[:, SLOTS : SLOTS + 1].astype(f32) > 0.0
    output = jnp.where(outside, 0.0, first_sum + branch + vectors[5:6]).astype(bf16)
    bit = 1
    while bit < place.nz:
        own = own + place.send(own, lambda z, y, c, x, bit=bit: (z ^ bit, y, c, x))
        if bit == 1:
            (own,) = cover([own], [send_rest])
        bit *= 2
    (own,) = cover([own], [send_one])
    other = place.shift(own, dc=1)
    summed = jnp.where(
        place.c == 0, jnp.concatenate([own, other], 0), jnp.concatenate([other, own], 0)
    )
    prompts_grad = summed[:PROMPTS]
    singles = [summed[PROMPTS + i] for i in range(8)]
    up_bias_grad = lax.dynamic_slice_in_dim(
        summed[PROMPTS + 8 : PROMPTS + 12].reshape(hidden), place.x * hidden_local, hidden_local, 0
    )
    rest = 3 * D - FIRST * GROUP
    qkv_weight_grad = pair_minor(
        jnp.concatenate([send_one.total, add_up([term[:, :rest] for term in send_rest.terms])], axis=1)
    )
    out_weight_grad = add_up([term[:, rest:] for term in send_rest.terms])
    up_weight_grad = send_own.total[0]
    down_weight_grad = send_own.total[1].T
    return (
        output.reshape(tokens.shape),
        input_grad.reshape(tokens.shape),
        prompts_grad,
        singles[0],
        singles[1],
        qkv_weight_grad,
        singles[2],
        singles[3],
        out_weight_grad,
        singles[4],
        singles[5],
        singles[6],
        up_weight_grad,
        up_bias_grad,
        down_weight_grad,
        singles[7],
    )


def solution(mesh):
    both = ("dp", "mlp")
    in_specs = (
        P(None, both, None),
        P(None, both, None),
        P(None, both, None),
        P(None, both),
        P(),
        P(),
        P(),
        P(),
        P(both, None),
        P(),
        P(),
        P(both, None),
        P(),
        P(),
        P(),
        P("dp", "mlp"),
        P("mlp"),
        P("mlp", "dp"),
        P(),
    )
    out_specs = (
        P(None, both, None),
        P(None, both, None),
        P(),
        P(),
        P(),
        P(both, None),
        P(),
        P(),
        P(both, None),
        P(),
        P(),
        P(),
        P("dp", "mlp"),
        P("mlp"),
        P("mlp", "dp"),
        P(),
    )
    return jax.shard_map(
        per_device, mesh=mesh, in_specs=in_specs, out_specs=out_specs, check_vma=False
    )
```
